32 devices in a mesh: seq: 8 (over y, x, core), fsdp: 4 (over z).
Axes of the slice: x: 2, y: 2, z: 4, core: 2. Of those that a mesh axis runs over, the one named last changes fastest.
Arguments:
- tokens: bfloat16 [4, 4096, 2048], P('fsdp', 'seq'), may hold values from -6 to 6
- doc_starts: int32 [4, 4096], P('fsdp', 'seq'), may hold values from 0 to 1, as said below
- gain_attn: bfloat16 [2048], P(('seq', 'fsdp')), may hold values from 0.5 to 1.5
- w_query: bfloat16 [2048, 2048], P(('seq', 'fsdp')), may hold values from -0.125 to 0.125
- w_key: bfloat16 [2048, 256], P(('seq', 'fsdp')), may hold values from -0.125 to 0.125
- w_value: bfloat16 [2048, 256], P(('seq', 'fsdp')), may hold values from -0.125 to 0.125
- w_out: bfloat16 [2048, 2048], P(('seq', 'fsdp')), may hold values from -1 to 1
- gain_ffn: bfloat16 [2048], P(('seq', 'fsdp')), may hold values from 0.5 to 1.5
- w_gate: bfloat16 [2048, 5632], P(('seq', 'fsdp')), may hold values from -0.125 to 0.125
- w_up: bfloat16 [2048, 5632], P(('seq', 'fsdp')), may hold values from -0.125 to 0.125
- w_down: bfloat16 [5632, 2048], P(('seq', 'fsdp')), may hold values from -0.078125 to 0.078125
- cotangent: bfloat16 [4, 4096, 2048], P('fsdp', 'seq'), may hold values from -6 to 6
Outputs:
- output: bfloat16 [4, 4096, 2048], P('fsdp', 'seq')
- grad_tokens: float32 [4, 4096, 2048], P('fsdp', 'seq')
- grad_gain_attn: float32 [2048], P(('seq', 'fsdp'))
- grad_query: float32 [2048, 2048], P(('seq', 'fsdp'))
- grad_key: float32 [2048, 256], P(('seq', 'fsdp'))
- grad_value: float32 [2048, 256], P(('seq', 'fsdp'))
- grad_out: float32 [2048, 2048], P(('seq', 'fsdp'))
- grad_gain_ffn: float32 [2048], P(('seq', 'fsdp'))
- grad_gate: float32 [2048, 5632], P(('seq', 'fsdp'))
- grad_up: float32 [2048, 5632], P(('seq', 'fsdp'))
- grad_down: float32 [5632, 2048], P(('seq', 'fsdp'))
The draws below stay inside these ranges and needn't reach their ends.
Inputs may be any that keep to these rules, and one draw needn't show every extreme that they name: `doc_starts`: position 0 of every stream begins a document whatever its entry; one stream or more holds a document of 3072 positions or more.
All inputs are finite; a program needn't handle non-finite values.
Results may differ from the reference program's by a relative error of at most 0.015.
Values may be sent and summed in bfloat16 or wider, within the bound.
A program may use at most 384 MiB of HBM per device.

```python
import math
import jax
import jax.numpy as jnp
from jax import lax

D = 2048
H = 32
KV = 4
HD = 64
FF = 5632
LEN = 4096
STREAMS = 4


def draw_doc_starts(key, part):
    key_coins = jax.random.fold_in(key, 11)
    key_begin = jax.random.fold_in(key, 12)
    key_stream = jax.random.fold_in(key, 13)
    coin_draws = jax.random.randint(key_coins, (STREAMS, LEN), 0, LEN // 16)
    starts = jnp.where(coin_draws == 0, 1, 0).astype(jnp.int32)
    long_start = jax.random.randint(key_begin, (STREAMS, 1), 0, LEN // 4 + 1)
    chosen_stream = jax.random.randint(key_stream, (), 0, STREAMS)
    places = jnp.arange(LEN, dtype=jnp.int32)[None, :]
    picked = (jnp.arange(STREAMS, dtype=jnp.int32) == chosen_stream)[:, None]
    inside = picked & (places > long_start) & (places < long_start + 3 * LEN // 4)
    starts = jnp.where(inside, 0, starts)
    starts = jnp.where(picked & (places == long_start), 1, starts)
    return starts.astype(jnp.int32)


def shard_levels(key, shape, cuts, least, top_value):
    def one(position, parts):
        draws = jax.random.uniform(jax.random.fold_in(jax.random.fold_in(key, 6), position), (parts,), jnp.float32, least / len(cuts), top_value / len(cuts))
        return jnp.repeat(jnp.exp(draws), shape[position] // parts).reshape((-1,) + (1,) * (len(shape) - position - 1))

    loudness = one(*cuts[0])
    for cut in cuts[1:]:
        loudness = loudness * one(*cut)
    return loudness


def gaussian(rng, dims, spread, most, pieces=(), kind=jnp.bfloat16):
    loudness = shard_levels(rng, dims, pieces, -0.22, 0.18) if pieces else 1.0
    values = jax.random.normal(rng, dims, jnp.float32) * spread * loudness
    return jnp.minimum(jnp.maximum(values, -most), most).astype(kind)


def setup_inputs(seed: int = 0) -> dict:
    key_of = jax.random.split(jax.random.key(seed), 13)
    return {
        "tokens": gaussian(key_of[0], (STREAMS, LEN, D), 1.0, 6.0, ((0, 4), (1, 8))),
        "doc_starts": draw_doc_starts(jax.random.fold_in(key_of[12], 71), 0),
        "gain_attn": jnp.clip(1.0 + 0.1 * jax.random.normal(key_of[2], (D,), jnp.float32), 0.5, 1.5).astype(jnp.bfloat16),
        "w_query": gaussian(key_of[3], (D, H * HD), D ** -0.5, 0.125, ((0, 32),)),
        "w_key": gaussian(key_of[4], (D, KV * HD), D ** -0.5, 0.125, ((0, 32),)),
        "w_value": gaussian(key_of[5], (D, KV * HD), D ** -0.5, 0.125, ((0, 32),)),
        "w_out": gaussian(key_of[6], (H * HD, D), (D // 64) ** -0.5, 1.0, ((0, 32),)),
        "gain_ffn": jnp.clip(1.0 + 0.1 * jax.random.normal(key_of[7], (D,), jnp.float32), 0.5, 1.5).astype(jnp.bfloat16),
        "w_gate": gaussian(key_of[8], (D, FF), D ** -0.5, 0.125, ((0, 32),)),
        "w_up": gaussian(key_of[9], (D, FF), D ** -0.5, 0.125, ((0, 32),)),
        "w_down": gaussian(key_of[10], (FF, D), FF ** -0.5, 0.078125, ((0, 32),)),
        "cotangent": gaussian(key_of[11], (STREAMS, LEN, D), 1.0, 6.0, ((0, 4), (1, 8))),
    }


@jax.custom_vjp
def low(v):
    return lax.optimization_barrier(v.astype(jnp.bfloat16)).astype(jnp.float32)

@jax.custom_vjp
def low_back(v):
    return v

def low_keep(v):
    return (low(v), None)

def low_pass(kept, grad):
    return (grad,)

def back_keep(v):
    return (v, None)

def back_low(kept, grad):
    return (low(grad),)
low.defvjp(low_keep, low_pass)
low_back.defvjp(back_keep, back_low)
epsilon = 1e-05

def matmul(left, right):
    return jnp.dot(left, right, precision=lax.Precision.HIGHEST, preferred_element_type=jnp.float32)

def norm_scale(value):
    return lax.rsqrt(lax.optimization_barrier(jnp.mean(value * value, axis=-1, keepdims=True)) + epsilon)

def rotary_tables(places, head_width):
    half_width = head_width // 2
    frequency = jnp.exp(jnp.arange(half_width, dtype=jnp.float32) * (-2.0 * math.log(10000.0) / head_width))
    angles = places.astype(jnp.float32)[..., None] * frequency
    return (jnp.cos(angles), jnp.sin(angles))

def rotate(values, cosine, sine):
    half_width = values.shape[-1] // 2
    first_half = values[..., :half_width]
    second_half = values[..., half_width:]
    cos_part = cosine[..., None, :]
    sin_part = sine[..., None, :]
    return jnp.concatenate([first_half * cos_part - second_half * sin_part, second_half * cos_part + first_half * sin_part], axis=-1)

def attention(queries, keys, values, segment):
    length = queries.shape[0]
    block_rows = min(512, length)
    keys = jnp.repeat(keys, H // KV, axis=1)
    values = jnp.repeat(values, H // KV, axis=1)
    key_place = jnp.arange(length, dtype=jnp.int32)
    score_scale = HD ** (-0.5)

    def one_block(first_row):
        query_block = lax.dynamic_slice_in_dim(queries, first_row, block_rows, 0)
        query_segment = lax.dynamic_slice_in_dim(segment, first_row, block_rows, 0)
        query_place = first_row + jnp.arange(block_rows, dtype=jnp.int32)
        allowed = (key_place[None, :] <= query_place[:, None]) & (segment[None, :] == query_segment[:, None])
        scores = jnp.einsum('qhd,khd->hqk', query_block, keys, precision=lax.Precision.HIGHEST, preferred_element_type=jnp.float32) * score_scale
        scores = low_back(scores)
        probability = low(jax.nn.softmax(jnp.where(allowed[None], scores, -1000000000.0), axis=-1))
        return jnp.einsum('hqk,khd->qhd', probability, values, precision=lax.Precision.HIGHEST, preferred_element_type=jnp.float32)
    first_rows = (jnp.arange(length // block_rows, dtype=jnp.int32) * block_rows).astype(jnp.int32)
    blocks = lax.map(jax.checkpoint(one_block), first_rows)
    return blocks.reshape(length, H * HD)

def layer(inputs, gain_attn, w_query, w_key, w_value, w_out, gain_ffn, w_gate, w_up, w_down, segment, cosine, sine):
    length = inputs.shape[0]
    normed_attn = low(inputs * norm_scale(inputs) * gain_attn)
    queries = low_back(matmul(normed_attn, w_query)).reshape(length, H, HD)
    keys = low_back(matmul(normed_attn, w_key)).reshape(length, KV, HD)
    values = low(low_back(matmul(normed_attn, w_value))).reshape(length, KV, HD)
    queries = low(rotate(queries, cosine, sine))
    keys = low(rotate(keys, cosine, sine))
    attended = low(low_back(attention(queries, keys, values, segment)))
    hidden_one = inputs + low_back(matmul(attended, w_out))
    normed_ffn = low(hidden_one * norm_scale(hidden_one) * gain_ffn)
    gate_proj = low_back(matmul(normed_ffn, w_gate))
    up_proj = low_back(matmul(normed_ffn, w_up))
    activation = low(jax.nn.silu(gate_proj) * up_proj)
    return hidden_one + low_back(matmul(activation, w_down))

def reference(tokens, doc_starts, gain_attn, w_query, w_key, w_value, w_out, gain_ffn, w_gate, w_up, w_down, cotangent):
    params = tuple((param.astype(jnp.float32) for param in (gain_attn, w_query, w_key, w_value, w_out, gain_ffn, w_gate, w_up, w_down)))
    length = tokens.shape[1]
    positions = jnp.arange(length, dtype=jnp.int32)

    def one_stream(running, stream_data):
        stream_tokens, stream_starts, stream_grad = stream_data
        doc_flags = jnp.where((stream_starts != 0) | (positions == 0), 1, 0).astype(jnp.int32)
        segment = jnp.cumsum(doc_flags).astype(jnp.int32)
        last_start = lax.cummax(jnp.where(doc_flags == 1, positions, 0).astype(jnp.int32), axis=0)
        cosine, sine = rotary_tables((positions - last_start).astype(jnp.int32), HD)

        def forward(stream_in, *weights):
            return layer(stream_in, *weights, segment, cosine, sine)
        result, pullback = jax.vjp(forward, stream_tokens.astype(jnp.float32), *params)
        gradients = pullback(stream_grad.astype(jnp.float32))
        running = tuple((total_term + new_term for total_term, new_term in zip(running, gradients[1:])))
        return (running, (result.astype(jnp.bfloat16), gradients[0]))
    initial = tuple((jnp.zeros(param.shape, jnp.float32) for param in params))
    totals, (outputs, input_grads) = lax.scan(one_stream, initial, (tokens, doc_starts, cotangent))
    return (outputs, input_grads, totals[0], totals[1], totals[2], totals[3], totals[4], totals[5], totals[6], totals[7], totals[8])
```

```python
import functools
import math

import jax
import jax.numpy as jnp
from jax import lax
from jax.experimental import pallas as pl
from jax.experimental.pallas import tpu as pltpu
from jax.sharding import PartitionSpec as P

H = 32
KV = 4
HD = 64
HALF = HD // 2
EPS = 1e-05
NEG = -1e30
BQ = 256
BK = 512
BF = jnp.bfloat16
F32 = jnp.float32
VMEM_LIMIT = 56 * 1024 * 1024


def dot_f32(a, b):
    return jnp.dot(a, b, preferred_element_type=F32)


def heads_wide(block, group):
    return jnp.concatenate([block[h * HD : (h + 1) * HD] for h in range(group)], axis=1)


def heads_tall(block, group):
    width = block.shape[1] // group
    return jnp.concatenate([block[:, h * width : (h + 1) * width] for h in range(group)], axis=0)


def allowed_block(step, block_keys, first_row, block_rows, wide, starts):
    key = step * block_keys + lax.broadcasted_iota(jnp.int32, (block_keys, 1), 0)
    row = first_row + (lax.broadcasted_iota(jnp.int32, (1, wide), 1) & (block_rows - 1))
    return (key <= row) & (key >= starts)


def three_loops(bounds_ref, index, body):
    low, first, second, high = (bounds_ref[index, n] for n in range(4))
    lax.fori_loop(low, first, lambda j, c: body(j, True), None)
    lax.fori_loop(first, second, lambda j, c: body(j, False), None)
    lax.fori_loop(second, high, lambda j, c: body(j, True), None)


def forward_kernel(group, bounds_ref, q_ref, k_ref, vt_ref, start_ref, o_ref, lse_ref, acc, top, total):
    i = pl.program_id(0)
    rows = q_ref.shape[1]
    wide = rows * group
    q4 = heads_wide(q_ref[...], group)
    starts = start_ref[0]
    acc[...] = jnp.zeros_like(acc)
    top[...] = jnp.full_like(top, NEG)
    total[...] = jnp.zeros_like(total)

    def block(j, masked):
        at = pl.multiple_of(j * BK, BK)
        s = dot_f32(k_ref[pl.ds(at, BK), :], q4)
        if masked:
            s = jnp.where(allowed_block(j, BK, i * rows, rows, wide, starts), s, NEG)
        old = top[...]
        new = jnp.maximum(old, jnp.max(s, axis=0, keepdims=True))
        p = jnp.exp(s - new)
        keep = jnp.exp(old - new)
        top[...] = new
        total[...] = total[...] * keep + jnp.sum(p, axis=0, keepdims=True)
        acc[...] = acc[...] * keep + dot_f32(vt_ref[:, pl.ds(at, BK)], p.astype(BF))

    three_loops(bounds_ref, i, block)
    o = acc[...] / total[...]
    o_ref[0] = heads_tall(o, group).astype(BF)
    lse_ref[0] = top[...] + jnp.log(total[...])


def backward_kernel(
    group, bounds_ref, q_ref, k_ref, kt_ref, v_ref, start_ref, o_ref, do_ref, lse_ref,
    dq_ref, dk_ref, dv_ref, acc,
):
    i = pl.program_id(0)
    rows = q_ref.shape[1]
    wide = rows * group
    q4 = heads_wide(q_ref[...], group)
    g4 = heads_wide(do_ref[0], group)
    o4 = heads_wide(o_ref[0], group)
    delta = jnp.sum(g4.astype(F32) * o4.astype(F32), axis=0, keepdims=True)
    q4t = q4.T
    g4t = g4.T
    starts = start_ref[0]
    lse = lse_ref[0]
    acc[...] = jnp.zeros_like(acc)

    @pl.when(i == 0)
    def _():
        dk_ref[...] = jnp.zeros_like(dk_ref)
        dv_ref[...] = jnp.zeros_like(dv_ref)

    def block(j, masked):
        at = pl.multiple_of(j * BK, BK)
        s = dot_f32(k_ref[pl.ds(at, BK), :], q4)
        p = jnp.exp(s - lse)
        if masked:
            p = jnp.where(allowed_block(j, BK, i * rows, rows, wide, starts), p, 0.0)
        dp = dot_f32(v_ref[pl.ds(at, BK), :], g4)
        ds = (p * (dp - delta)).astype(BF)
        dv_ref[pl.ds(at, BK), :] += dot_f32(p.astype(BF), g4t)
        dk_ref[pl.ds(at, BK), :] += dot_f32(ds, q4t)
        acc[...] += dot_f32(kt_ref[:, pl.ds(at, BK)], ds)

    three_loops(bounds_ref, i, block)
    dq_ref[...] = heads_tall(acc[...], group)


def whole_spec(shape):
    return pl.BlockSpec(shape, lambda i, b: (0,) * len(shape))


def attend(bounds, qt, k, vt, starts, group, senders, local):
    length = k.shape[0]
    blocks = length // BQ
    per = local // BQ
    piece = pl.BlockSpec((1, group * HD, BQ), lambda i, b: (i // per, 0, i % per))
    line = pl.BlockSpec((1, 1, group * BQ), lambda i, b: (i, 0, 0))
    return pl.pallas_call(
        functools.partial(forward_kernel, group),
        out_shape=(
            jax.ShapeDtypeStruct((senders, group * HD, local), BF),
            jax.ShapeDtypeStruct((blocks, 1, group * BQ), F32),
        ),
        grid_spec=pltpu.PrefetchScalarGridSpec(
            num_scalar_prefetch=1,
            grid=(blocks,),
            in_specs=[
                pl.BlockSpec((group * HD, BQ), lambda i, b: (0, i)),
                whole_spec((length, HD)),
                whole_spec((HD, length)),
                line,
            ],
            out_specs=(piece, line),
            scratch_shapes=[
                pltpu.VMEM((HD, group * BQ), F32),
                pltpu.VMEM((1, group * BQ), F32),
                pltpu.VMEM((1, group * BQ), F32),
            ],
        ),
        compiler_params=pltpu.CompilerParams(
            dimension_semantics=("arbitrary",), vmem_limit_bytes=VMEM_LIMIT
        ),
        cost_estimate=pl.CostEstimate(
            flops=4 * group * length * length * HD // 2,
            bytes_accessed=4 * group * length * HD * 2,
            transcendentals=group * length * length // 4,
        ),
        name="attend",
    )(bounds, qt, k, vt, starts)


def attend_back(bounds, qt, k, kt, v, starts, o, do, lse, group):
    length = k.shape[0]
    blocks = length // BQ
    senders, _, local = o.shape
    per = local // BQ
    piece = pl.BlockSpec((1, group * HD, BQ), lambda i, b: (i // per, 0, i % per))
    line = pl.BlockSpec((1, 1, group * BQ), lambda i, b: (i, 0, 0))
    flat = pl.BlockSpec((group * HD, BQ), lambda i, b: (0, i))
    return pl.pallas_call(
        functools.partial(backward_kernel, group),
        out_shape=(
            jax.ShapeDtypeStruct((group * HD, length), F32),
            jax.ShapeDtypeStruct((length, HD), F32),
            jax.ShapeDtypeStruct((length, HD), F32),
        ),
        grid_spec=pltpu.PrefetchScalarGridSpec(
            num_scalar_prefetch=1,
            grid=(blocks,),
            in_specs=[
                flat,
                whole_spec((length, HD)),
                whole_spec((HD, length)),
                whole_spec((length, HD)),
                line,
                piece,
                piece,
                line,
            ],
            out_specs=(flat, whole_spec((length, HD)), whole_spec((length, HD))),
            scratch_shapes=[pltpu.VMEM((HD, group * BQ), F32)],
        ),
        compiler_params=pltpu.CompilerParams(
            dimension_semantics=("arbitrary",), vmem_limit_bytes=VMEM_LIMIT
        ),
        cost_estimate=pl.CostEstimate(
            flops=10 * group * length * length * HD // 2,
            bytes_accessed=8 * group * length * HD * 2,
            transcendentals=group * length * length // 4,
        ),
        name="attend_back",
    )(bounds, qt, k, kt, v, starts, o, do, lse)


def ring(axis):
    count = lax.axis_size(axis)
    return [(n, (n + 1) % count) for n in range(count)]


def ring_gather(block, axis):
    count = lax.axis_size(axis)
    me = lax.axis_index(axis)
    pieces = [block]
    for _ in range(count - 1):
        block = lax.ppermute(block, axis, ring(axis))
        pieces.append(block)
    whole = jnp.zeros((count,) + block.shape, block.dtype)
    for back, piece in enumerate(pieces):
        whole = lax.dynamic_update_index_in_dim(whole, piece, (me + count - back) % count, 0)
    return whole


def ring_scatter(terms, axis):
    count = lax.axis_size(axis)
    me = lax.axis_index(axis)

    def pick(back):
        return lax.dynamic_index_in_dim(terms, (me + 2 * count - 1 - back) % count, 0, False)

    state = pick(0)
    for step in range(1, count):
        moved = lax.ppermute(state.astype(BF), axis, ring(axis))
        state = moved.astype(F32) + pick(step).astype(F32)
    return state


def exchange(array):
    return lax.all_to_all(array, "seq", split_axis=0, concat_axis=0, tiled=True)


def document_starts(flags_all):
    length = flags_all.shape[0]
    lanes = 128
    table = flags_all.reshape(length // lanes, lanes)
    place = jnp.arange(length, dtype=jnp.int32).reshape(table.shape)
    marked = jnp.where((table != 0) & (place > 0), place, 0)
    inside = jnp.arange(lanes)[None, :] <= jnp.arange(lanes)[:, None]
    local = jnp.max(jnp.where(inside[None], marked[:, None, :], 0), axis=-1)
    rows = jnp.max(marked, axis=1)
    count = length // lanes
    before = jnp.arange(count)[None, :] < jnp.arange(count)[:, None]
    carried = jnp.max(jnp.where(before, rows[None, :], 0), axis=-1)
    return jnp.maximum(local, carried[:, None]).reshape(length)


def rotate(block, cosine, sine, direction):
    first, second = block[:, :HALF], block[:, HALF:]
    sine = sine * direction
    return jnp.concatenate(
        [first * cosine - second * sine, second * cosine + first * sine], axis=1
    )


def body(
    tokens, doc_starts, gain_attn, w_query, w_key, w_value, w_out, gain_ffn, w_gate, w_up, w_down,
    cotangent,
):
    streams, local, width = tokens.shape
    assert streams == 1
    count = lax.axis_size("seq")
    parts = lax.axis_size("fsdp")
    length = local * count
    group = H // count
    share = (H // KV) // group
    rows = w_query.shape[0]
    hidden = w_gate.shape[1] // count
    group_width = group * HD
    both = ("seq", "fsdp")

    gains = lax.all_gather(jnp.stack([gain_attn, gain_ffn]), both, axis=1, tiled=True)
    gain_one, gain_two = gains[0].astype(F32), gains[1].astype(F32)
    flags = lax.all_gather(doc_starts[0], "seq", axis=0, tiled=True)
    x = tokens[0].astype(F32)
    r1 = lax.rsqrt(jnp.mean(x * x, axis=-1, keepdims=True) + EPS)
    n1 = (x * r1 * gain_one).astype(BF)
    n1_all = lax.all_gather(n1, "seq", axis=0, tiled=True)

    last = document_starts(flags)
    place = (jnp.arange(length, dtype=jnp.int32) - last).astype(F32)
    frequency = jnp.exp(jnp.arange(HALF, dtype=F32) * (-2.0 * math.log(10000.0) / HD))
    angle = frequency[:, None] * place[None, :]
    cosine, sine = jnp.cos(angle), jnp.sin(angle)
    blocks = length // BQ
    by_block = last.reshape(blocks, BQ)
    starts = jnp.tile(by_block, (1, group)).reshape(blocks, 1, group * BQ)
    first_row = jnp.arange(blocks, dtype=jnp.int32) * BQ
    low = by_block[:, 0] // BK
    high = (first_row + BQ + BK - 1) // BK
    begin = jnp.minimum((by_block[:, -1] + BK - 1) // BK, high)
    end = jnp.maximum((first_row + 1) // BK, begin)
    bounds = jnp.stack([low, begin, end, high], axis=1)

    attn_send = jnp.concatenate(
        [
            w_query.reshape(rows, count, group_width),
            jnp.repeat(w_key.reshape(rows, KV, HD), share, axis=1),
            jnp.repeat(w_value.reshape(rows, KV, HD), share, axis=1),
        ],
        axis=2,
    ).transpose(1, 2, 0)
    attn_cols = group_width + 2 * HD
    attn_part = exchange(attn_send)
    attn_t = ring_gather(attn_part, "fsdp").transpose(2, 1, 0, 3).reshape(attn_cols, width)

    ffn_send = jnp.concatenate(
        [w_gate.reshape(rows, count, hidden), w_up.reshape(rows, count, hidden)], axis=0
    ).transpose(1, 0, 2)
    ffn_part = exchange(ffn_send).reshape(count, 2, rows, hidden)
    ffn_w = ring_gather(ffn_part, "fsdp").transpose(2, 1, 0, 3, 4).reshape(2, width, hidden)
    gate_w, up_w = ffn_w[0], ffn_w[1]
    down_w = ring_gather(w_down, "fsdp").reshape(hidden, width)

    projected = jnp.einsum("ed,td->et", attn_t, n1_all, preferred_element_type=F32)
    q_t = rotate(projected[:group_width].reshape(group, HD, length), cosine, sine, 1.0)
    k_t = rotate(projected[group_width : group_width + HD].reshape(1, HD, length), cosine, sine, 1.0)
    q_t = (q_t.astype(BF) * BF(HD**-0.5)).reshape(group_width, length)
    k_t = k_t.astype(BF).reshape(HD, length)
    v_t = projected[group_width + HD :].astype(BF)
    k_n, v_n = k_t.T, v_t.T
    o_heads, lse = attend(bounds, q_t, k_n, v_t, starts, group, count, local)
    o_t = exchange(o_heads).reshape(count * group_width, local)
    out_w = lax.all_gather(w_out, both, axis=0, tiled=True)
    h1 = x + jnp.einsum("et,ed->td", o_t, out_w, preferred_element_type=F32)
    r2 = lax.rsqrt(jnp.mean(h1 * h1, axis=-1, keepdims=True) + EPS)
    n2 = (h1 * r2 * gain_two).astype(BF)
    n2_all = lax.all_gather(n2, "seq", axis=0, tiled=True)
    dy = cotangent[0]
    dy_all = lax.all_gather(dy, "seq", axis=0, tiled=True)

    gate = dot_f32(n2_all, gate_w)
    up = dot_f32(n2_all, up_w)
    sig = jax.nn.sigmoid(gate)
    silu = gate * sig
    act = (silu * up).astype(BF)
    d_act = jnp.einsum("td,fd->tf", dy_all, down_w, preferred_element_type=F32)
    d_gate = (d_act * up * sig * (1.0 + gate * (1.0 - sig))).astype(BF)
    d_up = (d_act * silu).astype(BF)
    dn2_part = jnp.einsum("tf,df->td", d_gate, gate_w, preferred_element_type=F32) + jnp.einsum(
        "tf,df->td", d_up, up_w, preferred_element_type=F32
    )
    dn2 = lax.psum_scatter(dn2_part.astype(BF), "seq", scatter_dimension=0, tiled=True).astype(F32)
    y_part = dot_f32(act, down_w).astype(BF)
    y = lax.psum_scatter(y_part, "seq", scatter_dimension=0, tiled=True).astype(F32)
    output = (h1 + y).astype(BF)

    def by_fsdp(term):
        return term.reshape(count, parts, rows, -1).transpose(1, 0, 2, 3)

    term_gate = jnp.einsum("td,tf->df", n2_all, d_gate, preferred_element_type=F32)
    term_up = jnp.einsum("td,tf->df", n2_all, d_up, preferred_element_type=F32)
    term_down = jnp.einsum("tf,td->fd", act, dy_all, preferred_element_type=F32)
    part_gate = ring_scatter(by_fsdp(term_gate), "fsdp")
    part_up = ring_scatter(by_fsdp(term_up), "fsdp")
    grad_down = ring_scatter(term_down.reshape(parts, hidden // parts, width), "fsdp")

    m2 = h1 * r2
    e2 = dn2 * gain_two
    dh1 = dy.astype(F32) + r2 * (e2 - m2 * jnp.mean(e2 * m2, axis=-1, keepdims=True))
    db = dh1.astype(BF)
    do_t = jnp.einsum("ed,td->et", out_w, db, preferred_element_type=F32).astype(BF)
    do_heads = exchange(do_t.reshape(count, group_width, local))
    term_out = dot_f32(o_t, db).astype(BF)
    part_out = lax.psum_scatter(term_out, "seq", scatter_dimension=0, tiled=True)
    grad_out = ring_scatter(part_out.reshape(parts, rows, width), "fsdp")

    dq_t, dk_n, dv_n = attend_back(
        bounds, q_t, k_n, k_t, v_n, starts, o_heads, do_heads, lse, group
    )
    dq_t = rotate(dq_t.reshape(group, HD, length) * (HD**-0.5), cosine, sine, -1.0)
    dk_t = rotate(dk_n.T.reshape(1, HD, length), cosine, sine, -1.0)
    d_t = jnp.concatenate(
        [
            dq_t.reshape(group_width, length).astype(BF),
            dk_t.reshape(HD, length).astype(BF),
            dv_n.T.astype(BF),
        ],
        axis=0,
    )
    dn1_part = jnp.einsum("et,ed->td", d_t, attn_t, preferred_element_type=F32)
    dn1 = lax.psum_scatter(dn1_part.astype(BF), "seq", scatter_dimension=0, tiled=True).astype(F32)
    term_attn = jnp.einsum("td,et->de", n1_all, d_t, preferred_element_type=F32)
    part_attn = ring_scatter(by_fsdp(term_attn), "fsdp")
    m1 = x * r1
    e1 = dn1 * gain_one
    grad_tokens = dh1 + r1 * (e1 - m1 * jnp.mean(e1 * m1, axis=-1, keepdims=True))

    ffn_back = exchange(jnp.stack([part_gate, part_up], axis=1).astype(BF)).astype(F32)
    grad_gate = ffn_back[:, 0].transpose(1, 0, 2).reshape(rows, count * hidden)
    grad_up = ffn_back[:, 1].transpose(1, 0, 2).reshape(rows, count * hidden)
    attn_back = exchange(part_attn.astype(BF)).astype(F32)
    grad_query = attn_back[:, :, :group_width].transpose(1, 0, 2).reshape(rows, H * HD)
    pair = attn_back[:, :, group_width:].reshape(KV, share, rows, 2 * HD).sum(axis=1)
    grad_key = pair[:, :, :HD].transpose(1, 0, 2).reshape(rows, KV * HD)
    grad_value = pair[:, :, HD:].transpose(1, 0, 2).reshape(rows, KV * HD)

    def along(weight, grad):
        return jnp.sum(weight.astype(F32) * grad, axis=1)

    grad_gain_attn = (
        along(w_query, grad_query) + along(w_key, grad_key) + along(w_value, grad_value)
    ) / gain_attn.astype(F32)
    grad_gain_ffn = (along(w_gate, grad_gate) + along(w_up, grad_up)) / gain_ffn.astype(F32)
    return (
        output[None],
        grad_tokens[None],
        grad_gain_attn,
        grad_query,
        grad_key,
        grad_value,
        grad_out,
        grad_gain_ffn,
        grad_gate,
        grad_up,
        grad_down,
    )


def solution(mesh):
    sheet = P("fsdp", "seq", None)
    line = P(("seq", "fsdp"))
    matrix = P(("seq", "fsdp"), None)
    return jax.shard_map(
        body,
        mesh=mesh,
        in_specs=(
            sheet, P("fsdp", "seq"), line, matrix, matrix, matrix, matrix, line, matrix, matrix,
            matrix, sheet,
        ),
        out_specs=(
            sheet, sheet, line, matrix, matrix, matrix, matrix, line, matrix, matrix, matrix,
        ),
        check_vma=False,
    )
```

```python
import functools
import math

import jax
import jax.numpy as jnp
from jax import lax
from jax.experimental import pallas as pl
from jax.experimental.pallas import tpu as pltpu
from jax.sharding import PartitionSpec as P

H = 32
KV = 4
HD = 64
HALF = HD // 2
EPS = 1e-05
NEG = -1e30
BQ = 256
BK = 512
BF = jnp.bfloat16
F32 = jnp.float32
VMEM_LIMIT = 56 * 1024 * 1024
MESH = pl.DeviceIdType.MESH


def dot_f32(a, b):
    return jnp.dot(a, b, preferred_element_type=F32)


def heads_wide(block, group):
    return jnp.concatenate([block[h * HD : (h + 1) * HD] for h in range(group)], axis=1)


def heads_tall(block, group):
    width = block.shape[1] // group
    return jnp.concatenate([block[:, h * width : (h + 1) * width] for h in range(group)], axis=0)


def allowed_block(step, block_keys, first_row, block_rows, wide, starts):
    key = step * block_keys + lax.broadcasted_iota(jnp.int32, (block_keys, 1), 0)
    row = first_row + (lax.broadcasted_iota(jnp.int32, (1, wide), 1) & (block_rows - 1))
    return (key <= row) & (key >= starts)


def three_loops(bounds_ref, index, body):
    low, first, second, high = (bounds_ref[index, n] for n in range(4))
    lax.fori_loop(low, first, lambda j, c: body(j, True), None)
    lax.fori_loop(first, second, lambda j, c: body(j, False), None)
    lax.fori_loop(second, high, lambda j, c: body(j, True), None)


def turned(block, cosine, sine):
    first, second = block[:HALF], block[HALF:]
    return jnp.concatenate(
        [first * cosine - second * sine, second * cosine + first * sine], axis=0
    )


def turned_back(block, cosine, sine):
    first, second = block[:HALF], block[HALF:]
    return jnp.concatenate(
        [first * cosine + second * sine, second * cosine - first * sine], axis=0
    )


def forward_kernel(
    group, bounds_ref, q_ref, kv_ref, cos_ref, sin_ref, start_ref,
    o_ref, lse_ref, qt_ref, kt_ref, kn_ref, vn_ref, vt, acc, top, total,
):
    i = pl.program_id(0)
    rows = q_ref.shape[1]
    wide = rows * group
    here = pl.ds(pl.multiple_of(i * rows, rows), rows)
    cosine, sine = cos_ref[:, here], sin_ref[:, here]

    @pl.when(i == 0)
    def _():
        for part in range(kv_ref.shape[1] // BK):
            at = pl.ds(part * BK, BK)
            k = turned(kv_ref[:HD, at], cos_ref[:, at], sin_ref[:, at]).astype(BF)
            v = kv_ref[HD:, at].astype(BF)
            kt_ref[:, at] = k
            vt[:, at] = v
            kn_ref[at, :] = k.T
            vn_ref[at, :] = v.T

    heads = [
        turned(q_ref[h * HD : (h + 1) * HD, :], cosine, sine).astype(BF) * BF(HD**-0.5)
        for h in range(group)
    ]
    qt_ref[...] = jnp.concatenate(heads, axis=0)
    q4 = jnp.concatenate(heads, axis=1)
    starts = start_ref[0]
    acc[...] = jnp.zeros_like(acc)
    top[...] = jnp.full_like(top, NEG)
    total[...] = jnp.zeros_like(total)

    def block(j, masked):
        at = pl.multiple_of(j * BK, BK)
        s = dot_f32(kn_ref[pl.ds(at, BK), :], q4)
        if masked:
            s = jnp.where(allowed_block(j, BK, i * rows, rows, wide, starts), s, NEG)
        old = top[...]
        new = jnp.maximum(old, jnp.max(s, axis=0, keepdims=True))
        p = jnp.exp(s - new)
        keep = jnp.exp(old - new)
        top[...] = new
        total[...] = total[...] * keep + jnp.sum(p, axis=0, keepdims=True)
        acc[...] = acc[...] * keep + dot_f32(vt[:, pl.ds(at, BK)], p.astype(BF))

    three_loops(bounds_ref, i, block)
    o = acc[...] / total[...]
    o_ref[0] = heads_tall(o, group).astype(BF)
    lse_ref[0] = top[...] + jnp.log(total[...])


def backward_kernel(
    group, bounds_ref, q_ref, k_ref, kt_ref, v_ref, cos_ref, sin_ref, start_ref, o_ref, do_ref,
    lse_ref, dq_ref, dkv_ref, dk, dv, acc,
):
    i = pl.program_id(0)
    rows = q_ref.shape[1]
    wide = rows * group
    q4 = heads_wide(q_ref[...], group)
    g4 = heads_wide(do_ref[0], group)
    o4 = heads_wide(o_ref[0], group)
    delta = jnp.sum(g4.astype(F32) * o4.astype(F32), axis=0, keepdims=True)
    q4t = q4.T
    g4t = g4.T
    starts = start_ref[0]
    lse = lse_ref[0]
    acc[...] = jnp.zeros_like(acc)

    @pl.when(i == 0)
    def _():
        dk[...] = jnp.zeros_like(dk)
        dv[...] = jnp.zeros_like(dv)

    def block(j, masked):
        at = pl.multiple_of(j * BK, BK)
        s = dot_f32(k_ref[pl.ds(at, BK), :], q4)
        p = jnp.exp(s - lse)
        if masked:
            p = jnp.where(allowed_block(j, BK, i * rows, rows, wide, starts), p, 0.0)
        dp = dot_f32(v_ref[pl.ds(at, BK), :], g4)
        ds = (p * (dp - delta)).astype(BF)
        dv[pl.ds(at, BK), :] += dot_f32(p.astype(BF), g4t)
        dk[pl.ds(at, BK), :] += dot_f32(ds, q4t)
        acc[...] += dot_f32(kt_ref[:, pl.ds(at, BK)], ds)

    three_loops(bounds_ref, i, block)
    here = pl.ds(pl.multiple_of(i * rows, rows), rows)
    cosine, sine = cos_ref[:, here], sin_ref[:, here]
    for h in range(group):
        dq = acc[:, h * rows : (h + 1) * rows] * (HD**-0.5)
        dq_ref[h * HD : (h + 1) * HD, :] = turned_back(dq, cosine, sine).astype(BF)

    @pl.when(i == pl.num_programs(0) - 1)
    def _():
        for part in range(dk.shape[0] // BK):
            at = pl.ds(part * BK, BK)
            dk_t = turned_back(dk[at, :].T, cos_ref[:, at], sin_ref[:, at])
            dkv_ref[:HD, at] = dk_t.astype(BF)
            dkv_ref[HD:, at] = dv[at, :].T.astype(BF)


def whole_spec(shape):
    return pl.BlockSpec(shape, lambda i, b: (0,) * len(shape))


def attend(bounds, projected, cosine, sine, starts, group, senders, local):
    length = projected.shape[1]
    blocks = length // BQ
    per = local // BQ
    wide = group * HD
    piece = pl.BlockSpec((1, wide, BQ), lambda i, b: (i // per, 0, i % per))
    line = pl.BlockSpec((1, 1, group * BQ), lambda i, b: (i, 0, 0))
    flat = pl.BlockSpec((wide, BQ), lambda i, b: (0, i))
    return pl.pallas_call(
        functools.partial(forward_kernel, group),
        out_shape=(
            jax.ShapeDtypeStruct((senders, wide, local), BF),
            jax.ShapeDtypeStruct((blocks, 1, group * BQ), F32),
            jax.ShapeDtypeStruct((wide, length), BF),
            jax.ShapeDtypeStruct((HD, length), BF),
            jax.ShapeDtypeStruct((length, HD), BF),
            jax.ShapeDtypeStruct((length, HD), BF),
        ),
        grid_spec=pltpu.PrefetchScalarGridSpec(
            num_scalar_prefetch=1,
            grid=(blocks,),
            in_specs=[
                flat,
                pl.BlockSpec((2 * HD, length), lambda i, b: (wide // (2 * HD), 0)),
                whole_spec((HALF, length)),
                whole_spec((HALF, length)),
                line,
            ],
            out_specs=(
                piece,
                line,
                flat,
                whole_spec((HD, length)),
                whole_spec((length, HD)),
                whole_spec((length, HD)),
            ),
            scratch_shapes=[
                pltpu.VMEM((HD, length), BF),
                pltpu.VMEM((HD, group * BQ), F32),
                pltpu.VMEM((1, group * BQ), F32),
                pltpu.VMEM((1, group * BQ), F32),
            ],
        ),
        compiler_params=pltpu.CompilerParams(
            dimension_semantics=("arbitrary",), vmem_limit_bytes=VMEM_LIMIT
        ),
        cost_estimate=pl.CostEstimate(
            flops=40 * group * length * length * HD // 2,
            bytes_accessed=4 * group * length * HD * 2,
            transcendentals=group * length * length // 4,
        ),
        name="attend",
    )(bounds, projected, projected, cosine, sine, starts)


def attend_back(bounds, qt, k, kt, v, cosine, sine, starts, o, do, lse, group):
    length = k.shape[0]
    blocks = length // BQ
    senders, _, local = o.shape
    per = local // BQ
    piece = pl.BlockSpec((1, group * HD, BQ), lambda i, b: (i // per, 0, i % per))
    line = pl.BlockSpec((1, 1, group * BQ), lambda i, b: (i, 0, 0))
    flat = pl.BlockSpec((group * HD, BQ), lambda i, b: (0, i))
    return pl.pallas_call(
        functools.partial(backward_kernel, group),
        out_shape=(
            jax.ShapeDtypeStruct((group * HD, length), BF),
            jax.ShapeDtypeStruct((2 * HD, length), BF),
        ),
        grid_spec=pltpu.PrefetchScalarGridSpec(
            num_scalar_prefetch=1,
            grid=(blocks,),
            in_specs=[
                flat,
                whole_spec((length, HD)),
                whole_spec((HD, length)),
                whole_spec((length, HD)),
                whole_spec((HALF, length)),
                whole_spec((HALF, length)),
                line,
                piece,
                piece,
                line,
            ],
            out_specs=(flat, whole_spec((2 * HD, length))),
            scratch_shapes=[
                pltpu.VMEM((length, HD), F32),
                pltpu.VMEM((length, HD), F32),
                pltpu.VMEM((HD, group * BQ), F32),
            ],
        ),
        compiler_params=pltpu.CompilerParams(
            dimension_semantics=("arbitrary",), vmem_limit_bytes=VMEM_LIMIT
        ),
        cost_estimate=pl.CostEstimate(
            flops=50 * group * length * length * HD // 2,
            bytes_accessed=8 * group * length * HD,
            transcendentals=group * length * length // 4,
        ),
        name="attend_back",
    )(bounds, qt, k, kt, v, cosine, sine, starts, o, do, lse)


def project_kernel(cols, x_ref, w_ref, n_ref, p_ref, wt_ref):
    @pl.when(pl.program_id(0) == 0)
    def _():
        wt_ref[...] = w_ref[...].T

    wide = x_ref[0].astype(F32)
    scale = lax.rsqrt(jnp.mean(wide * wide, axis=-1, keepdims=True) + EPS)
    gain = wt_ref[pl.ds(cols, 8), :].astype(F32)[0:1]
    normed = (wide * scale * gain).astype(BF)
    n_ref[0] = normed
    p_ref[...] = lax.dot_general(
        wt_ref[:cols, :], normed, (((1,), (1,)), ((), ())), preferred_element_type=F32
    )


def project(x_all, w_ext, cols):
    count, local, width = x_all.shape
    wide = w_ext.shape[1]
    block = pl.BlockSpec((1, local, width), lambda i: (i, 0, 0))
    return pl.pallas_call(
        functools.partial(project_kernel, cols),
        out_shape=(
            jax.ShapeDtypeStruct(x_all.shape, BF),
            jax.ShapeDtypeStruct((cols, count * local), F32),
            jax.ShapeDtypeStruct((wide, width), BF),
        ),
        grid=(count,),
        in_specs=[block, pl.BlockSpec((width, wide), lambda i: (0, 0))],
        out_specs=(
            block,
            pl.BlockSpec((cols, local), lambda i: (0, i)),
            pl.BlockSpec((wide, width), lambda i: (0, 0)),
        ),
        compiler_params=pltpu.CompilerParams(
            dimension_semantics=("arbitrary",), vmem_limit_bytes=VMEM_LIMIT
        ),
        cost_estimate=pl.CostEstimate(
            flops=2 * cols * width * count * local,
            bytes_accessed=4 * width * count * local,
            transcendentals=0,
        ),
        name="project",
    )(x_all, w_ext)


def ffn_kernel(
    places_ref, first_ref, second_ref, dy_ref, gate_ref, up_ref, down_ref, *rest
):
    act_ref, dg_ref, du_ref, n_ref, y_ref, pa_ref, pb_ref = rest[-7:]
    which = pl.program_id(0)
    n = jnp.where(which == 0, first_ref[...], second_ref[...])
    n_ref[0] = n
    dy = dy_ref[0]
    across = (((1,), (1,)), ((), ()))
    gate = dot_f32(n, gate_ref[...])
    up = dot_f32(n, up_ref[...])
    d_act = lax.dot_general(dy, down_ref[...], across, preferred_element_type=F32)
    sig = jax.nn.sigmoid(gate)
    silu = gate * sig
    act = (silu * up).astype(BF)
    d_gate = (d_act * up * sig * (1.0 + gate * (1.0 - sig))).astype(BF)
    d_up = (d_act * silu).astype(BF)
    act_ref[0] = act
    dg_ref[0] = d_gate
    du_ref[0] = d_up
    y_ref[0] = dot_f32(act, down_ref[...]).astype(BF)
    part = lax.dot_general(d_gate, gate_ref[...], across, preferred_element_type=F32)
    part += lax.dot_general(d_up, up_ref[...], across, preferred_element_type=F32)
    part = part.astype(BF)

    @pl.when(which == 0)
    def _():
        pa_ref[...] = part

    @pl.when(which == 1)
    def _():
        pb_ref[...] = part


def ffn_chunk(places, first, second, dy_all, gate_w, up_w, down_w, kept):
    local, width = first.shape
    hidden = gate_w.shape[1]
    tall = min(512, local)
    tiles = local // tall
    count = dy_all.shape[0]

    def at_place(last):
        return pl.BlockSpec((1, tall, last), lambda i, t, p: (p[i], t, 0))

    ahead = pl.BlockSpec((tall, width), lambda i, t, p: (jnp.where(i == 0, t, tiles - 1), 0))
    behind = pl.BlockSpec((tall, width), lambda i, t, p: (jnp.where(i == 0, 0, t), 0))

    def held(shape):
        return pl.BlockSpec(shape, lambda i, t, p: (0, 0), pipeline_mode=pl.Buffered(1))

    in_specs = [
        ahead, behind, at_place(width), held((width, hidden)), held((width, hidden)),
        held((hidden, width)),
    ]
    arrays = [first, second, dy_all, gate_w, up_w, down_w]
    aliases = {}
    if kept is not None:
        in_specs += [pl.BlockSpec(memory_space=pl.ANY)] * 5
        arrays += list(kept)
        aliases = {7 + n: n for n in range(5)}
    narrow = jax.ShapeDtypeStruct((count, local, hidden), BF)
    broad = jax.ShapeDtypeStruct((count, local, width), BF)
    single = jax.ShapeDtypeStruct((local, width), BF)
    outs = pl.pallas_call(
        ffn_kernel,
        out_shape=(narrow, narrow, narrow, broad, broad, single, single),
        grid_spec=pltpu.PrefetchScalarGridSpec(
            num_scalar_prefetch=1,
            grid=(2, tiles),
            in_specs=in_specs,
            out_specs=(
                at_place(hidden), at_place(hidden), at_place(hidden), at_place(width),
                at_place(width), ahead, behind,
            ),
        ),
        input_output_aliases=aliases,
        compiler_params=pltpu.CompilerParams(
            dimension_semantics=("arbitrary", "arbitrary"), vmem_limit_bytes=VMEM_LIMIT
        ),
        cost_estimate=pl.CostEstimate(
            flops=2 * 6 * 2 * local * width * hidden,
            bytes_accessed=2 * (5 * 2 * local * width + 3 * width * hidden),
            transcendentals=2 * local * hidden,
        ),
        name="ffn",
    )(places, *arrays)
    return outs[:5], outs[5], outs[6]


def start_kernel(
    count, parts, x_ref, attn_ref, ffn_ref, x_all, attn_all, ffn_all, attn_mid, ffn_mid,
    send, arrive, local_sem,
):
    me = lax.axis_index("seq")
    z = lax.axis_index("fsdp")
    after_z, before_z = (z + 1) % parts, (z + parts - 1) % parts
    half = x_ref.shape[0] // 2
    barrier = pltpu.get_barrier_semaphore()
    for bit in (1, 2, 4):
        pl.semaphore_signal(barrier, inc=1, device_id=(me ^ bit, z), device_id_type=MESH)
    for other in (after_z, before_z):
        pl.semaphore_signal(barrier, inc=1, device_id=(me, other), device_id_type=MESH)
    pl.semaphore_wait(barrier, 5)
    made = {}

    def start(name, source, target, device):
        n = len(made)
        copy = pltpu.make_async_remote_copy(
            src_ref=source, dst_ref=target, send_sem=send.at[n], recv_sem=arrive.at[n],
            device_id=device, device_id_type=MESH,
        )
        made[name] = copy
        copy.start()

    def to_bit(name, bit, source, target):
        start(name, source, target, (me ^ bit, z))

    def arrived(*names):
        for name in names:
            made[name].wait_recv()

    held = [
        pltpu.make_async_copy(x_ref, x_all.at[me], local_sem.at[0]),
        pltpu.make_async_copy(attn_ref.at[me], attn_all.at[z, me], local_sem.at[1]),
        pltpu.make_async_copy(ffn_ref.at[me], ffn_all.at[z, me], local_sem.at[2]),
    ]
    for copy in held:
        copy.start()

    def swap_first(tag, source, final, mid):
        to_bit(tag + "b3", 2, source.at[me ^ 6], mid.at[4])
        to_bit(tag + "a2", 1, source.at[me ^ 3], mid.at[1])
        to_bit(tag + "a4", 1, source.at[me ^ 7], mid.at[3])
        to_bit(tag + "a3", 1, source.at[me ^ 5], mid.at[2])
        to_bit(tag + "a1", 1, source.at[me ^ 1], final.at[z, me])
        to_bit(tag + "b1", 2, source.at[me ^ 2], final.at[z, me])
        to_bit(tag + "c1", 4, source.at[me ^ 4], final.at[z, me])

    def swap_rest(tag, final, mid):
        arrived(tag + "a2", tag + "a4", tag + "a3")
        to_bit(tag + "b4", 2, mid.at[3], mid.at[5])
        to_bit(tag + "b2", 2, mid.at[1], final.at[z, me ^ 1])
        to_bit(tag + "c2", 4, mid.at[2], final.at[z, me ^ 1])
        arrived(tag + "b3")
        to_bit(tag + "c3", 4, mid.at[4], final.at[z, me ^ 2])
        arrived(tag + "b4")
        to_bit(tag + "c4", 4, mid.at[5], final.at[z, me ^ 3])

    def swap_end(tag):
        arrived(*[tag + n for n in ("a1", "b1", "c1", "b2", "c2", "c3", "c4")])

    swap_first("attn", attn_ref, attn_all, attn_mid)
    to_bit("x1", 1, x_ref, x_all.at[me])
    to_bit("x2", 2, x_ref, x_all.at[me])
    to_bit("x4", 4, x_ref, x_all.at[me])
    swap_rest("attn", attn_all, attn_mid)
    swap_first("ffn", ffn_ref, ffn_all, ffn_mid)
    swap_end("attn")
    held[1].wait()
    start("z1", attn_all.at[z], attn_all.at[z], (me, after_z))
    arrived("x2")
    to_bit("x3", 1, x_all.at[me ^ 2], x_all.at[me ^ 2])
    to_bit("f1", 4, x_all.at[me ^ 2, pl.ds(0, half)], x_all.at[me ^ 2, pl.ds(0, half)])
    arrived("x4")
    to_bit("x5", 1, x_all.at[me ^ 4], x_all.at[me ^ 4])
    to_bit("f2", 2, x_all.at[me ^ 4, pl.ds(half, half)], x_all.at[me ^ 4, pl.ds(half, half)])
    swap_rest("ffn", ffn_all, ffn_mid)
    for step in range(2, parts):
        arrived("z" + str(step - 1))
        at = (z + parts + 1 - step) % parts
        start("z" + str(step), attn_all.at[at], attn_all.at[at], (me, after_z))
    swap_end("ffn")
    held[2].wait()
    start("zffn", ffn_all.at[z], ffn_all.at[z], (me, after_z))
    arrived("f1", "f2")
    to_bit("x7", 1, x_all.at[me ^ 6], x_all.at[me ^ 6])
    arrived("x1", "x3", "x5", "x7", "z" + str(parts - 1), "zffn")
    for copy in made.values():
        copy.wait_send()
    held[0].wait()


def start_gather(x, attn_send, ffn_send, count, parts):
    anyspace = pl.BlockSpec(memory_space=pl.ANY)
    copies = 8 + 2 * 12 + parts
    shapes = (
        jax.ShapeDtypeStruct((count,) + x.shape, BF),
        jax.ShapeDtypeStruct((parts,) + attn_send.shape, BF),
        jax.ShapeDtypeStruct((parts,) + ffn_send.shape, BF),
        jax.ShapeDtypeStruct((6,) + attn_send.shape[1:], BF),
        jax.ShapeDtypeStruct((6,) + ffn_send.shape[1:], BF),
    )
    return pl.pallas_call(
        functools.partial(start_kernel, count, parts),
        out_shape=shapes,
        in_specs=[anyspace] * 3,
        out_specs=(anyspace,) * 5,
        scratch_shapes=[
            pltpu.SemaphoreType.DMA((copies,)),
            pltpu.SemaphoreType.DMA((copies,)),
            pltpu.SemaphoreType.DMA((3,)),
        ],
        compiler_params=pltpu.CompilerParams(
            collective_id=0, has_side_effects=True, vmem_limit_bytes=8 * 1024 * 1024
        ),
        name="start_gather",
    )(x, attn_send, ffn_send)[:3]


def ring(axis):
    count = lax.axis_size(axis)
    return [(n, (n + 1) % count) for n in range(count)]


def hop(*blocks):
    return [lax.ppermute(block, "fsdp", ring("fsdp")) for block in blocks]


def collect(pieces, axis):
    count = lax.axis_size(axis)
    me = lax.axis_index(axis)
    whole = jnp.zeros((count,) + pieces[0].shape, pieces[0].dtype)
    for back, piece in enumerate(pieces):
        whole = lax.dynamic_update_index_in_dim(whole, piece, (me + count - back) % count, 0)
    return whole


def term_of(terms, step):
    count = lax.axis_size("fsdp")
    me = lax.axis_index("fsdp")
    return lax.dynamic_index_in_dim(terms, (me + 2 * count - 1 - step) % count, 1, False)


def ring_step(states, terms, step):
    moved = hop(*[state.astype(BF) for state in states])
    return [m.astype(F32) + term_of(t, step).astype(F32) for m, t in zip(moved, terms)]


def ring_finish(states, terms, step):
    for n in range(step, lax.axis_size("fsdp")):
        states = ring_step(states, terms, n)
    return states


def fence(*values):
    return lax.optimization_barrier(values)


def swap(block, bit):
    count = lax.axis_size("seq")
    return lax.ppermute(block, "seq", [(n, n ^ bit) for n in range(count)])


def gather_plain(block):
    me = lax.axis_index("seq")
    whole = lax.all_gather(block, "seq", axis=0, tiled=False)
    return [lax.dynamic_index_in_dim(whole, me ^ c, 0, False) for c in range(whole.shape[0])]


def scatter_plain(parts):
    me = lax.axis_index("seq")
    whole = jnp.zeros((len(parts),) + parts[0].shape, BF)
    for c, part in enumerate(parts):
        whole = lax.dynamic_update_index_in_dim(whole, part.astype(BF), me ^ c, 0)
    return lax.psum_scatter(whole, "seq", scatter_dimension=0, tiled=False).astype(F32)


def far_halves(over_x, over_y):
    half = over_x.shape[0] // 2
    return swap(over_x[:half], 4), swap(over_y[half:], 2)


def chip_sum(own, other):
    return own.astype(F32) + swap(other, 1).astype(F32)


def exchange(array):
    return lax.all_to_all(array, "seq", split_axis=0, concat_axis=0, tiled=True)


def document_starts(flags_all):
    length = flags_all.shape[0]
    lanes = 128
    table = flags_all.reshape(length // lanes, lanes)
    place = jnp.arange(length, dtype=jnp.int32).reshape(table.shape)
    marked = jnp.where((table != 0) & (place > 0), place, 0)
    inside = jnp.arange(lanes)[None, :] <= jnp.arange(lanes)[:, None]
    local = jnp.max(jnp.where(inside[None], marked[:, None, :], 0), axis=-1)
    rows = jnp.max(marked, axis=1)
    count = length // lanes
    before = jnp.arange(count)[None, :] < jnp.arange(count)[:, None]
    carried = jnp.max(jnp.where(before, rows[None, :], 0), axis=-1)
    return jnp.maximum(local, carried[:, None]).reshape(length)


def body(
    tokens, doc_starts, gain_attn, w_query, w_key, w_value, w_out, gain_ffn, w_gate, w_up, w_down,
    cotangent,
):
    streams, local, width = tokens.shape
    assert streams == 1
    count = lax.axis_size("seq")
    parts = lax.axis_size("fsdp")
    me = lax.axis_index("seq")
    cube = count == 8
    length = local * count
    half = local // 2
    group = H // count
    share = (H // KV) // group
    rows = w_query.shape[0]
    hidden = w_gate.shape[1] // count
    group_width = group * HD
    attn_cols = group_width + 2 * HD
    flag_cols = local // rows
    extra_cols = 128
    sheet = (length, width)

    own = tokens[0]
    attn_send = jnp.concatenate(
        [
            w_query.reshape(rows, count, group_width),
            jnp.repeat(w_key.reshape(rows, KV, HD), share, axis=1),
            jnp.repeat(w_value.reshape(rows, KV, HD), share, axis=1),
        ],
        axis=2,
    ).transpose(1, 0, 2)
    extra = jnp.concatenate(
        [
            gain_attn[:, None],
            gain_ffn[:, None],
            doc_starts[0].astype(BF).reshape(rows, flag_cols),
            jnp.zeros((rows, extra_cols - 2 - flag_cols), BF),
        ],
        axis=1,
    )
    attn_send = jnp.concatenate(
        [attn_send, jnp.broadcast_to(extra[None], (count,) + extra.shape)], axis=2
    )
    ffn_send = jnp.concatenate(
        [w_gate.reshape(rows, count, hidden), w_up.reshape(rows, count, hidden)], axis=0
    ).transpose(1, 0, 2)
    down_w = lax.all_gather(w_down, "fsdp", axis=0, tiled=True)
    z = lax.axis_index("fsdp")
    if cube:
        x_all, attn_all, ffn_all = start_gather(own, attn_send, ffn_send, count, parts)
        ffn_pieces = [
            lax.dynamic_index_in_dim(ffn_all, (z + parts - back) % parts, 0, False)
            for back in range(min(2, parts))
        ]
    else:
        x_all = lax.all_gather(own, "seq", axis=0, tiled=False)
        attn_all = lax.all_gather(exchange(attn_send), "fsdp", axis=0, tiled=False)
        ffn_pieces = [exchange(ffn_send)]
    dy = cotangent[0]
    own, x_all, attn_all, ffn_pieces, dy = fence(own, x_all, attn_all, ffn_pieces, dy)
    ffn_pieces = [piece.reshape(count, 2, rows, hidden) for piece in ffn_pieces]

    dy_all = lax.all_gather(dy, "seq", axis=0, tiled=False)
    if len(ffn_pieces) < parts:
        ffn_pieces += hop(ffn_pieces[-1])
    flags = lax.dynamic_index_in_dim(attn_all, z, 0, False)
    flags = flags[:, :, attn_cols + 2 : attn_cols + 2 + flag_cols].reshape(length)
    last = document_starts(flags)
    position = (jnp.arange(length, dtype=jnp.int32) - last).astype(F32)
    frequency = jnp.exp(jnp.arange(HALF, dtype=F32) * (-2.0 * math.log(10000.0) / HD))
    angle = frequency[:, None] * position[None, :]
    cosine, sine = jnp.cos(angle), jnp.sin(angle)
    blocks = length // BQ
    by_block = last.reshape(blocks, BQ)
    starts = jnp.tile(by_block, (1, group)).reshape(blocks, 1, group * BQ)
    first_row = jnp.arange(blocks, dtype=jnp.int32) * BQ
    low = by_block[:, 0] // BK
    high = (first_row + BQ + BK - 1) // BK
    begin = jnp.minimum((by_block[:, -1] + BK - 1) // BK, high)
    end = jnp.maximum((first_row + 1) // BK, begin)
    bounds = jnp.stack([low, begin, end, high], axis=1)
    w_ext = attn_all.transpose(1, 0, 2, 3).reshape(width, attn_cols + extra_cols)
    n1_all, projected, wt_ext = project(x_all, w_ext, attn_cols)
    attn_t = wt_ext[:attn_cols]
    gain_one = wt_ext[attn_cols].astype(F32)
    gain_two = wt_ext[attn_cols + 1].astype(F32)
    projected, cosine, sine, starts, bounds, ffn_last, w_out, down_w = fence(
        projected, cosine, sine, starts, bounds, ffn_pieces[-1], w_out, down_w
    )
    ffn_pieces[-1] = ffn_last

    out_w = lax.all_gather(w_out, ("seq", "fsdp"), axis=0, tiled=True)
    if len(ffn_pieces) < parts:
        ffn_pieces += hop(ffn_pieces[-1])
    o_heads, lse, q_t, k_t, k_n, v_n = attend(
        bounds, projected, cosine, sine, starts, group, count, local
    )
    o_heads, lse, q_t, k_t, k_n, v_n, ffn_last, dy_all = fence(
        o_heads, lse, q_t, k_t, k_n, v_n, ffn_pieces[-1], dy_all
    )
    ffn_pieces[-1] = ffn_last

    while len(ffn_pieces) < parts:
        ffn_pieces += hop(ffn_pieces[-1])
    o_t = exchange(o_heads).reshape(count * group_width, local)
    o_t, ffn_pieces = fence(o_t, ffn_pieces)

    ffn_w = collect(ffn_pieces, "fsdp").transpose(2, 1, 0, 3, 4).reshape(2, width, hidden)
    gate_w, up_w = ffn_w[0], ffn_w[1]
    x = own.astype(F32)
    r1 = lax.rsqrt(jnp.mean(x * x, axis=-1, keepdims=True) + EPS)
    h1 = x + jnp.einsum("et,ed->td", o_t, out_w, preferred_element_type=F32)
    r2 = lax.rsqrt(jnp.mean(h1 * h1, axis=-1, keepdims=True) + EPS)
    n2 = (h1 * r2 * gain_two).astype(BF)
    n2, h1, r2 = fence(n2, h1, r2)

    kept = None

    def chunk(kept, first, second, c):
        places = jnp.stack([me ^ c, me ^ (c + 1)]).astype(jnp.int32)
        return ffn_chunk(places, first, second, dy_all, gate_w, up_w, down_w, kept)

    if cube:
        side, over_x, over_y = swap(n2, 1), swap(n2, 2), swap(n2, 4)
        side, gate_w, up_w = fence(side, gate_w, up_w)
        kept, own_a, own_b = chunk(kept, n2, side, 0)
        kept, own_a, own_b, over_x, over_y = fence(kept, own_a, own_b, over_x, over_y)

        far_a, far_b = far_halves(over_x, over_y)
        side_x, side_y, own_c = swap(over_x, 1), swap(over_y, 1), swap(own_b, 1)
        side_x, side_y, over_x, over_y, kept = fence(side_x, side_y, over_x, over_y, kept)
        kept, x_a, x_b = chunk(kept, over_x, side_x, 2)
        kept, x_a, x_b, far_a, far_b, own_c = fence(kept, x_a, x_b, far_a, far_b, own_c)

        far = jnp.concatenate([far_a, far_b], axis=0)
        side_far = swap(far, 1)
        x_sum = chip_sum(x_a, x_b)
        x_first = swap(x_sum[:half].astype(BF), 2)
        kept, y_a, y_b = chunk(kept, over_y, side_y, 4)
        kept, y_a, y_b, far, side_far, x_sum = fence(kept, y_a, y_b, far, side_far, x_sum)

        y_sum = chip_sum(y_a, y_b)
        y_second = swap(y_sum[half:].astype(BF), 4)
        kept, far_one, far_two = chunk(kept, far, side_far, 6)
        kept, far_one, far_two, x_first, y_second, y_sum = fence(
            kept, far_one, far_two, x_first, y_second, y_sum
        )
        act, d_gate, d_up, n2_all, y_part = kept
        n2_all, dy_rows = n2_all.reshape(sheet), dy_all.reshape(sheet)
        act, d_gate, d_up = [a.reshape(length, hidden) for a in (act, d_gate, d_up)]

        far_sum = chip_sum(far_one, far_two).astype(BF)
        x_far, y_far = swap(far_sum[:half], 2), swap(far_sum[half:], 4)
        term_gate = jnp.einsum("td,tf->df", n2_all, d_gate, preferred_element_type=F32)
        x_far, y_far, term_gate = fence(x_far, y_far, term_gate)

        x_second = swap((x_sum[half:] + y_far.astype(F32)).astype(BF), 2)
        y_first = swap((y_sum[:half] + x_far.astype(F32)).astype(BF), 4)
        term_up = jnp.einsum("td,tf->df", n2_all, d_up, preferred_element_type=F32)
        x_second, y_first, term_up = fence(x_second, y_first, term_up)
        own_sum = own_a.astype(F32) + own_c.astype(F32)
        first = own_sum[:half] + x_first.astype(F32) + y_first.astype(F32)
        second = own_sum[half:] + x_second.astype(F32) + y_second.astype(F32)
        dn2 = jnp.concatenate([first, second], axis=0)
    else:
        n2_blocks = gather_plain(n2)
        dn2_parts = []
        for c in range(0, count, 2):
            kept, part_a, part_b = chunk(kept, n2_blocks[c], n2_blocks[c + 1], c)
            dn2_parts += [part_a, part_b]
        act, d_gate, d_up, n2_all, y_part = kept
        n2_all, dy_rows = n2_all.reshape(sheet), dy_all.reshape(sheet)
        act, d_gate, d_up = [a.reshape(length, hidden) for a in (act, d_gate, d_up)]
        dn2 = scatter_plain(dn2_parts)
        term_gate = jnp.einsum("td,tf->df", n2_all, d_gate, preferred_element_type=F32)
        term_up = jnp.einsum("td,tf->df", n2_all, d_up, preferred_element_type=F32)
    y_part = y_part.reshape(sheet)

    m2 = h1 * r2
    e2 = dn2 * gain_two
    dh1 = dy.astype(F32) + r2 * (e2 - m2 * jnp.mean(e2 * m2, axis=-1, keepdims=True))
    db = dh1.astype(BF)
    do_t = jnp.einsum("ed,td->et", out_w, db, preferred_element_type=F32).astype(BF)
    do_t, db, dh1, term_gate, term_up, y_part = fence(
        do_t, db, dh1, term_gate, term_up, y_part
    )
    y = lax.psum_scatter(y_part, "seq", scatter_dimension=0, tiled=True)
    gate_up = [
        term_gate.reshape(count, parts, rows, hidden),
        term_up.reshape(count, parts, rows, hidden),
    ]
    moved = hop(*[term_of(term, 0).astype(BF) for term in gate_up])
    do_heads = exchange(do_t.reshape(count, group_width, local))
    term_out = dot_f32(o_t, db).astype(BF)
    do_heads, term_out, moved = fence(do_heads, term_out, moved)

    part_out = lax.psum_scatter(term_out, "seq", scatter_dimension=0, tiled=True)
    states = [m.astype(F32) + term_of(t, 1) for m, t in zip(moved, gate_up)]
    if parts > 2:
        moved = hop(*[state.astype(BF) for state in states])
    dq_t, dkv_t = attend_back(
        bounds, q_t, k_n, k_t, v_n, cosine, sine, starts, o_heads, do_heads, lse, group
    )
    dq_t, dkv_t, moved, states, act = fence(dq_t, dkv_t, moved, states, act)

    d_t = jnp.concatenate([dq_t, dkv_t], axis=0)

    def pair_of(c):
        return jnp.concatenate(
            [lax.dynamic_slice_in_dim(d_t, (me ^ n) * local, local, 1) for n in (c, c + 1)], axis=1
        )

    def dn1_chunk(c):
        part = jnp.einsum("et,ed->td", pair_of(c), attn_t, preferred_element_type=F32).astype(BF)
        return part[:local], part[local:]

    term_down = jnp.einsum("tf,td->fd", act, dy_rows, preferred_element_type=F32)
    if parts > 2:
        states = [m.astype(F32) + term_of(t, 2) for m, t in zip(moved, gate_up)]
    if cube:
        far_sum = chip_sum(*dn1_chunk(6)).astype(BF)
        x_sum = chip_sum(*dn1_chunk(2))
        y_sum = chip_sum(*dn1_chunk(4))
        far_sum, x_sum, y_sum = fence(far_sum, x_sum, y_sum)
        x_far, y_far = swap(far_sum[:half], 2), swap(far_sum[half:], 4)
        x_first = swap(x_sum[:half].astype(BF), 2)
        y_second = swap(y_sum[half:].astype(BF), 4)
        own_sum = chip_sum(*dn1_chunk(0))
        term_attn = jnp.einsum(
            "td,et->de", n1_all.reshape(sheet), d_t, preferred_element_type=F32
        )
        states = ring_finish(states, gate_up, 3)
        x_far, y_far, own_sum, term_attn, states, term_down = fence(
            x_far, y_far, own_sum, term_attn, states, term_down
        )
        x_second = swap((x_sum[half:] + y_far.astype(F32)).astype(BF), 2)
        y_first = swap((y_sum[:half] + x_far.astype(F32)).astype(BF), 4)
        first = own_sum[:half] + x_first.astype(F32) + y_first.astype(F32)
        second = own_sum[half:] + x_second.astype(F32) + y_second.astype(F32)
        dn1 = jnp.concatenate([first, second], axis=0)
    else:
        dn1 = scatter_plain([piece for c in range(0, count, 2) for piece in dn1_chunk(c)])
        term_attn = jnp.einsum(
            "td,et->de", n1_all.reshape(sheet), d_t, preferred_element_type=F32
        )
        states = ring_finish(states, gate_up, 3)
    part_gate, part_up = states
    output = (h1 + y.astype(F32)).astype(BF)
    down_terms = [term_down.reshape(1, parts, hidden // parts, width)]
    (grad_down,) = ring_finish([term_of(down_terms[0], 0)], down_terms, 1)
    grad_down = grad_down.reshape(hidden // parts, width)
    attn_terms = [term_attn.reshape(count, parts, rows, attn_cols)]
    (part_attn,) = ring_finish([term_of(attn_terms[0], 0)], attn_terms, 1)
    out_terms = [part_out.reshape(1, parts, rows, width)]
    (grad_out,) = ring_finish([term_of(out_terms[0], 0)], out_terms, 1)
    grad_out = grad_out.reshape(rows, width)
    m1 = x * r1
    e1 = dn1 * gain_one
    grad_tokens = dh1 + r1 * (e1 - m1 * jnp.mean(e1 * m1, axis=-1, keepdims=True))

    ffn_back = exchange(jnp.stack([part_gate, part_up], axis=1).astype(BF)).astype(F32)
    grad_gate = ffn_back[:, 0].transpose(1, 0, 2).reshape(rows, count * hidden)
    grad_up = ffn_back[:, 1].transpose(1, 0, 2).reshape(rows, count * hidden)
    attn_back = exchange(part_attn.astype(BF)).astype(F32)
    grad_query = attn_back[:, :, :group_width].transpose(1, 0, 2).reshape(rows, H * HD)
    pair = attn_back[:, :, group_width:].reshape(KV, share, rows, 2 * HD).sum(axis=1)
    grad_key = pair[:, :, :HD].transpose(1, 0, 2).reshape(rows, KV * HD)
    grad_value = pair[:, :, HD:].transpose(1, 0, 2).reshape(rows, KV * HD)

    def along(weight, grad):
        return jnp.sum(weight.astype(F32) * grad, axis=1)

    grad_gain_attn = (
        along(w_query, grad_query) + along(w_key, grad_key) + along(w_value, grad_value)
    ) / gain_attn.astype(F32)
    grad_gain_ffn = (along(w_gate, grad_gate) + along(w_up, grad_up)) / gain_ffn.astype(F32)
    return (
        output[None],
        grad_tokens[None],
        grad_gain_attn,
        grad_query,
        grad_key,
        grad_value,
        grad_out,
        grad_gain_ffn,
        grad_gate,
        grad_up,
        grad_down,
    )


def solution(mesh):
    sheet = P("fsdp", "seq", None)
    line = P(("seq", "fsdp"))
    matrix = P(("seq", "fsdp"), None)
    return jax.shard_map(
        body,
        mesh=mesh,
        in_specs=(
            sheet, P("fsdp", "seq"), line, matrix, matrix, matrix, matrix, line, matrix, matrix,
            matrix, sheet,
        ),
        out_specs=(
            sheet, sheet, line, matrix, matrix, matrix, matrix, line, matrix, matrix, matrix,
        ),
        check_vma=False,
    )
```

```python
import functools
import math

import jax
import jax.numpy as jnp
from jax import lax
from jax.experimental import pallas as pl
from jax.experimental.pallas import tpu as pltpu
from jax.sharding import PartitionSpec as P

H = 32
KV = 4
HD = 64
HALF = HD // 2
EPS = 1e-05
NEG = -1e30
BQ = 256
BK = 512
BF = jnp.bfloat16
F32 = jnp.float32
VMEM_LIMIT = 56 * 1024 * 1024
MESH = pl.DeviceIdType.MESH


def dot_f32(a, b):
    return jnp.dot(a, b, preferred_element_type=F32)


def heads_wide(block, group):
    return jnp.concatenate([block[h * HD : (h + 1) * HD] for h in range(group)], axis=1)


def heads_tall(block, group):
    width = block.shape[1] // group
    return jnp.concatenate([block[:, h * width : (h + 1) * width] for h in range(group)], axis=0)


def allowed_block(step, block_keys, first_row, block_rows, wide, starts):
    key = step * block_keys + lax.broadcasted_iota(jnp.int32, (block_keys, 1), 0)
    row = first_row + (lax.broadcasted_iota(jnp.int32, (1, wide), 1) & (block_rows - 1))
    return (key <= row) & (key >= starts)


def three_loops(bounds_ref, index, body):
    low, first, second, high = (bounds_ref[index, n] for n in range(4))
    lax.fori_loop(low, first, lambda j, c: body(j, True), None)
    lax.fori_loop(first, second, lambda j, c: body(j, False), None)
    lax.fori_loop(second, high, lambda j, c: body(j, True), None)


def turned(block, cosine, sine):
    first, second = block[:HALF], block[HALF:]
    return jnp.concatenate(
        [first * cosine - second * sine, second * cosine + first * sine], axis=0
    )


def turned_back(block, cosine, sine):
    first, second = block[:HALF], block[HALF:]
    return jnp.concatenate(
        [first * cosine + second * sine, second * cosine - first * sine], axis=0
    )


def forward_kernel(
    group, bounds_ref, q_ref, kv_ref, cos_ref, sin_ref, start_ref,
    o_ref, lse_ref, qt_ref, kt_ref, kn_ref, vn_ref, vt, acc, top, total,
):
    i = pl.program_id(0)
    rows = q_ref.shape[1]
    wide = rows * group
    here = pl.ds(pl.multiple_of(i * rows, rows), rows)
    cosine, sine = cos_ref[:, here], sin_ref[:, here]

    @pl.when(i == 0)
    def _():
        for part in range(kv_ref.shape[1] // BK):
            at = pl.ds(part * BK, BK)
            k = turned(kv_ref[:HD, at], cos_ref[:, at], sin_ref[:, at]).astype(BF)
            v = kv_ref[HD:, at].astype(BF)
            kt_ref[:, at] = k
            vt[:, at] = v
            kn_ref[at, :] = k.T
            vn_ref[at, :] = v.T

    heads = [
        turned(q_ref[h * HD : (h + 1) * HD, :], cosine, sine).astype(BF) * BF(HD**-0.5)
        for h in range(group)
    ]
    qt_ref[...] = jnp.concatenate(heads, axis=0)
    q4 = jnp.concatenate(heads, axis=1)
    starts = start_ref[0]
    acc[...] = jnp.zeros_like(acc)
    top[...] = jnp.full_like(top, NEG)
    total[...] = jnp.zeros_like(total)

    def block(j, masked):
        at = pl.multiple_of(j * BK, BK)
        s = dot_f32(kn_ref[pl.ds(at, BK), :], q4)
        if masked:
            s = jnp.where(allowed_block(j, BK, i * rows, rows, wide, starts), s, NEG)
        old = top[...]
        new = jnp.maximum(old, jnp.max(s, axis=0, keepdims=True))
        p = jnp.exp(s - new)
        keep = jnp.exp(old - new)
        top[...] = new
        total[...] = total[...] * keep + jnp.sum(p, axis=0, keepdims=True)
        acc[...] = acc[...] * keep + dot_f32(vt[:, pl.ds(at, BK)], p.astype(BF))

    three_loops(bounds_ref, i, block)
    o = acc[...] / total[...]
    o_ref[0] = heads_tall(o, group).astype(BF)
    lse_ref[0] = top[...] + jnp.log(total[...])


def backward_kernel(
    group, skip, final, bounds_ref, q_ref, k_ref, kt_ref, v_ref, cos_ref, sin_ref, start_ref,
    o_ref, do_ref, lse_ref, *rest
):
    if final:
        dk_before, dv_before, dq_ref, dkv_ref, dk, dv, acc = rest
    else:
        dq_ref, dk, dv, acc = rest
    step = pl.program_id(0)
    i = step + skip
    rows = q_ref.shape[1]
    wide = rows * group
    q4 = heads_wide(q_ref[...], group)
    g4 = heads_wide(do_ref[0], group)
    o4 = heads_wide(o_ref[0], group)
    delta = jnp.sum(g4.astype(F32) * o4.astype(F32), axis=0, keepdims=True)
    q4t = q4.T
    g4t = g4.T
    starts = start_ref[0]
    lse = lse_ref[0]
    acc[...] = jnp.zeros_like(acc)

    @pl.when(step == 0)
    def _():
        dk[...] = dk_before[...] if final else jnp.zeros_like(dk)
        dv[...] = dv_before[...] if final else jnp.zeros_like(dv)

    def block(j, masked):
        at = pl.multiple_of(j * BK, BK)
        s = dot_f32(k_ref[pl.ds(at, BK), :], q4)
        p = jnp.exp(s - lse)
        if masked:
            p = jnp.where(allowed_block(j, BK, i * rows, rows, wide, starts), p, 0.0)
        dp = dot_f32(v_ref[pl.ds(at, BK), :], g4)
        ds = (p * (dp - delta)).astype(BF)
        dv[pl.ds(at, BK), :] += dot_f32(p.astype(BF), g4t)
        dk[pl.ds(at, BK), :] += dot_f32(ds, q4t)
        acc[...] += dot_f32(kt_ref[:, pl.ds(at, BK)], ds)

    three_loops(bounds_ref, i, block)
    here = pl.ds(pl.multiple_of(i * rows, rows), rows)
    cosine, sine = cos_ref[:, here], sin_ref[:, here]
    for h in range(group):
        dq = acc[:, h * rows : (h + 1) * rows] * (HD**-0.5)
        dq_ref[h * HD : (h + 1) * HD, :] = turned_back(dq, cosine, sine).astype(BF)

    if final:

        @pl.when(step == pl.num_programs(0) - 1)
        def _():
            for part in range(dk.shape[0] // BK):
                at = pl.ds(part * BK, BK)
                dk_t = turned_back(dk[at, :].T, cos_ref[:, at], sin_ref[:, at])
                dkv_ref[:HD, at] = dk_t.astype(BF)
                dkv_ref[HD:, at] = dv[at, :].T.astype(BF)


def whole_spec(shape):
    return pl.BlockSpec(shape, lambda i, b: (0,) * len(shape))


def attend(bounds, projected, cosine, sine, starts, group, senders, local):
    length = projected.shape[1]
    blocks = length // BQ
    per = local // BQ
    wide = group * HD
    piece = pl.BlockSpec((1, wide, BQ), lambda i, b: (i // per, 0, i % per))
    line = pl.BlockSpec((1, 1, group * BQ), lambda i, b: (i, 0, 0))
    flat = pl.BlockSpec((wide, BQ), lambda i, b: (0, i))
    return pl.pallas_call(
        functools.partial(forward_kernel, group),
        out_shape=(
            jax.ShapeDtypeStruct((senders, wide, local), BF),
            jax.ShapeDtypeStruct((blocks, 1, group * BQ), F32),
            jax.ShapeDtypeStruct((wide, length), BF),
            jax.ShapeDtypeStruct((HD, length), BF),
            jax.ShapeDtypeStruct((length, HD), BF),
            jax.ShapeDtypeStruct((length, HD), BF),
        ),
        grid_spec=pltpu.PrefetchScalarGridSpec(
            num_scalar_prefetch=1,
            grid=(blocks,),
            in_specs=[
                flat,
                pl.BlockSpec((2 * HD, length), lambda i, b: (wide // (2 * HD), 0)),
                whole_spec((HALF, length)),
                whole_spec((HALF, length)),
                line,
            ],
            out_specs=(
                piece,
                line,
                flat,
                whole_spec((HD, length)),
                whole_spec((length, HD)),
                whole_spec((length, HD)),
            ),
            scratch_shapes=[
                pltpu.VMEM((HD, length), BF),
                pltpu.VMEM((HD, group * BQ), F32),
                pltpu.VMEM((1, group * BQ), F32),
                pltpu.VMEM((1, group * BQ), F32),
            ],
        ),
        compiler_params=pltpu.CompilerParams(
            dimension_semantics=("arbitrary",), vmem_limit_bytes=VMEM_LIMIT
        ),
        cost_estimate=pl.CostEstimate(
            flops=40 * group * length * length * HD // 2,
            bytes_accessed=4 * group * length * HD * 2,
            transcendentals=group * length * length // 4,
        ),
        name="attend",
    )(bounds, projected, projected, cosine, sine, starts)


def attend_back(
    bounds, qt, k, kt, v, cosine, sine, starts, o, do, lse, group, skip, blocks, before
):
    length = k.shape[0]
    senders, _, local = o.shape
    per = local // BQ
    final = before is not None
    wide = group * HD
    piece = pl.BlockSpec((1, wide, BQ), lambda i, b: ((i + skip) // per, 0, (i + skip) % per))
    line = pl.BlockSpec((1, 1, group * BQ), lambda i, b: (i + skip, 0, 0))
    tall = whole_spec((length, HD))
    arrays = [qt, k, kt, v, cosine, sine, starts, o, do, lse]
    in_specs = [
        pl.BlockSpec((wide, BQ), lambda i, b: (0, i + skip)),
        tall,
        whole_spec((HD, length)),
        tall,
        whole_spec((HALF, length)),
        whole_spec((HALF, length)),
        line,
        piece,
        piece,
        line,
    ]
    out_specs = [pl.BlockSpec((wide, BQ), lambda i, b: (0, i))]
    out_shape = [jax.ShapeDtypeStruct((wide, blocks * BQ), BF)]
    scratch = [pltpu.VMEM((HD, group * BQ), F32)]
    if final:
        arrays += list(before)
        in_specs += [tall, tall]
        out_specs += [whole_spec((2 * HD, length))]
        out_shape += [jax.ShapeDtypeStruct((2 * HD, length), BF)]
        scratch = [pltpu.VMEM((length, HD), F32), pltpu.VMEM((length, HD), F32)] + scratch
    else:
        out_specs += [tall, tall]
        out_shape += [jax.ShapeDtypeStruct((length, HD), F32)] * 2
    return pl.pallas_call(
        functools.partial(backward_kernel, group, skip, final),
        out_shape=out_shape,
        grid_spec=pltpu.PrefetchScalarGridSpec(
            num_scalar_prefetch=1,
            grid=(blocks,),
            in_specs=in_specs,
            out_specs=out_specs,
            scratch_shapes=scratch,
        ),
        compiler_params=pltpu.CompilerParams(
            dimension_semantics=("arbitrary",), vmem_limit_bytes=VMEM_LIMIT
        ),
        cost_estimate=pl.CostEstimate(
            flops=25 * group * length * length * HD // 2,
            bytes_accessed=8 * group * length * HD,
            transcendentals=group * length * length // 8,
        ),
        name="attend_back",
    )(bounds, *arrays)


def project_kernel(cols, x_ref, w_ref, n_ref, p_ref, wt_ref):
    @pl.when(pl.program_id(0) == 0)
    def _():
        wt_ref[...] = w_ref[...].T

    wide = x_ref[0].astype(F32)
    scale = lax.rsqrt(jnp.mean(wide * wide, axis=-1, keepdims=True) + EPS)
    gain = wt_ref[pl.ds(cols, 8), :].astype(F32)[0:1]
    normed = (wide * scale * gain).astype(BF)
    n_ref[0] = normed
    p_ref[...] = lax.dot_general(
        wt_ref[:cols, :], normed, (((1,), (1,)), ((), ())), preferred_element_type=F32
    )


def project(x_all, w_ext, cols):
    count, local, width = x_all.shape
    wide = w_ext.shape[1]
    block = pl.BlockSpec((1, local, width), lambda i: (i, 0, 0))
    return pl.pallas_call(
        functools.partial(project_kernel, cols),
        out_shape=(
            jax.ShapeDtypeStruct(x_all.shape, BF),
            jax.ShapeDtypeStruct((cols, count * local), F32),
            jax.ShapeDtypeStruct((wide, width), BF),
        ),
        grid=(count,),
        in_specs=[block, pl.BlockSpec((width, wide), lambda i: (0, 0))],
        out_specs=(
            block,
            pl.BlockSpec((cols, local), lambda i: (0, i)),
            pl.BlockSpec((wide, width), lambda i: (0, 0)),
        ),
        compiler_params=pltpu.CompilerParams(
            dimension_semantics=("arbitrary",), vmem_limit_bytes=VMEM_LIMIT
        ),
        cost_estimate=pl.CostEstimate(
            flops=2 * cols * width * count * local,
            bytes_accessed=4 * width * count * local,
            transcendentals=0,
        ),
        name="project",
    )(x_all, w_ext)


def ffn_kernel(
    places_ref, first_ref, second_ref, dy_ref, gate_ref, up_ref, down_ref, *rest
):
    act_ref, dg_ref, du_ref, n_ref, ya_ref, yb_ref, pa_ref, pb_ref = rest[-8:]
    which = pl.program_id(0)
    n = jnp.where(which == 0, first_ref[...], second_ref[...])
    n_ref[0] = n
    dy = dy_ref[0]
    across = (((1,), (1,)), ((), ()))
    gate = dot_f32(n, gate_ref[...])
    up = dot_f32(n, up_ref[...])
    d_act = lax.dot_general(dy, down_ref[...], across, preferred_element_type=F32)
    sig = jax.nn.sigmoid(gate)
    silu = gate * sig
    act = (silu * up).astype(BF)
    d_gate = (d_act * up * sig * (1.0 + gate * (1.0 - sig))).astype(BF)
    d_up = (d_act * silu).astype(BF)
    act_ref[0] = act
    dg_ref[0] = d_gate
    du_ref[0] = d_up
    split = ya_ref.shape[-1]
    ya_ref[0] = dot_f32(act, down_ref[:, :split]).astype(BF)
    yb_ref[0] = dot_f32(act, down_ref[:, split:]).astype(BF)
    part = lax.dot_general(d_gate, gate_ref[...], across, preferred_element_type=F32)
    part += lax.dot_general(d_up, up_ref[...], across, preferred_element_type=F32)
    part = part.astype(BF)

    @pl.when(which == 0)
    def _():
        pa_ref[...] = part

    @pl.when(which == 1)
    def _():
        pb_ref[...] = part


def ffn_chunk(places, first, second, dy_all, gate_w, up_w, down_w, kept):
    local, width = first.shape
    hidden = gate_w.shape[1]
    tall = min(512, local)
    tiles = local // tall
    count = dy_all.shape[0]

    def at_place(last):
        return pl.BlockSpec((1, tall, last), lambda i, t, p: (p[i], t, 0))

    ahead = pl.BlockSpec((tall, width), lambda i, t, p: (jnp.where(i == 0, t, tiles - 1), 0))
    behind = pl.BlockSpec((tall, width), lambda i, t, p: (jnp.where(i == 0, 0, t), 0))

    def held(shape):
        return pl.BlockSpec(shape, lambda i, t, p: (0, 0), pipeline_mode=pl.Buffered(1))

    in_specs = [
        ahead, behind, at_place(width), held((width, hidden)), held((width, hidden)),
        held((hidden, width)),
    ]
    arrays = [first, second, dy_all, gate_w, up_w, down_w]
    aliases = {}
    if kept is not None:
        in_specs += [pl.BlockSpec(memory_space=pl.ANY)] * 6
        arrays += list(kept)
        aliases = {7 + n: n for n in range(6)}
    narrow = jax.ShapeDtypeStruct((count, local, hidden), BF)
    broad = jax.ShapeDtypeStruct((count, local, width), BF)
    part = jax.ShapeDtypeStruct((count, local, width // 2), BF)
    single = jax.ShapeDtypeStruct((local, width), BF)
    outs = pl.pallas_call(
        ffn_kernel,
        out_shape=(narrow, narrow, narrow, broad, part, part, single, single),
        grid_spec=pltpu.PrefetchScalarGridSpec(
            num_scalar_prefetch=1,
            grid=(2, tiles),
            in_specs=in_specs,
            out_specs=(
                at_place(hidden), at_place(hidden), at_place(hidden), at_place(width),
                at_place(width // 2), at_place(width // 2), ahead, behind,
            ),
        ),
        input_output_aliases=aliases,
        compiler_params=pltpu.CompilerParams(
            dimension_semantics=("arbitrary", "arbitrary"), vmem_limit_bytes=VMEM_LIMIT
        ),
        cost_estimate=pl.CostEstimate(
            flops=2 * 6 * 2 * local * width * hidden,
            bytes_accessed=2 * (5 * 2 * local * width + 3 * width * hidden),
            transcendentals=2 * local * hidden,
        ),
        name="ffn",
    )(places, *arrays)
    return outs[:6], outs[6], outs[7]


def spread(out_ref, value, per, parts, rows):
    for s in range(per):
        for f in range(parts):
            at = (s * parts + f) * rows
            out_ref[f, s] = value[at : at + rows].astype(BF)


def side_kernel(per, parts, rows, n_ref, d_ref, t_ref):
    spread(t_ref, dot_f32(n_ref[...].T, d_ref[...]), per, parts, rows)


def side_terms(n2, d, count, parts):
    length, width = n2.shape
    hidden = d.shape[1]
    rows = width // (count * parts)
    per = max(1, 512 // (parts * rows))
    wide = per * parts * rows
    return pl.pallas_call(
        functools.partial(side_kernel, per, parts, rows),
        out_shape=jax.ShapeDtypeStruct((parts, count, rows, hidden), BF),
        grid=(width // wide,),
        in_specs=[
            pl.BlockSpec((length, wide), lambda i: (0, i)),
            pl.BlockSpec((length, hidden), lambda i: (0, 0), pipeline_mode=pl.Buffered(1)),
        ],
        out_specs=pl.BlockSpec((parts, per, rows, hidden), lambda i: (0, i, 0, 0)),
        compiler_params=pltpu.CompilerParams(
            dimension_semantics=("arbitrary",), vmem_limit_bytes=VMEM_LIMIT
        ),
        cost_estimate=pl.CostEstimate(
            flops=2 * length * width * hidden,
            bytes_accessed=2 * length * (width + 2 * hidden),
            transcendentals=0,
        ),
        name="side_terms",
    )(n2, d)


def down_kernel(a_ref, dy_ref, t_ref, a_t):
    @pl.when(pl.program_id(0) == 0)
    def _():
        a_t[...] = a_ref[...].T

    t_ref[...] = dot_f32(a_t[...], dy_ref[...]).astype(BF)


def down_terms_of(act, dy):
    length, width = dy.shape
    hidden = act.shape[1]
    wide = min(512, width)
    return pl.pallas_call(
        down_kernel,
        out_shape=jax.ShapeDtypeStruct((hidden, width), BF),
        grid=(width // wide,),
        in_specs=[
            pl.BlockSpec((length, hidden), lambda i: (0, 0), pipeline_mode=pl.Buffered(1)),
            pl.BlockSpec((length, wide), lambda i: (0, i)),
        ],
        out_specs=pl.BlockSpec((hidden, wide), lambda i: (0, i)),
        scratch_shapes=[pltpu.VMEM((hidden, length), BF)],
        compiler_params=pltpu.CompilerParams(
            dimension_semantics=("arbitrary",), vmem_limit_bytes=VMEM_LIMIT
        ),
        cost_estimate=pl.CostEstimate(
            flops=2 * length * width * hidden,
            bytes_accessed=2 * length * (width + hidden),
            transcendentals=0,
        ),
        name="down_terms",
    )(act, dy)


def attn_kernel(per, parts, rows, d_ref, n_ref, t_ref):
    spread(t_ref, dot_f32(d_ref[...], n_ref[...]).T, per, parts, rows)


def attn_terms_of(d_t, n1, count, parts):
    cols, length = d_t.shape
    width = n1.shape[1]
    rows = width // (count * parts)
    per = max(1, 512 // (parts * rows))
    wide = per * parts * rows
    return pl.pallas_call(
        functools.partial(attn_kernel, per, parts, rows),
        out_shape=jax.ShapeDtypeStruct((parts, count, rows, cols), BF),
        grid=(width // wide,),
        in_specs=[
            pl.BlockSpec((cols, length), lambda i: (0, 0), pipeline_mode=pl.Buffered(1)),
            pl.BlockSpec((length, wide), lambda i: (0, i)),
        ],
        out_specs=pl.BlockSpec((parts, per, rows, cols), lambda i: (0, i, 0, 0)),
        compiler_params=pltpu.CompilerParams(
            dimension_semantics=("arbitrary",), vmem_limit_bytes=VMEM_LIMIT
        ),
        cost_estimate=pl.CostEstimate(
            flops=2 * length * width * cols,
            bytes_accessed=2 * length * (width + cols),
            transcendentals=0,
        ),
        name="attn_terms",
    )(d_t, n1)


def tail_kernel(
    parts, cols, d_ref, w_ref, x_ref, dh_ref, n_ref, grad_ref, back_ref,
    even, side_send, side_recv, landing, n_buf, terms, hop_send, hop_recv, last, mid,
    send, arrive, n_sem, own_sem,
):
    me = lax.axis_index("seq")
    z = lax.axis_index("fsdp")
    after_z, before_z = (z + 1) % parts, (z + parts - 1) % parts
    local, width = x_ref.shape
    half = local // 2
    low, high = pl.ds(0, half), pl.ds(half, half)
    barrier = pltpu.get_barrier_semaphore()
    for bit in (1, 2, 4):
        pl.semaphore_signal(barrier, inc=1, device_id=(me ^ bit, z), device_id_type=MESH)
    for other in (after_z, before_z):
        pl.semaphore_signal(barrier, inc=1, device_id=(me, other), device_id_type=MESH)
    pl.semaphore_wait(barrier, 5)
    made = {}

    def start(name, source, target, device):
        n = len(made)
        copy = pltpu.make_async_remote_copy(
            src_ref=source, dst_ref=target, send_sem=send.at[n], recv_sem=arrive.at[n],
            device_id=device, device_id_type=MESH,
        )
        made[name] = copy
        copy.start()

    def to_bit(name, bit, source, target):
        start(name, source, target, (me ^ bit, z))

    def arrived(*names):
        for name in names:
            made[name].wait_recv()

    chunk = n_buf.shape[2]
    chunks = width // chunk

    def fetch(i):
        return pltpu.make_async_copy(
            n_ref.at[:, pl.ds(i * chunk, chunk)], n_buf.at[i % 2], n_sem.at[i % 2]
        )

    fetch(0).start()
    tile = 512

    def product(c, out):
        at = pl.multiple_of((me ^ c) * local, local)
        d = d_ref[:, pl.ds(at, local)].T

        def one(t, carry):
            here = pl.ds(pl.multiple_of(t * tile, tile), tile)
            out[:, here] = dot_f32(d, w_ref[pl.ds(0, cols), here]).astype(BF)
            return carry

        lax.fori_loop(0, width // tile, one, 0)

    def chip(pair):
        product(2 * pair + 1, side_send.at[pair])
        to_bit("s" + str(pair), 1, side_send.at[pair], side_recv.at[pair])
        product(2 * pair, even.at[pair])

    def add_side(pair, part):
        even[pair, part] = (
            even[pair, part].astype(F32) + side_recv[pair, part].astype(F32)
        ).astype(BF)

    chip(3)
    chip(1)
    arrived("s3")
    add_side(3, low)
    to_bit("far_x", 2, even.at[3, low], landing.at[0])
    add_side(3, high)
    to_bit("far_y", 4, even.at[3, high], landing.at[1])
    chip(2)
    arrived("s1")
    add_side(1, low)
    to_bit("first_x", 2, even.at[1, low], landing.at[2])
    add_side(1, high)
    chip(0)
    arrived("s2")
    add_side(2, high)
    to_bit("second_y", 4, even.at[2, high], landing.at[3])
    add_side(2, low)

    count, rows = back_ref.shape[0], back_ref.shape[1]
    per = chunk // (parts * rows)
    for i in range(chunks):
        if i + 1 < chunks:
            fetch(i + 1).start()
        fetch(i).wait()
        value = dot_f32(d_ref[...], n_buf[i % 2]).T
        for s in range(per):
            for f in range(parts):
                at = (s * parts + f) * rows
                terms[f, i * per + s] = value[at : at + rows].astype(BF)
    start("r1", terms.at[before_z], hop_recv.at[0], (me, after_z))

    def add_far(pair, part, slot):
        even[pair, part] = (even[pair, part].astype(F32) + landing[slot].astype(F32)).astype(BF)

    arrived("far_x")
    add_far(2, low, 0)
    to_bit("first_y", 4, even.at[2, low], landing.at[4])
    arrived("far_y")
    add_far(1, high, 1)
    to_bit("second_x", 2, even.at[1, high], landing.at[5])
    arrived("s0")
    for step in range(1, parts):
        arrived("r" + str(step))
        state = hop_recv[step - 1].astype(F32)
        state = state + terms[(z + 2 * parts - 1 - step) % parts].astype(F32)
        if step < parts - 1:
            hop_send[step - 1] = state.astype(BF)
            start("r" + str(step + 1), hop_send.at[step - 1], hop_recv.at[step], (me, after_z))
        else:
            last[...] = state.astype(BF)

    mine = pltpu.make_async_copy(last.at[me], back_ref.at[me], own_sem.at[0])
    mine.start()
    to_bit("b3", 2, last.at[me ^ 6], mid.at[4])
    to_bit("a2", 1, last.at[me ^ 3], mid.at[1])
    to_bit("a4", 1, last.at[me ^ 7], mid.at[3])
    to_bit("a3", 1, last.at[me ^ 5], mid.at[2])
    to_bit("a1", 1, last.at[me ^ 1], back_ref.at[me])
    to_bit("b1", 2, last.at[me ^ 2], back_ref.at[me])
    to_bit("c1", 4, last.at[me ^ 4], back_ref.at[me])
    arrived("a4", "a2", "a3")
    to_bit("b4", 2, mid.at[3], mid.at[5])
    to_bit("b2", 2, mid.at[1], back_ref.at[me ^ 1])
    to_bit("c2", 4, mid.at[2], back_ref.at[me ^ 1])
    arrived("b3")
    to_bit("c3", 4, mid.at[4], back_ref.at[me ^ 2])
    arrived("b4")
    to_bit("c4", 4, mid.at[5], back_ref.at[me ^ 3])

    arrived("first_x", "second_y", "first_y", "second_x")
    gain = w_ref[pl.ds(cols, 8), :].astype(F32)[0:1]
    tall = 64

    def finish(first_slot, second_slot, offset):
        def one(t, carry):
            from_half = pl.ds(pl.multiple_of(t * tall, tall), tall)
            at = pl.ds(pl.multiple_of(t * tall + offset, tall), tall)
            dn = even[0, at].astype(F32) + side_recv[0, at].astype(F32)
            dn = dn + landing[first_slot, from_half].astype(F32)
            dn = dn + landing[second_slot, from_half].astype(F32)
            x = x_ref[at].astype(F32)
            r = lax.rsqrt(jnp.mean(x * x, axis=-1, keepdims=True) + EPS)
            m = x * r
            e = dn * gain
            inner = jnp.mean(e * m, axis=-1, keepdims=True)
            grad_ref[at] = dh_ref[at] + r * (e - m * inner)
            return carry

        lax.fori_loop(0, half // tall, one, 0)

    finish(2, 4, 0)
    finish(3, 5, half)
    arrived("a1", "b1", "c1", "b2", "c2", "c3", "c4")
    mine.wait()
    for copy in made.values():
        copy.wait_send()


def tail(d_t, wt_ext, x, dh1, n1, cols, count, parts):
    local, width = x.shape
    length = n1.shape[0]
    rows = width // (count * parts)
    half = local // 2
    chunk = 512
    anyspace = pl.BlockSpec(memory_space=pl.ANY)
    vmem = pl.BlockSpec(memory_space=pltpu.VMEM)
    copies = 4 + 6 + parts - 1 + 12
    block = (count, rows, cols)
    return pl.pallas_call(
        functools.partial(tail_kernel, parts, cols),
        out_shape=(
            jax.ShapeDtypeStruct((local, width), F32),
            jax.ShapeDtypeStruct(block, BF),
        ),
        in_specs=[vmem, vmem, vmem, vmem, anyspace],
        out_specs=(vmem, anyspace),
        scratch_shapes=[
            pltpu.VMEM((4, local, width), BF),
            pltpu.VMEM((4, local, width), BF),
            pltpu.VMEM((4, local, width), BF),
            pltpu.VMEM((6, half, width), BF),
            pltpu.VMEM((2, length, chunk), BF),
            pltpu.VMEM((parts,) + block, BF),
            pltpu.VMEM((max(1, parts - 2),) + block, BF),
            pltpu.VMEM((parts - 1,) + block, BF),
            pltpu.VMEM(block, BF),
            pltpu.VMEM((6, rows, cols), BF),
            pltpu.SemaphoreType.DMA((copies,)),
            pltpu.SemaphoreType.DMA((copies,)),
            pltpu.SemaphoreType.DMA((2,)),
            pltpu.SemaphoreType.DMA((1,)),
        ],
        compiler_params=pltpu.CompilerParams(
            collective_id=1, has_side_effects=True, vmem_limit_bytes=62 * 1024 * 1024
        ),
        cost_estimate=pl.CostEstimate(
            flops=1 << 30, bytes_accessed=1 << 20, transcendentals=0
        ),
        name="tail",
    )(d_t, wt_ext, x, dh1, n1)


def start_kernel(
    parts, x_ref, attn_ref, ffn_ref, out_ref, down_ref, x_all, attn_all, ffn_mine, out_all,
    down_all, attn_mid, ffn_mid, send, arrive, local_sem,
):
    me = lax.axis_index("seq")
    z = lax.axis_index("fsdp")
    after_z, before_z = (z + 1) % parts, (z + parts - 1) % parts
    half = x_ref.shape[0] // 2
    barrier = pltpu.get_barrier_semaphore()
    for bit in (1, 2, 4):
        pl.semaphore_signal(barrier, inc=1, device_id=(me ^ bit, z), device_id_type=MESH)
    for other in (after_z, before_z):
        pl.semaphore_signal(barrier, inc=1, device_id=(me, other), device_id_type=MESH)
    pl.semaphore_wait(barrier, 5)
    made = {}

    def start(name, source, target, device):
        n = len(made)
        copy = pltpu.make_async_remote_copy(
            src_ref=source, dst_ref=target, send_sem=send.at[n], recv_sem=arrive.at[n],
            device_id=device, device_id_type=MESH,
        )
        made[name] = copy
        copy.start()

    def to_bit(name, bit, source, target):
        start(name, source, target, (me ^ bit, z))

    def arrived(*names):
        for name in names:
            made[name].wait_recv()

    held = [
        pltpu.make_async_copy(x_ref, x_all.at[me], local_sem.at[0]),
        pltpu.make_async_copy(attn_ref.at[me], attn_all.at[z, me], local_sem.at[1]),
        pltpu.make_async_copy(ffn_ref.at[me], ffn_mine.at[me], local_sem.at[2]),
        pltpu.make_async_copy(out_ref, out_all.at[z], local_sem.at[3]),
        pltpu.make_async_copy(down_ref, down_all.at[z], local_sem.at[4]),
    ]
    for copy in held:
        copy.start()

    def swap_first(tag, source, final, mid):
        to_bit(tag + "a2", 1, source.at[me ^ 3], mid.at[1])
        to_bit(tag + "a4", 1, source.at[me ^ 7], mid.at[3])
        to_bit(tag + "a3", 1, source.at[me ^ 5], mid.at[2])
        to_bit(tag + "a1", 1, source.at[me ^ 1], final.at[me])

    def swap_second(tag, source, final, mid):
        to_bit(tag + "b3", 2, source.at[me ^ 6], mid.at[4])
        to_bit(tag + "b1", 2, source.at[me ^ 2], final.at[me])
        arrived(tag + "a4", tag + "a2")
        to_bit(tag + "b4", 2, mid.at[3], mid.at[5])
        to_bit(tag + "b2", 2, mid.at[1], final.at[me ^ 1])

    def swap_third(tag, source, final, mid):
        to_bit(tag + "c1", 4, source.at[me ^ 4], final.at[me])
        arrived(tag + "a3")
        to_bit(tag + "c2", 4, mid.at[2], final.at[me ^ 1])
        arrived(tag + "b3")
        to_bit(tag + "c3", 4, mid.at[4], final.at[me ^ 2])
        arrived(tag + "b4")
        to_bit(tag + "c4", 4, mid.at[5], final.at[me ^ 3])

    def swap_end(tag):
        arrived(*[tag + n for n in ("a1", "b1", "c1", "b2", "c2", "c3", "c4")])

    def around(tag, step, whole):
        if step > 1:
            arrived(tag + str(step - 1))
        at = (z + parts + 1 - step) % parts
        start(tag + str(step), whole.at[at], whole.at[at], (me, after_z))

    attn_sets = (attn_ref, attn_all.at[z], attn_mid)
    ffn_sets = (ffn_ref, ffn_mine, ffn_mid)
    start("o1", out_ref, out_all.at[z], (me, after_z))
    swap_first("attn", *attn_sets)
    swap_second("attn", *attn_sets)
    to_bit("x2", 2, x_ref, x_all.at[me])
    swap_third("attn", *attn_sets)
    to_bit("x4", 4, x_ref, x_all.at[me])
    to_bit("x1", 1, x_ref, x_all.at[me])
    swap_first("ffn", *ffn_sets)
    swap_end("attn")
    held[1].wait()
    around("z", 1, attn_all)
    held[4].wait()
    around("d", 1, down_all)
    for step in range(2, parts):
        around("o", step, out_all)
        around("z", step, attn_all)
    arrived("x2")
    to_bit("x3", 1, x_all.at[me ^ 2], x_all.at[me ^ 2])
    to_bit("f1", 4, x_all.at[me ^ 2, pl.ds(0, half)], x_all.at[me ^ 2, pl.ds(0, half)])
    arrived("x4")
    to_bit("x5", 1, x_all.at[me ^ 4], x_all.at[me ^ 4])
    to_bit("f2", 2, x_all.at[me ^ 4, pl.ds(half, half)], x_all.at[me ^ 4, pl.ds(half, half)])
    around("d", 2, down_all)
    swap_second("ffn", *ffn_sets)
    swap_third("ffn", *ffn_sets)
    for step in range(3, parts):
        around("d", step, down_all)
    arrived("f1", "f2")
    to_bit("x7", 1, x_all.at[me ^ 6], x_all.at[me ^ 6])
    swap_end("ffn")
    arrived("x1", "x3", "x5", "x7", "z" + str(parts - 1), "o" + str(parts - 1))
    arrived("d" + str(parts - 1))
    for copy in made.values():
        copy.wait_send()
    for copy in (held[0], held[2], held[3]):
        copy.wait()


def start_gather(x, attn_send, ffn_send, w_out, w_down, count, parts):
    anyspace = pl.BlockSpec(memory_space=pl.ANY)
    copies = 8 + 2 * 12 + 3 * (parts - 1)
    shapes = (
        jax.ShapeDtypeStruct((count,) + x.shape, BF),
        jax.ShapeDtypeStruct((parts,) + attn_send.shape, BF),
        jax.ShapeDtypeStruct(ffn_send.shape, BF),
        jax.ShapeDtypeStruct((parts,) + w_out.shape, BF),
        jax.ShapeDtypeStruct((parts,) + w_down.shape, BF),
        jax.ShapeDtypeStruct((6,) + attn_send.shape[1:], BF),
        jax.ShapeDtypeStruct((6,) + ffn_send.shape[1:], BF),
    )
    return pl.pallas_call(
        functools.partial(start_kernel, parts),
        out_shape=shapes,
        in_specs=[anyspace] * 5,
        out_specs=(anyspace,) * 7,
        scratch_shapes=[
            pltpu.SemaphoreType.DMA((copies,)),
            pltpu.SemaphoreType.DMA((copies,)),
            pltpu.SemaphoreType.DMA((5,)),
        ],
        compiler_params=pltpu.CompilerParams(
            collective_id=0, has_side_effects=True, vmem_limit_bytes=8 * 1024 * 1024
        ),
        name="start_gather",
    )(x, attn_send, ffn_send, w_out, w_down)[:5]


def ring(axis):
    count = lax.axis_size(axis)
    return [(n, (n + 1) % count) for n in range(count)]


def hop(*blocks):
    return [lax.ppermute(block, "fsdp", ring("fsdp")) for block in blocks]


def collect(pieces, axis):
    count = lax.axis_size(axis)
    me = lax.axis_index(axis)
    whole = jnp.zeros((count,) + pieces[0].shape, pieces[0].dtype)
    for back, piece in enumerate(pieces):
        whole = lax.dynamic_update_index_in_dim(whole, piece, (me + count - back) % count, 0)
    return whole


def term_of(terms, step):
    count = lax.axis_size("fsdp")
    me = lax.axis_index("fsdp")
    return lax.dynamic_index_in_dim(terms, (me + 2 * count - 1 - step) % count, 0, False)


def launch(states):
    return hop(*[state.astype(BF) for state in states])


def landed(moved, terms, step):
    return [m.astype(F32) + term_of(t, step).astype(F32) for m, t in zip(moved, terms)]


def ring_finish(moved, terms, step):
    states = landed(moved, terms, step)
    for n in range(step + 1, lax.axis_size("fsdp")):
        states = landed(launch(states), terms, n)
    return states


def fence(*values):
    return lax.optimization_barrier(values)


def swap(block, bit):
    count = lax.axis_size("seq")
    return lax.ppermute(block, "seq", [(n, n ^ bit) for n in range(count)])


def gather_plain(block):
    me = lax.axis_index("seq")
    whole = lax.all_gather(block, "seq", axis=0, tiled=False)
    return [lax.dynamic_index_in_dim(whole, me ^ c, 0, False) for c in range(whole.shape[0])]


def scatter_plain(parts):
    me = lax.axis_index("seq")
    whole = jnp.zeros((len(parts),) + parts[0].shape, BF)
    for c, part in enumerate(parts):
        whole = lax.dynamic_update_index_in_dim(whole, part.astype(BF), me ^ c, 0)
    return lax.psum_scatter(whole, "seq", scatter_dimension=0, tiled=False).astype(F32)


def far_halves(over_x, over_y):
    half = over_x.shape[0] // 2
    return swap(over_x[:half], 4), swap(over_y[half:], 2)


def chip_sum(own, other):
    return own.astype(F32) + swap(other, 1).astype(F32)


def exchange(array):
    return lax.all_to_all(array, "seq", split_axis=0, concat_axis=0, tiled=True)


def document_starts(flags_all):
    length = flags_all.shape[0]
    lanes = 128
    table = flags_all.reshape(length // lanes, lanes)
    place = jnp.arange(length, dtype=jnp.int32).reshape(table.shape)
    marked = jnp.where((table != 0) & (place > 0), place, 0)
    inside = jnp.arange(lanes)[None, :] <= jnp.arange(lanes)[:, None]
    local = jnp.max(jnp.where(inside[None], marked[:, None, :], 0), axis=-1)
    rows = jnp.max(marked, axis=1)
    count = length // lanes
    before = jnp.arange(count)[None, :] < jnp.arange(count)[:, None]
    carried = jnp.max(jnp.where(before, rows[None, :], 0), axis=-1)
    return jnp.maximum(local, carried[:, None]).reshape(length)


def body(
    tokens, doc_starts, gain_attn, w_query, w_key, w_value, w_out, gain_ffn, w_gate, w_up, w_down,
    cotangent,
):
    streams, local, width = tokens.shape
    assert streams == 1
    count = lax.axis_size("seq")
    parts = lax.axis_size("fsdp")
    me = lax.axis_index("seq")
    cube = count == 8
    length = local * count
    half = local // 2
    group = H // count
    share = (H // KV) // group
    rows = w_query.shape[0]
    hidden = w_gate.shape[1] // count
    group_width = group * HD
    attn_cols = group_width + 2 * HD
    flag_cols = local // rows
    extra_cols = 128
    sheet = (length, width)

    own = tokens[0]
    attn_send = jnp.concatenate(
        [
            w_query.reshape(rows, count, group_width),
            jnp.repeat(w_key.reshape(rows, KV, HD), share, axis=1),
            jnp.repeat(w_value.reshape(rows, KV, HD), share, axis=1),
        ],
        axis=2,
    ).transpose(1, 0, 2)
    extra = jnp.concatenate(
        [
            gain_attn[:, None],
            gain_ffn[:, None],
            doc_starts[0].astype(BF).reshape(rows, flag_cols),
            jnp.zeros((rows, extra_cols - 2 - flag_cols), BF),
        ],
        axis=1,
    )
    attn_send = jnp.concatenate(
        [attn_send, jnp.broadcast_to(extra[None], (count,) + extra.shape)], axis=2
    )
    ffn_send = jnp.concatenate(
        [w_gate.reshape(rows, count, hidden), w_up.reshape(rows, count, hidden)], axis=0
    ).transpose(1, 0, 2)
    z = lax.axis_index("fsdp")
    if cube:
        x_all, attn_all, ffn_part, out_part, down_w = start_gather(
            own, attn_send, ffn_send, w_out, w_down, count, parts
        )
    else:
        x_all = lax.all_gather(own, "seq", axis=0, tiled=False)
        attn_all = lax.all_gather(exchange(attn_send), "fsdp", axis=0, tiled=False)
        ffn_part = exchange(ffn_send)
        out_part = lax.all_gather(w_out, "fsdp", axis=0, tiled=False)
        down_w = lax.all_gather(w_down, "fsdp", axis=0, tiled=False)
    down_w = down_w.reshape(hidden, width)
    dy = cotangent[0]
    own, x_all, attn_all, ffn_part, out_part, dy = fence(
        own, x_all, attn_all, ffn_part, out_part, dy
    )
    ffn_pieces = [[ffn_part.reshape(count, 2, rows, hidden)]]

    dy_all = lax.all_gather(dy, "seq", axis=0, tiled=False)
    if len(ffn_pieces) < parts:
        ffn_pieces.append(hop(*ffn_pieces[-1]))
    flags = lax.dynamic_index_in_dim(attn_all, z, 0, False)
    flags = flags[:, :, attn_cols + 2 : attn_cols + 2 + flag_cols].reshape(length)
    last = document_starts(flags)
    position = (jnp.arange(length, dtype=jnp.int32) - last).astype(F32)
    frequency = jnp.exp(jnp.arange(HALF, dtype=F32) * (-2.0 * math.log(10000.0) / HD))
    angle = frequency[:, None] * position[None, :]
    cosine, sine = jnp.cos(angle), jnp.sin(angle)
    blocks = length // BQ
    by_block = last.reshape(blocks, BQ)
    starts = jnp.tile(by_block, (1, group)).reshape(blocks, 1, group * BQ)
    first_row = jnp.arange(blocks, dtype=jnp.int32) * BQ
    low = by_block[:, 0] // BK
    high = (first_row + BQ + BK - 1) // BK
    begin = jnp.minimum((by_block[:, -1] + BK - 1) // BK, high)
    end = jnp.maximum((first_row + 1) // BK, begin)
    bounds = jnp.stack([low, begin, end, high], axis=1)
    w_ext = attn_all.transpose(1, 0, 2, 3).reshape(width, attn_cols + extra_cols)
    n1_all, projected, wt_ext = project(x_all, w_ext, attn_cols)
    attn_t = wt_ext[:attn_cols]
    gain_one = wt_ext[attn_cols].astype(F32)
    gain_two = wt_ext[attn_cols + 1].astype(F32)
    projected, cosine, sine, starts, bounds, ffn_last, out_part = fence(
        projected, cosine, sine, starts, bounds, ffn_pieces[-1], out_part
    )
    ffn_pieces[-1] = ffn_last

    out_w = lax.all_gather(out_part.reshape(parts * rows, width), "seq", axis=0, tiled=True)
    if len(ffn_pieces) < parts:
        ffn_pieces.append(hop(*ffn_pieces[-1]))
    o_heads, lse, q_t, k_t, k_n, v_n = attend(
        bounds, projected, cosine, sine, starts, group, count, local
    )
    o_heads, lse, q_t, k_t, k_n, v_n, ffn_last, dy_all = fence(
        o_heads, lse, q_t, k_t, k_n, v_n, ffn_pieces[-1], dy_all
    )
    ffn_pieces[-1] = ffn_last

    while len(ffn_pieces) < parts:
        ffn_pieces.append(hop(*ffn_pieces[-1]))
    o_t = exchange(o_heads).reshape(count * group_width, local)
    o_t, ffn_pieces = fence(o_t, ffn_pieces)

    ffn_w = collect([piece[0] for piece in ffn_pieces], "fsdp").transpose(2, 1, 0, 3, 4).reshape(2, width, hidden)
    gate_w, up_w = ffn_w[0], ffn_w[1]
    x = own.astype(F32)
    r1 = lax.rsqrt(jnp.mean(x * x, axis=-1, keepdims=True) + EPS)
    h1 = x + jnp.einsum("et,ed->td", o_t, out_w, preferred_element_type=F32)
    r2 = lax.rsqrt(jnp.mean(h1 * h1, axis=-1, keepdims=True) + EPS)
    n2 = (h1 * r2 * gain_two).astype(BF)
    n2, h1, r2 = fence(n2, h1, r2)

    def over_seq(part):
        whole = part.reshape(-1, part.shape[-1])
        return lax.psum_scatter(whole, "seq", scatter_dimension=0, tiled=True)

    kept = None

    def chunk(kept, first, second, c):
        places = jnp.stack([me ^ c, me ^ (c + 1)]).astype(jnp.int32)
        return ffn_chunk(places, first, second, dy_all, gate_w, up_w, down_w, kept)

    if cube:
        side, over_x, over_y = swap(n2, 1), swap(n2, 2), swap(n2, 4)
        side, gate_w, up_w = fence(side, gate_w, up_w)
        kept, own_a, own_b = chunk(kept, n2, side, 0)
        kept, own_a, own_b, over_x, over_y = fence(kept, own_a, own_b, over_x, over_y)

        far_a, far_b = far_halves(over_x, over_y)
        side_x, side_y, own_c = swap(over_x, 1), swap(over_y, 1), swap(own_b, 1)
        side_x, side_y, over_x, over_y, kept = fence(side_x, side_y, over_x, over_y, kept)
        kept, x_a, x_b = chunk(kept, over_x, side_x, 2)
        kept, x_a, x_b, far_a, far_b, own_c = fence(kept, x_a, x_b, far_a, far_b, own_c)

        far = jnp.concatenate([far_a, far_b], axis=0)
        side_far = swap(far, 1)
        x_sum = chip_sum(x_a, x_b)
        x_first = swap(x_sum[:half].astype(BF), 2)
        kept, y_a, y_b = chunk(kept, over_y, side_y, 4)
        kept, y_a, y_b, far, side_far, x_sum = fence(kept, y_a, y_b, far, side_far, x_sum)

        y_sum = chip_sum(y_a, y_b)
        y_second = swap(y_sum[half:].astype(BF), 4)
        kept, far_one, far_two = chunk(kept, far, side_far, 6)
        kept, far_one, far_two, x_first, y_second, y_sum = fence(
            kept, far_one, far_two, x_first, y_second, y_sum
        )
        act, d_gate, d_up, n2_all, y_one, y_two = kept
        n2_all, dy_rows = n2_all.reshape(sheet), dy_all.reshape(sheet)
        act, d_gate, d_up = [a.reshape(length, hidden) for a in (act, d_gate, d_up)]

        far_sum = chip_sum(far_one, far_two).astype(BF)
        x_far, y_far = swap(far_sum[:half], 2), swap(far_sum[half:], 4)
        gate_t = side_terms(n2_all, d_gate, count, parts)
        x_far, y_far, gate_t, y_one = fence(x_far, y_far, gate_t, y_one)

        x_second = swap((x_sum[half:] + y_far.astype(F32)).astype(BF), 2)
        y_first = swap((y_sum[:half] + x_far.astype(F32)).astype(BF), 4)
        (gate_moved,) = launch([term_of(gate_t, 0)])
        y_one = over_seq(y_one)
        up_t = side_terms(n2_all, d_up, count, parts)
        x_second, y_first, up_t, gate_moved, act = fence(x_second, y_first, up_t, gate_moved, act)
        own_sum = own_a.astype(F32) + own_c.astype(F32)
        first = own_sum[:half] + x_first.astype(F32) + y_first.astype(F32)
        second = own_sum[half:] + x_second.astype(F32) + y_second.astype(F32)
        dn2 = jnp.concatenate([first, second], axis=0)
    else:
        n2_blocks = gather_plain(n2)
        dn2_parts = []
        for c in range(0, count, 2):
            kept, part_a, part_b = chunk(kept, n2_blocks[c], n2_blocks[c + 1], c)
            dn2_parts += [part_a, part_b]
        act, d_gate, d_up, n2_all, y_one, y_two = kept
        n2_all, dy_rows = n2_all.reshape(sheet), dy_all.reshape(sheet)
        act, d_gate, d_up = [a.reshape(length, hidden) for a in (act, d_gate, d_up)]
        dn2 = scatter_plain(dn2_parts)
        gate_t = side_terms(n2_all, d_gate, count, parts)
        up_t = side_terms(n2_all, d_up, count, parts)
        (gate_moved,) = launch([term_of(gate_t, 0)])
        y_one = over_seq(y_one)

    m2 = h1 * r2
    e2 = dn2 * gain_two
    dh1 = dy.astype(F32) + r2 * (e2 - m2 * jnp.mean(e2 * m2, axis=-1, keepdims=True))
    db = dh1.astype(BF)
    do_t = jnp.einsum("ed,td->et", out_w, db, preferred_element_type=F32).astype(BF)
    (up_moved,) = launch([term_of(up_t, 0)])
    (gate_state,) = landed([gate_moved], [gate_t], 1)
    if parts > 2:
        (gate_moved,) = launch([gate_state])
    do_t, db, dh1, up_moved, gate_moved, gate_state = fence(
        do_t, db, dh1, up_moved, gate_moved, gate_state
    )
    do_heads = exchange(do_t.reshape(count, group_width, local))
    term_out = dot_f32(o_t, db).astype(BF)
    term_down = down_terms_of(act, dy_rows).reshape(parts, hidden // parts, width)
    (up_state,) = landed([up_moved], [up_t], 1)
    if parts > 2:
        (up_moved,) = launch([up_state])
    do_heads, term_out, term_down, y_one, up_moved, up_state = fence(
        do_heads, term_out, term_down, y_one, up_moved, up_state
    )

    part_out = over_seq(term_out)
    pair_t = [gate_t, up_t]
    pair = [gate_state, up_state]
    if parts > 2:
        pair = landed([gate_moved, up_moved], pair_t, 2)
    moved = launch((pair if parts > 3 else []) + [term_of(term_down, 0)])
    cut = blocks * 11 // 16
    saved = (bounds, q_t, k_n, k_t, v_n, cosine, sine, starts, o_heads, do_heads, lse, group)
    dq_one, dk, dv = attend_back(*saved, 0, cut, None)
    dq_one, dk, dv, moved, pair, do_heads, y_two, part_out = fence(
        dq_one, dk, dv, moved, pair, do_heads, y_two, part_out
    )
    y_two = over_seq(y_two)
    down_state = landed(moved[-1:], [term_down], 1)
    if parts > 3:
        pair = ring_finish(moved[:2], pair_t, 3)
    ffn_back = exchange(jnp.stack(pair, axis=1).astype(BF))
    moved = launch(down_state if parts > 2 else [])
    saved = (bounds, q_t, k_n, k_t, v_n, cosine, sine, starts, o_heads, do_heads, lse, group)
    dq_two, dkv_t = attend_back(*saved, cut, blocks - cut, (dk, dv))
    dq_two, dkv_t, moved, down_state, part_out, ffn_back = fence(
        dq_two, dkv_t, moved, down_state, part_out, ffn_back
    )

    d_t = jnp.concatenate([jnp.concatenate([dq_one, dq_two], axis=1), dkv_t], axis=0)
    def pair_of(c):
        return jnp.concatenate(
            [lax.dynamic_slice_in_dim(d_t, (me ^ n) * local, local, 1) for n in (c, c + 1)], axis=1
        )

    def dn1_chunk(c):
        part = jnp.einsum("et,ed->td", pair_of(c), attn_t, preferred_element_type=F32).astype(BF)
        return part[:local], part[local:]

    n1_rows = n1_all.reshape(sheet)
    if parts > 2:
        down_state = landed(moved, [term_down], 2)
    moved = launch(down_state if parts > 3 else [])
    grad_out = lax.psum_scatter(part_out, "fsdp", scatter_dimension=0, tiled=True).astype(F32)
    if cube:
        grad_tokens, attn_back = tail(d_t, wt_ext, own, dh1, n1_rows, attn_cols, count, parts)
    else:
        dn1 = scatter_plain([piece for c in range(0, count, 2) for piece in dn1_chunk(c)])
        attn_terms = [attn_terms_of(d_t, n1_rows, count, parts)]
        (part_attn,) = ring_finish(launch([term_of(attn_terms[0], 0)]), attn_terms, 1)
        attn_back = exchange(part_attn.astype(BF))
        m1 = x * r1
        e1 = dn1 * gain_one
        grad_tokens = dh1 + r1 * (e1 - m1 * jnp.mean(e1 * m1, axis=-1, keepdims=True))
    grad_tokens, attn_back, moved, ffn_back, y_one, y_two, grad_out = fence(
        grad_tokens, attn_back, moved, ffn_back, y_one, y_two, grad_out
    )
    if parts > 3:
        down_state = ring_finish(moved, [term_down], 3)
    grad_down = down_state[0].reshape(hidden // parts, width)
    output = (h1 + jnp.concatenate([y_one, y_two], axis=1).astype(F32)).astype(BF)

    ffn_back = ffn_back.astype(F32)
    grad_gate = ffn_back[:, 0].transpose(1, 0, 2).reshape(rows, count * hidden)
    grad_up = ffn_back[:, 1].transpose(1, 0, 2).reshape(rows, count * hidden)
    attn_back = attn_back.astype(F32)
    grad_query = attn_back[:, :, :group_width].transpose(1, 0, 2).reshape(rows, H * HD)
    pair = attn_back[:, :, group_width:].reshape(KV, share, rows, 2 * HD).sum(axis=1)
    grad_key = pair[:, :, :HD].transpose(1, 0, 2).reshape(rows, KV * HD)
    grad_value = pair[:, :, HD:].transpose(1, 0, 2).reshape(rows, KV * HD)

    def along(weight, grad):
        return jnp.sum(weight.astype(F32) * grad, axis=1)

    grad_gain_attn = (
        along(w_query, grad_query) + along(w_key, grad_key) + along(w_value, grad_value)
    ) / gain_attn.astype(F32)
    grad_gain_ffn = (along(w_gate, grad_gate) + along(w_up, grad_up)) / gain_ffn.astype(F32)
    return (
        output[None],
        grad_tokens[None],
        grad_gain_attn,
        grad_query,
        grad_key,
        grad_value,
        grad_out,
        grad_gain_ffn,
        grad_gate,
        grad_up,
        grad_down,
    )


def solution(mesh):
    sheet = P("fsdp", "seq", None)
    line = P(("seq", "fsdp"))
    matrix = P(("seq", "fsdp"), None)
    return jax.shard_map(
        body,
        mesh=mesh,
        in_specs=(
            sheet, P("fsdp", "seq"), line, matrix, matrix, matrix, matrix, line, matrix, matrix,
            matrix, sheet,
        ),
        out_specs=(
            sheet, sheet, line, matrix, matrix, matrix, matrix, line, matrix, matrix, matrix,
        ),
        check_vma=False,
    )
```

```python
import functools
import math

import jax
import jax.numpy as jnp
from jax import lax
from jax.experimental import pallas as pl
from jax.experimental.pallas import tpu as pltpu
from jax.sharding import PartitionSpec as P

H = 32
KV = 4
HD = 64
HALF = HD // 2
EPS = 1e-05
NEG = -1e30
BQ = 256
BK = 512
BF = jnp.bfloat16
F32 = jnp.float32
VMEM_LIMIT = 56 * 1024 * 1024
FFN_VMEM = 34 * 1024 * 1024
MESH = pl.DeviceIdType.MESH


def dot_f32(a, b):
    return jnp.dot(a, b, preferred_element_type=F32)


def heads_wide(block, group):
    return jnp.concatenate([block[h * HD : (h + 1) * HD] for h in range(group)], axis=1)


def heads_tall(block, group):
    width = block.shape[1] // group
    return jnp.concatenate([block[:, h * width : (h + 1) * width] for h in range(group)], axis=0)


def allowed_block(step, block_keys, first_row, block_rows, wide, starts):
    key = step * block_keys + lax.broadcasted_iota(jnp.int32, (block_keys, 1), 0)
    row = first_row + (lax.broadcasted_iota(jnp.int32, (1, wide), 1) & (block_rows - 1))
    return (key <= row) & (key >= starts)


def three_loops(bounds_ref, index, body):
    low, first, second, high = (bounds_ref[index, n] for n in range(4))
    lax.fori_loop(low, first, lambda j, c: body(j, True), None)
    lax.fori_loop(first, second, lambda j, c: body(j, False), None)
    lax.fori_loop(second, high, lambda j, c: body(j, True), None)


def turned(block, cosine, sine):
    first, second = block[:HALF], block[HALF:]
    return jnp.concatenate(
        [first * cosine - second * sine, second * cosine + first * sine], axis=0
    )


def turned_back(block, cosine, sine):
    first, second = block[:HALF], block[HALF:]
    return jnp.concatenate(
        [first * cosine + second * sine, second * cosine - first * sine], axis=0
    )


def forward_kernel(
    group, skip, final, bounds_ref, q_ref, kv_ref, cos_ref, sin_ref, start_ref, *rest
):
    if final:
        kn_ref, vt, o_ref, lse_ref, qt_ref, acc, top, total = rest
    else:
        o_ref, lse_ref, qt_ref, kt_ref, kn_ref, vn_ref, vt, acc, top, total = rest
    step = pl.program_id(0)
    i = step + skip
    rows = q_ref.shape[1]
    wide = rows * group
    here = pl.ds(pl.multiple_of(i * rows, rows), rows)
    cosine, sine = cos_ref[:, here], sin_ref[:, here]

    if not final:

        @pl.when(step == 0)
        def _():
            for part in range(kv_ref.shape[1] // BK):
                at = pl.ds(part * BK, BK)
                k = turned(kv_ref[:HD, at], cos_ref[:, at], sin_ref[:, at]).astype(BF)
                v = kv_ref[HD:, at].astype(BF)
                kt_ref[:, at] = k
                vt[:, at] = v
                kn_ref[at, :] = k.T
                vn_ref[at, :] = v.T

    heads = [
        turned(q_ref[h * HD : (h + 1) * HD, :], cosine, sine).astype(BF) * BF(HD**-0.5)
        for h in range(group)
    ]
    qt_ref[...] = jnp.concatenate(heads, axis=0)
    q4 = jnp.concatenate(heads, axis=1)
    starts = start_ref[0]
    acc[...] = jnp.zeros_like(acc)
    top[...] = jnp.full_like(top, NEG)
    total[...] = jnp.zeros_like(total)

    def block(j, masked):
        at = pl.multiple_of(j * BK, BK)
        s = dot_f32(kn_ref[pl.ds(at, BK), :], q4)
        if masked:
            s = jnp.where(allowed_block(j, BK, i * rows, rows, wide, starts), s, NEG)
        old = top[...]
        new = jnp.maximum(old, jnp.max(s, axis=0, keepdims=True))
        p = jnp.exp(s - new)
        keep = jnp.exp(old - new)
        top[...] = new
        total[...] = total[...] * keep + jnp.sum(p, axis=0, keepdims=True)
        acc[...] = acc[...] * keep + dot_f32(vt[:, pl.ds(at, BK)], p.astype(BF))

    three_loops(bounds_ref, i, block)
    o = acc[...] / total[...]
    o_ref[0] = heads_tall(o, group).astype(BF)
    lse_ref[0] = top[...] + jnp.log(total[...])


def backward_kernel(
    group, skip, final, bounds_ref, q_ref, k_ref, kt_ref, v_ref, cos_ref, sin_ref, start_ref,
    o_ref, do_ref, lse_ref, *rest
):
    if final:
        dk_before, dv_before, dq_ref, dkv_ref, dk, dv, acc = rest
    else:
        dq_ref, dk, dv, acc = rest
    step = pl.program_id(0)
    i = step + skip
    rows = q_ref.shape[1]
    wide = rows * group
    q4 = heads_wide(q_ref[...], group)
    g4 = heads_wide(do_ref[0], group)
    o4 = heads_wide(o_ref[0], group)
    delta = jnp.sum(g4.astype(F32) * o4.astype(F32), axis=0, keepdims=True)
    q4t = q4.T
    g4t = g4.T
    starts = start_ref[0]
    lse = lse_ref[0]
    acc[...] = jnp.zeros_like(acc)

    @pl.when(step == 0)
    def _():
        dk[...] = dk_before[...] if final else jnp.zeros_like(dk)
        dv[...] = dv_before[...] if final else jnp.zeros_like(dv)

    def block(j, masked):
        at = pl.multiple_of(j * BK, BK)
        s = dot_f32(k_ref[pl.ds(at, BK), :], q4)
        p = jnp.exp(s - lse)
        if masked:
            p = jnp.where(allowed_block(j, BK, i * rows, rows, wide, starts), p, 0.0)
        dp = dot_f32(v_ref[pl.ds(at, BK), :], g4)
        ds = (p * (dp - delta)).astype(BF)
        dv[pl.ds(at, BK), :] += dot_f32(p.astype(BF), g4t)
        dk[pl.ds(at, BK), :] += dot_f32(ds, q4t)
        acc[...] += dot_f32(kt_ref[:, pl.ds(at, BK)], ds)

    three_loops(bounds_ref, i, block)
    here = pl.ds(pl.multiple_of(i * rows, rows), rows)
    cosine, sine = cos_ref[:, here], sin_ref[:, here]
    for h in range(group):
        dq = acc[:, h * rows : (h + 1) * rows] * (HD**-0.5)
        dq_ref[h * HD : (h + 1) * HD, :] = turned_back(dq, cosine, sine).astype(BF)

    if final:

        @pl.when(step == pl.num_programs(0) - 1)
        def _():
            for part in range(dk.shape[0] // BK):
                at = pl.ds(part * BK, BK)
                dk_t = turned_back(dk[at, :].T, cos_ref[:, at], sin_ref[:, at])
                dkv_ref[:HD, at] = dk_t.astype(BF)
                dkv_ref[HD:, at] = dv[at, :].T.astype(BF)


def whole_spec(shape):
    return pl.BlockSpec(shape, lambda i, b: (0,) * len(shape))


def attend(
    bounds, projected, cosine, sine, starts, group, senders, local, skip, blocks, before
):
    length = projected.shape[1]
    per = local // BQ
    wide = group * HD
    final = before is not None
    line = pl.BlockSpec((1, 1, group * BQ), lambda i, b: (i + skip, 0, 0))
    piece = pl.BlockSpec((1, wide, BQ), lambda i, b: ((i + skip) // per, 0, (i + skip) % per))
    own_line = pl.BlockSpec((1, 1, group * BQ), lambda i, b: (i, 0, 0))
    tall, flat = whole_spec((length, HD)), whole_spec((HD, length))
    arrays = [projected, projected, cosine, sine, starts]
    in_specs = [
        pl.BlockSpec((wide, BQ), lambda i, b: (0, i + skip)),
        pl.BlockSpec((2 * HD, length), lambda i, b: (wide // (2 * HD), 0)),
        whole_spec((HALF, length)),
        whole_spec((HALF, length)),
        line,
    ]
    out_shape = [
        jax.ShapeDtypeStruct((senders, wide, local), BF),
        jax.ShapeDtypeStruct((blocks, 1, group * BQ), F32),
        jax.ShapeDtypeStruct((wide, blocks * BQ), BF),
    ]
    out_specs = [piece, own_line, pl.BlockSpec((wide, BQ), lambda i, b: (0, i))]
    scratch = [
        pltpu.VMEM((HD, group * BQ), F32),
        pltpu.VMEM((1, group * BQ), F32),
        pltpu.VMEM((1, group * BQ), F32),
    ]
    aliases = {}
    kernel = functools.partial(forward_kernel, group, skip, final)
    if final:
        o_before, kn, vt = before
        arrays += [kn, vt, o_before]
        in_specs += [tall, flat, pl.BlockSpec(memory_space=pl.ANY)]
        aliases = {8: 0}
        inner = kernel

        def kernel(*refs):
            return inner(*refs[:8], *refs[9:])

    else:
        out_shape += [
            jax.ShapeDtypeStruct((HD, length), BF),
            jax.ShapeDtypeStruct((length, HD), BF),
            jax.ShapeDtypeStruct((length, HD), BF),
            jax.ShapeDtypeStruct((HD, length), BF),
        ]
        out_specs += [flat, tall, tall, flat]
    return pl.pallas_call(
        kernel,
        out_shape=out_shape,
        grid_spec=pltpu.PrefetchScalarGridSpec(
            num_scalar_prefetch=1,
            grid=(blocks,),
            in_specs=in_specs,
            out_specs=out_specs,
            scratch_shapes=scratch,
        ),
        input_output_aliases=aliases,
        compiler_params=pltpu.CompilerParams(
            dimension_semantics=("arbitrary",), vmem_limit_bytes=VMEM_LIMIT
        ),
        cost_estimate=pl.CostEstimate(
            flops=20 * group * length * length * HD // 2,
            bytes_accessed=4 * group * length * HD,
            transcendentals=group * length * length // 8,
        ),
        name="attend",
    )(bounds, *arrays)


def attend_back(
    bounds, qt, k, kt, v, cosine, sine, starts, o, do, lse, group, skip, blocks, before
):
    length = k.shape[0]
    senders, _, local = o.shape
    per = local // BQ
    final = before is not None
    wide = group * HD
    piece = pl.BlockSpec((1, wide, BQ), lambda i, b: ((i + skip) // per, 0, (i + skip) % per))
    line = pl.BlockSpec((1, 1, group * BQ), lambda i, b: (i + skip, 0, 0))
    tall = whole_spec((length, HD))
    arrays = [qt, k, kt, v, cosine, sine, starts, o, do, lse]
    in_specs = [
        pl.BlockSpec((wide, BQ), lambda i, b: (0, i)),
        tall,
        whole_spec((HD, length)),
        tall,
        whole_spec((HALF, length)),
        whole_spec((HALF, length)),
        line,
        piece,
        piece,
        pl.BlockSpec((1, 1, group * BQ), lambda i, b: (i, 0, 0)),
    ]
    out_specs = [pl.BlockSpec((wide, BQ), lambda i, b: (0, i))]
    out_shape = [jax.ShapeDtypeStruct((wide, blocks * BQ), BF)]
    scratch = [pltpu.VMEM((HD, group * BQ), F32)]
    if final:
        arrays += list(before)
        in_specs += [tall, tall]
        out_specs += [whole_spec((2 * HD, length))]
        out_shape += [jax.ShapeDtypeStruct((2 * HD, length), BF)]
        scratch = [pltpu.VMEM((length, HD), F32), pltpu.VMEM((length, HD), F32)] + scratch
    else:
        out_specs += [tall, tall]
        out_shape += [jax.ShapeDtypeStruct((length, HD), F32)] * 2
    return pl.pallas_call(
        functools.partial(backward_kernel, group, skip, final),
        out_shape=out_shape,
        grid_spec=pltpu.PrefetchScalarGridSpec(
            num_scalar_prefetch=1,
            grid=(blocks,),
            in_specs=in_specs,
            out_specs=out_specs,
            scratch_shapes=scratch,
        ),
        compiler_params=pltpu.CompilerParams(
            dimension_semantics=("arbitrary",), vmem_limit_bytes=VMEM_LIMIT
        ),
        cost_estimate=pl.CostEstimate(
            flops=25 * group * length * length * HD // 2,
            bytes_accessed=8 * group * length * HD,
            transcendentals=group * length * length // 8,
        ),
        name="attend_back",
    )(bounds, *arrays)


def project_kernel(cols, x_ref, w_ref, n_ref, p_ref, wt_ref):
    @pl.when(pl.program_id(0) == 0)
    def _():
        wt_ref[...] = w_ref[...].T

    wide = x_ref[0].astype(F32)
    scale = lax.rsqrt(jnp.mean(wide * wide, axis=-1, keepdims=True) + EPS)
    gain = wt_ref[pl.ds(cols, 8), :].astype(F32)[0:1]
    normed = (wide * scale * gain).astype(BF)
    n_ref[0] = normed
    p_ref[...] = lax.dot_general(
        wt_ref[:cols, :], normed, (((1,), (1,)), ((), ())), preferred_element_type=F32
    )


def project(x_all, w_ext, cols):
    count, local, width = x_all.shape
    wide = w_ext.shape[1]
    block = pl.BlockSpec((1, local, width), lambda i: (i, 0, 0))
    return pl.pallas_call(
        functools.partial(project_kernel, cols),
        out_shape=(
            jax.ShapeDtypeStruct(x_all.shape, BF),
            jax.ShapeDtypeStruct((cols, count * local), F32),
            jax.ShapeDtypeStruct((wide, width), BF),
        ),
        grid=(count,),
        in_specs=[block, pl.BlockSpec((width, wide), lambda i: (0, 0))],
        out_specs=(
            block,
            pl.BlockSpec((cols, local), lambda i: (0, i)),
            pl.BlockSpec((wide, width), lambda i: (0, 0)),
        ),
        compiler_params=pltpu.CompilerParams(
            dimension_semantics=("arbitrary",), vmem_limit_bytes=VMEM_LIMIT
        ),
        cost_estimate=pl.CostEstimate(
            flops=2 * cols * width * count * local,
            bytes_accessed=4 * width * count * local,
            transcendentals=0,
        ),
        name="project",
    )(x_all, w_ext)


def ffn_kernel(
    places_ref, first_ref, second_ref, dy_ref, gate_ref, up_ref, down_ref, *rest
):
    act_ref, dg_ref, du_ref, n_ref, ya_ref, yb_ref, pa_ref, pb_ref = rest[-8:]
    which = pl.program_id(0)
    n = jnp.where(which == 0, first_ref[...], second_ref[...])
    n_ref[0] = n
    dy = dy_ref[0]
    across = (((1,), (1,)), ((), ()))
    gate = dot_f32(n, gate_ref[...])
    up = dot_f32(n, up_ref[...])
    d_act = lax.dot_general(dy, down_ref[...], across, preferred_element_type=F32)
    sig = jax.nn.sigmoid(gate)
    silu = gate * sig
    act = (silu * up).astype(BF)
    d_gate = (d_act * up * sig * (1.0 + gate * (1.0 - sig))).astype(BF)
    d_up = (d_act * silu).astype(BF)
    act_ref[0] = act
    dg_ref[0] = d_gate
    du_ref[0] = d_up
    split = ya_ref.shape[-1]
    ya_ref[0] = dot_f32(act, down_ref[:, :split]).astype(BF)
    yb_ref[0] = dot_f32(act, down_ref[:, split:]).astype(BF)
    part = lax.dot_general(d_gate, gate_ref[...], across, preferred_element_type=F32)
    part += lax.dot_general(d_up, up_ref[...], across, preferred_element_type=F32)
    part = part.astype(BF)

    @pl.when(which == 0)
    def _():
        pa_ref[...] = part

    @pl.when(which == 1)
    def _():
        pb_ref[...] = part


def ffn_chunk(places, first, second, dy_all, gate_w, up_w, down_w, kept):
    local, width = first.shape
    hidden = gate_w.shape[1]
    tall = min(256, local)
    tiles = local // tall
    count = dy_all.shape[0]

    def at_place(last):
        return pl.BlockSpec((1, tall, last), lambda i, t, p: (p[i], t, 0))

    ahead = pl.BlockSpec((tall, width), lambda i, t, p: (jnp.where(i == 0, t, tiles - 1), 0))
    behind = pl.BlockSpec((tall, width), lambda i, t, p: (jnp.where(i == 0, 0, t), 0))

    held = pl.BlockSpec(memory_space=pltpu.VMEM)
    in_specs = [ahead, behind, at_place(width), held, held, held]
    arrays = [first, second, dy_all, gate_w, up_w, down_w]
    aliases = {}
    if kept is not None:
        in_specs += [pl.BlockSpec(memory_space=pl.ANY)] * 6
        arrays += list(kept)
        aliases = {7 + n: n for n in range(6)}
    narrow = jax.ShapeDtypeStruct((count, local, hidden), BF)
    broad = jax.ShapeDtypeStruct((count, local, width), BF)
    part = jax.ShapeDtypeStruct((count, local, width // 2), BF)
    single = jax.ShapeDtypeStruct((local, width), BF)
    outs = pl.pallas_call(
        ffn_kernel,
        out_shape=(narrow, narrow, narrow, broad, part, part, single, single),
        grid_spec=pltpu.PrefetchScalarGridSpec(
            num_scalar_prefetch=1,
            grid=(2, tiles),
            in_specs=in_specs,
            out_specs=(
                at_place(hidden), at_place(hidden), at_place(hidden), at_place(width),
                at_place(width // 2), at_place(width // 2), ahead, behind,
            ),
        ),
        input_output_aliases=aliases,
        compiler_params=pltpu.CompilerParams(
            dimension_semantics=("arbitrary", "arbitrary"), vmem_limit_bytes=FFN_VMEM
        ),
        cost_estimate=pl.CostEstimate(
            flops=2 * 6 * 2 * local * width * hidden,
            bytes_accessed=2 * (5 * 2 * local * width + 3 * width * hidden),
            transcendentals=2 * local * hidden,
        ),
        name="ffn",
    )(places, *arrays)
    return outs[:6], outs[6], outs[7]


def spread(out_ref, value, per, parts, rows):
    for s in range(per):
        for f in range(parts):
            at = (s * parts + f) * rows
            out_ref[f, s] = value[at : at + rows].astype(BF)


def side_kernel(per, parts, rows, n_ref, d_ref, t_ref):
    spread(t_ref, dot_f32(n_ref[...].T, d_ref[...]), per, parts, rows)


def side_terms(n2, d, count, parts):
    length, width = n2.shape
    hidden = d.shape[1]
    rows = width // (count * parts)
    per = max(1, 512 // (parts * rows))
    wide = per * parts * rows
    return pl.pallas_call(
        functools.partial(side_kernel, per, parts, rows),
        out_shape=jax.ShapeDtypeStruct((parts, count, rows, hidden), BF),
        grid=(width // wide,),
        in_specs=[
            pl.BlockSpec((length, wide), lambda i: (0, i)),
            pl.BlockSpec((length, hidden), lambda i: (0, 0), pipeline_mode=pl.Buffered(1)),
        ],
        out_specs=pl.BlockSpec((parts, per, rows, hidden), lambda i: (0, i, 0, 0)),
        compiler_params=pltpu.CompilerParams(
            dimension_semantics=("arbitrary",), vmem_limit_bytes=VMEM_LIMIT
        ),
        cost_estimate=pl.CostEstimate(
            flops=2 * length * width * hidden,
            bytes_accessed=2 * length * (width + 2 * hidden),
            transcendentals=0,
        ),
        name="side_terms",
    )(n2, d)


def down_kernel(a_ref, dy_ref, t_ref, a_t):
    @pl.when(pl.program_id(0) == 0)
    def _():
        a_t[...] = a_ref[...].T

    t_ref[...] = dot_f32(a_t[...], dy_ref[...]).astype(BF)


def down_terms_of(act, dy):
    length, width = dy.shape
    hidden = act.shape[1]
    wide = min(512, width)
    return pl.pallas_call(
        down_kernel,
        out_shape=jax.ShapeDtypeStruct((hidden, width), BF),
        grid=(width // wide,),
        in_specs=[
            pl.BlockSpec((length, hidden), lambda i: (0, 0), pipeline_mode=pl.Buffered(1)),
            pl.BlockSpec((length, wide), lambda i: (0, i)),
        ],
        out_specs=pl.BlockSpec((hidden, wide), lambda i: (0, i)),
        scratch_shapes=[pltpu.VMEM((hidden, length), BF)],
        compiler_params=pltpu.CompilerParams(
            dimension_semantics=("arbitrary",), vmem_limit_bytes=VMEM_LIMIT
        ),
        cost_estimate=pl.CostEstimate(
            flops=2 * length * width * hidden,
            bytes_accessed=2 * length * (width + hidden),
            transcendentals=0,
        ),
        name="down_terms",
    )(act, dy)


def attn_kernel(per, parts, rows, d_ref, n_ref, t_ref):
    spread(t_ref, dot_f32(d_ref[...], n_ref[...]).T, per, parts, rows)


def attn_terms_of(d_t, n1, count, parts):
    cols, length = d_t.shape
    width = n1.shape[1]
    rows = width // (count * parts)
    per = max(1, 512 // (parts * rows))
    wide = per * parts * rows
    return pl.pallas_call(
        functools.partial(attn_kernel, per, parts, rows),
        out_shape=jax.ShapeDtypeStruct((parts, count, rows, cols), BF),
        grid=(width // wide,),
        in_specs=[
            pl.BlockSpec((cols, length), lambda i: (0, 0), pipeline_mode=pl.Buffered(1)),
            pl.BlockSpec((length, wide), lambda i: (0, i)),
        ],
        out_specs=pl.BlockSpec((parts, per, rows, cols), lambda i: (0, i, 0, 0)),
        compiler_params=pltpu.CompilerParams(
            dimension_semantics=("arbitrary",), vmem_limit_bytes=VMEM_LIMIT
        ),
        cost_estimate=pl.CostEstimate(
            flops=2 * length * width * cols,
            bytes_accessed=2 * length * (width + cols),
            transcendentals=0,
        ),
        name="attn_terms",
    )(d_t, n1)


def tail_kernel(
    parts, cols, d_ref, w_ref, x_ref, dh_ref, n_ref, grad_ref, back_ref,
    even, side_send, side_recv, landing, n_buf, terms, hop_send, hop_recv, last, mid,
    send, arrive, n_sem, own_sem,
):
    me = lax.axis_index("seq")
    z = lax.axis_index("fsdp")
    after_z, before_z = (z + 1) % parts, (z + parts - 1) % parts
    local, width = x_ref.shape
    half = local // 2
    low, high = pl.ds(0, half), pl.ds(half, half)
    barrier = pltpu.get_barrier_semaphore()
    for bit in (1, 2, 4):
        pl.semaphore_signal(barrier, inc=1, device_id=(me ^ bit, z), device_id_type=MESH)
    for other in (after_z, before_z):
        pl.semaphore_signal(barrier, inc=1, device_id=(me, other), device_id_type=MESH)
    pl.semaphore_wait(barrier, 5)
    made = {}

    def start(name, source, target, device):
        n = len(made)
        copy = pltpu.make_async_remote_copy(
            src_ref=source, dst_ref=target, send_sem=send.at[n], recv_sem=arrive.at[n],
            device_id=device, device_id_type=MESH,
        )
        made[name] = copy
        copy.start()

    def to_bit(name, bit, source, target):
        start(name, source, target, (me ^ bit, z))

    def arrived(*names):
        for name in names:
            made[name].wait_recv()

    chunk = n_buf.shape[2]
    chunks = width // chunk

    def fetch(i):
        return pltpu.make_async_copy(
            n_ref.at[:, pl.ds(i * chunk, chunk)], n_buf.at[i % 2], n_sem.at[i % 2]
        )

    fetch(0).start()
    tile = 512

    def product(c, out):
        at = pl.multiple_of((me ^ c) * local, local)
        d = d_ref[:, pl.ds(at, local)].T

        def one(t, carry):
            here = pl.ds(pl.multiple_of(t * tile, tile), tile)
            out[:, here] = dot_f32(d, w_ref[pl.ds(0, cols), here]).astype(BF)
            return carry

        lax.fori_loop(0, width // tile, one, 0)

    def chip(pair):
        product(2 * pair + 1, side_send.at[pair])
        to_bit("s" + str(pair), 1, side_send.at[pair], side_recv.at[pair])
        product(2 * pair, even.at[pair])

    def add_side(pair, part):
        even[pair, part] = (
            even[pair, part].astype(F32) + side_recv[pair, part].astype(F32)
        ).astype(BF)

    chip(3)
    chip(1)
    arrived("s3")
    add_side(3, low)
    to_bit("far_x", 2, even.at[3, low], landing.at[0])
    add_side(3, high)
    to_bit("far_y", 4, even.at[3, high], landing.at[1])
    chip(2)
    arrived("s1")
    add_side(1, low)
    to_bit("first_x", 2, even.at[1, low], landing.at[2])
    add_side(1, high)
    chip(0)
    arrived("s2")
    add_side(2, high)
    to_bit("second_y", 4, even.at[2, high], landing.at[3])
    add_side(2, low)

    count, rows = back_ref.shape[0], back_ref.shape[1]
    per = chunk // (parts * rows)
    for i in range(chunks):
        if i + 1 < chunks:
            fetch(i + 1).start()
        fetch(i).wait()
        value = dot_f32(d_ref[...], n_buf[i % 2]).T
        for s in range(per):
            for f in range(parts):
                at = (s * parts + f) * rows
                terms[f, i * per + s] = value[at : at + rows].astype(BF)
    start("r1", terms.at[before_z], hop_recv.at[0], (me, after_z))

    def add_far(pair, part, slot):
        even[pair, part] = (even[pair, part].astype(F32) + landing[slot].astype(F32)).astype(BF)

    arrived("far_x")
    add_far(2, low, 0)
    to_bit("first_y", 4, even.at[2, low], landing.at[4])
    arrived("far_y")
    add_far(1, high, 1)
    to_bit("second_x", 2, even.at[1, high], landing.at[5])
    arrived("s0")
    for step in range(1, parts):
        arrived("r" + str(step))
        state = hop_recv[step - 1].astype(F32)
        state = state + terms[(z + 2 * parts - 1 - step) % parts].astype(F32)
        if step < parts - 1:
            hop_send[step - 1] = state.astype(BF)
            start("r" + str(step + 1), hop_send.at[step - 1], hop_recv.at[step], (me, after_z))
        else:
            last[...] = state.astype(BF)

    mine = pltpu.make_async_copy(last.at[me], back_ref.at[me], own_sem.at[0])
    mine.start()
    to_bit("b3", 2, last.at[me ^ 6], mid.at[4])
    to_bit("a2", 1, last.at[me ^ 3], mid.at[1])
    to_bit("a4", 1, last.at[me ^ 7], mid.at[3])
    to_bit("a3", 1, last.at[me ^ 5], mid.at[2])
    to_bit("a1", 1, last.at[me ^ 1], back_ref.at[me])
    to_bit("b1", 2, last.at[me ^ 2], back_ref.at[me])
    to_bit("c1", 4, last.at[me ^ 4], back_ref.at[me])
    arrived("a4", "a2", "a3")
    to_bit("b4", 2, mid.at[3], mid.at[5])
    to_bit("b2", 2, mid.at[1], back_ref.at[me ^ 1])
    to_bit("c2", 4, mid.at[2], back_ref.at[me ^ 1])
    arrived("b3")
    to_bit("c3", 4, mid.at[4], back_ref.at[me ^ 2])
    arrived("b4")
    to_bit("c4", 4, mid.at[5], back_ref.at[me ^ 3])

    arrived("first_x", "second_y", "first_y", "second_x")
    gain = w_ref[pl.ds(cols, 8), :].astype(F32)[0:1]
    tall = 64

    def finish(first_slot, second_slot, offset):
        def one(t, carry):
            from_half = pl.ds(pl.multiple_of(t * tall, tall), tall)
            at = pl.ds(pl.multiple_of(t * tall + offset, tall), tall)
            dn = even[0, at].astype(F32) + side_recv[0, at].astype(F32)
            dn = dn + landing[first_slot, from_half].astype(F32)
            dn = dn + landing[second_slot, from_half].astype(F32)
            x = x_ref[at].astype(F32)
            r = lax.rsqrt(jnp.mean(x * x, axis=-1, keepdims=True) + EPS)
            m = x * r
            e = dn * gain
            inner = jnp.mean(e * m, axis=-1, keepdims=True)
            grad_ref[at] = dh_ref[at] + r * (e - m * inner)
            return carry

        lax.fori_loop(0, half // tall, one, 0)

    finish(2, 4, 0)
    finish(3, 5, half)
    arrived("a1", "b1", "c1", "b2", "c2", "c3", "c4")
    mine.wait()
    for copy in made.values():
        copy.wait_send()


def tail(d_t, wt_ext, x, dh1, n1, cols, count, parts):
    local, width = x.shape
    length = n1.shape[0]
    rows = width // (count * parts)
    half = local // 2
    chunk = 512
    anyspace = pl.BlockSpec(memory_space=pl.ANY)
    vmem = pl.BlockSpec(memory_space=pltpu.VMEM)
    copies = 4 + 6 + parts - 1 + 12
    block = (count, rows, cols)
    return pl.pallas_call(
        functools.partial(tail_kernel, parts, cols),
        out_shape=(
            jax.ShapeDtypeStruct((local, width), F32),
            jax.ShapeDtypeStruct(block, BF),
        ),
        in_specs=[vmem, vmem, vmem, vmem, anyspace],
        out_specs=(vmem, anyspace),
        scratch_shapes=[
            pltpu.VMEM((4, local, width), BF),
            pltpu.VMEM((4, local, width), BF),
            pltpu.VMEM((4, local, width), BF),
            pltpu.VMEM((6, half, width), BF),
            pltpu.VMEM((2, length, chunk), BF),
            pltpu.VMEM((parts,) + block, BF),
            pltpu.VMEM((max(1, parts - 2),) + block, BF),
            pltpu.VMEM((parts - 1,) + block, BF),
            pltpu.VMEM(block, BF),
            pltpu.VMEM((6, rows, cols), BF),
            pltpu.SemaphoreType.DMA((copies,)),
            pltpu.SemaphoreType.DMA((copies,)),
            pltpu.SemaphoreType.DMA((2,)),
            pltpu.SemaphoreType.DMA((1,)),
        ],
        compiler_params=pltpu.CompilerParams(
            collective_id=1, has_side_effects=True, vmem_limit_bytes=62 * 1024 * 1024
        ),
        cost_estimate=pl.CostEstimate(
            flops=1 << 30, bytes_accessed=1 << 20, transcendentals=0
        ),
        name="tail",
    )(d_t, wt_ext, x, dh1, n1)


def start_kernel(
    parts, x_ref, attn_ref, ffn_ref, out_ref, down_ref, x_all, attn_all, ffn_mine, out_all,
    down_all, attn_mid, ffn_mid, send, arrive, local_sem,
):
    me = lax.axis_index("seq")
    z = lax.axis_index("fsdp")
    after_z, before_z = (z + 1) % parts, (z + parts - 1) % parts
    half = x_ref.shape[0] // 2
    barrier = pltpu.get_barrier_semaphore()
    for bit in (1, 2, 4):
        pl.semaphore_signal(barrier, inc=1, device_id=(me ^ bit, z), device_id_type=MESH)
    for other in (after_z, before_z):
        pl.semaphore_signal(barrier, inc=1, device_id=(me, other), device_id_type=MESH)
    pl.semaphore_wait(barrier, 5)
    made = {}

    def start(name, source, target, device):
        n = len(made)
        copy = pltpu.make_async_remote_copy(
            src_ref=source, dst_ref=target, send_sem=send.at[n], recv_sem=arrive.at[n],
            device_id=device, device_id_type=MESH,
        )
        made[name] = copy
        copy.start()

    def to_bit(name, bit, source, target):
        start(name, source, target, (me ^ bit, z))

    def arrived(*names):
        for name in names:
            made[name].wait_recv()

    held = [
        pltpu.make_async_copy(x_ref, x_all.at[me], local_sem.at[0]),
        pltpu.make_async_copy(attn_ref.at[me], attn_all.at[z, me], local_sem.at[1]),
        pltpu.make_async_copy(ffn_ref.at[me], ffn_mine.at[me], local_sem.at[2]),
        pltpu.make_async_copy(out_ref, out_all.at[z], local_sem.at[3]),
        pltpu.make_async_copy(down_ref, down_all.at[z], local_sem.at[4]),
    ]
    for copy in held:
        copy.start()

    def swap_first(tag, source, final, mid):
        to_bit(tag + "a2", 1, source.at[me ^ 3], mid.at[1])
        to_bit(tag + "a4", 1, source.at[me ^ 7], mid.at[3])
        to_bit(tag + "a3", 1, source.at[me ^ 5], mid.at[2])
        to_bit(tag + "a1", 1, source.at[me ^ 1], final.at[me])

    def swap_second(tag, source, final, mid):
        to_bit(tag + "b3", 2, source.at[me ^ 6], mid.at[4])
        to_bit(tag + "b1", 2, source.at[me ^ 2], final.at[me])
        arrived(tag + "a4", tag + "a2")
        to_bit(tag + "b4", 2, mid.at[3], mid.at[5])
        to_bit(tag + "b2", 2, mid.at[1], final.at[me ^ 1])

    def swap_third(tag, source, final, mid):
        to_bit(tag + "c1", 4, source.at[me ^ 4], final.at[me])
        arrived(tag + "a3")
        to_bit(tag + "c2", 4, mid.at[2], final.at[me ^ 1])
        arrived(tag + "b3")
        to_bit(tag + "c3", 4, mid.at[4], final.at[me ^ 2])
        arrived(tag + "b4")
        to_bit(tag + "c4", 4, mid.at[5], final.at[me ^ 3])

    def swap_end(tag):
        arrived(*[tag + n for n in ("a1", "b1", "c1", "b2", "c2", "c3", "c4")])

    def around(tag, step, whole):
        if step > 1:
            arrived(tag + str(step - 1))
        at = (z + parts + 1 - step) % parts
        start(tag + str(step), whole.at[at], whole.at[at], (me, after_z))

    attn_sets = (attn_ref, attn_all.at[z], attn_mid)
    ffn_sets = (ffn_ref, ffn_mine, ffn_mid)
    start("o1", out_ref, out_all.at[z], (me, after_z))
    swap_first("attn", *attn_sets)
    swap_second("attn", *attn_sets)
    to_bit("x2", 2, x_ref, x_all.at[me])
    swap_third("attn", *attn_sets)
    to_bit("x4", 4, x_ref, x_all.at[me])
    to_bit("x1", 1, x_ref, x_all.at[me])
    swap_first("ffn", *ffn_sets)
    swap_end("attn")
    held[1].wait()
    around("z", 1, attn_all)
    held[4].wait()
    around("d", 1, down_all)
    for step in range(2, parts):
        around("o", step, out_all)
        around("z", step, attn_all)
    arrived("x2")
    to_bit("x3", 1, x_all.at[me ^ 2], x_all.at[me ^ 2])
    to_bit("f1", 4, x_all.at[me ^ 2, pl.ds(0, half)], x_all.at[me ^ 2, pl.ds(0, half)])
    arrived("x4")
    to_bit("x5", 1, x_all.at[me ^ 4], x_all.at[me ^ 4])
    to_bit("f2", 2, x_all.at[me ^ 4, pl.ds(half, half)], x_all.at[me ^ 4, pl.ds(half, half)])
    around("d", 2, down_all)
    swap_second("ffn", *ffn_sets)
    swap_third("ffn", *ffn_sets)
    for step in range(3, parts):
        around("d", step, down_all)
    arrived("f1", "f2")
    to_bit("x7", 1, x_all.at[me ^ 6], x_all.at[me ^ 6])
    swap_end("ffn")
    arrived("x1", "x3", "x5", "x7", "z" + str(parts - 1), "o" + str(parts - 1))
    arrived("d" + str(parts - 1))
    for copy in made.values():
        copy.wait_send()
    for copy in (held[0], held[2], held[3]):
        copy.wait()


def start_gather(x, attn_send, ffn_send, w_out, w_down, count, parts):
    anyspace = pl.BlockSpec(memory_space=pl.ANY)
    copies = 8 + 2 * 12 + 3 * (parts - 1)
    shapes = (
        jax.ShapeDtypeStruct((count,) + x.shape, BF),
        jax.ShapeDtypeStruct((parts,) + attn_send.shape, BF),
        jax.ShapeDtypeStruct(ffn_send.shape, BF),
        jax.ShapeDtypeStruct((parts,) + w_out.shape, BF),
        jax.ShapeDtypeStruct((parts,) + w_down.shape, BF),
        jax.ShapeDtypeStruct((6,) + attn_send.shape[1:], BF),
        jax.ShapeDtypeStruct((6,) + ffn_send.shape[1:], BF),
    )
    return pl.pallas_call(
        functools.partial(start_kernel, parts),
        out_shape=shapes,
        in_specs=[anyspace] * 5,
        out_specs=(anyspace,) * 7,
        scratch_shapes=[
            pltpu.SemaphoreType.DMA((copies,)),
            pltpu.SemaphoreType.DMA((copies,)),
            pltpu.SemaphoreType.DMA((5,)),
        ],
        compiler_params=pltpu.CompilerParams(
            collective_id=0, has_side_effects=True, vmem_limit_bytes=8 * 1024 * 1024
        ),
        name="start_gather",
    )(x, attn_send, ffn_send, w_out, w_down)[:5]


def ring(axis):
    count = lax.axis_size(axis)
    return [(n, (n + 1) % count) for n in range(count)]


def hop(*blocks):
    return [lax.ppermute(block, "fsdp", ring("fsdp")) for block in blocks]


def collect(pieces, axis):
    count = lax.axis_size(axis)
    me = lax.axis_index(axis)
    whole = jnp.zeros((count,) + pieces[0].shape, pieces[0].dtype)
    for back, piece in enumerate(pieces):
        whole = lax.dynamic_update_index_in_dim(whole, piece, (me + count - back) % count, 0)
    return whole


def term_of(terms, step):
    count = lax.axis_size("fsdp")
    me = lax.axis_index("fsdp")
    return lax.dynamic_index_in_dim(terms, (me + 2 * count - 1 - step) % count, 0, False)


def launch(states):
    return hop(*[state.astype(BF) for state in states])


def landed(moved, terms, step):
    return [m.astype(F32) + term_of(t, step).astype(F32) for m, t in zip(moved, terms)]


def ring_finish(moved, terms, step):
    states = landed(moved, terms, step)
    for n in range(step + 1, lax.axis_size("fsdp")):
        states = landed(launch(states), terms, n)
    return states


def fence(*values):
    return lax.optimization_barrier(values)


def swap(block, bit):
    count = lax.axis_size("seq")
    return lax.ppermute(block, "seq", [(n, n ^ bit) for n in range(count)])


def gather_plain(block):
    me = lax.axis_index("seq")
    whole = lax.all_gather(block, "seq", axis=0, tiled=False)
    return [lax.dynamic_index_in_dim(whole, me ^ c, 0, False) for c in range(whole.shape[0])]


def scatter_plain(parts):
    me = lax.axis_index("seq")
    whole = jnp.zeros((len(parts),) + parts[0].shape, BF)
    for c, part in enumerate(parts):
        whole = lax.dynamic_update_index_in_dim(whole, part.astype(BF), me ^ c, 0)
    return lax.psum_scatter(whole, "seq", scatter_dimension=0, tiled=False).astype(F32)


def far_halves(over_x, over_y):
    half = over_x.shape[0] // 2
    return swap(over_x[:half], 4), swap(over_y[half:], 2)


def chip_sum(own, other):
    return own.astype(F32) + swap(other, 1).astype(F32)


def exchange(array):
    return lax.all_to_all(array, "seq", split_axis=0, concat_axis=0, tiled=True)


def document_starts(flags_all):
    length = flags_all.shape[0]
    lanes = 128
    table = flags_all.reshape(length // lanes, lanes)
    place = jnp.arange(length, dtype=jnp.int32).reshape(table.shape)
    marked = jnp.where((table != 0) & (place > 0), place, 0)
    inside = jnp.arange(lanes)[None, :] <= jnp.arange(lanes)[:, None]
    local = jnp.max(jnp.where(inside[None], marked[:, None, :], 0), axis=-1)
    rows = jnp.max(marked, axis=1)
    count = length // lanes
    before = jnp.arange(count)[None, :] < jnp.arange(count)[:, None]
    carried = jnp.max(jnp.where(before, rows[None, :], 0), axis=-1)
    return jnp.maximum(local, carried[:, None]).reshape(length)


def body(
    tokens, doc_starts, gain_attn, w_query, w_key, w_value, w_out, gain_ffn, w_gate, w_up, w_down,
    cotangent,
):
    streams, local, width = tokens.shape
    assert streams == 1
    count = lax.axis_size("seq")
    parts = lax.axis_size("fsdp")
    me = lax.axis_index("seq")
    cube = count == 8
    length = local * count
    half = local // 2
    group = H // count
    share = (H // KV) // group
    rows = w_query.shape[0]
    hidden = w_gate.shape[1] // count
    group_width = group * HD
    attn_cols = group_width + 2 * HD
    flag_cols = local // rows
    extra_cols = 128
    sheet = (length, width)

    own = tokens[0]
    attn_send = jnp.concatenate(
        [
            w_query.reshape(rows, count, group_width),
            jnp.repeat(w_key.reshape(rows, KV, HD), share, axis=1),
            jnp.repeat(w_value.reshape(rows, KV, HD), share, axis=1),
        ],
        axis=2,
    ).transpose(1, 0, 2)
    extra = jnp.concatenate(
        [
            gain_attn[:, None],
            gain_ffn[:, None],
            doc_starts[0].astype(BF).reshape(rows, flag_cols),
            jnp.zeros((rows, extra_cols - 2 - flag_cols), BF),
        ],
        axis=1,
    )
    attn_send = jnp.concatenate(
        [attn_send, jnp.broadcast_to(extra[None], (count,) + extra.shape)], axis=2
    )
    ffn_send = jnp.concatenate(
        [w_gate.reshape(rows, count, hidden), w_up.reshape(rows, count, hidden)], axis=0
    ).transpose(1, 0, 2)
    z = lax.axis_index("fsdp")
    if cube:
        x_all, attn_all, ffn_part, out_part, down_w = start_gather(
            own, attn_send, ffn_send, w_out, w_down, count, parts
        )
    else:
        x_all = lax.all_gather(own, "seq", axis=0, tiled=False)
        attn_all = lax.all_gather(exchange(attn_send), "fsdp", axis=0, tiled=False)
        ffn_part = exchange(ffn_send)
        out_part = lax.all_gather(w_out, "fsdp", axis=0, tiled=False)
        down_w = lax.all_gather(w_down, "fsdp", axis=0, tiled=False)
    down_w = down_w.reshape(hidden, width)
    dy = cotangent[0]
    own, x_all, attn_all, ffn_part, out_part, dy = fence(
        own, x_all, attn_all, ffn_part, out_part, dy
    )
    ffn_pieces = [[ffn_part.reshape(count, 2, rows, hidden)]]

    out_w = lax.all_gather(out_part.reshape(parts * rows, width), "seq", axis=0, tiled=True)
    if len(ffn_pieces) < parts:
        ffn_pieces.append(hop(*ffn_pieces[-1]))
    flags = lax.dynamic_index_in_dim(attn_all, z, 0, False)
    flags = flags[:, :, attn_cols + 2 : attn_cols + 2 + flag_cols].reshape(length)
    last = document_starts(flags)
    position = (jnp.arange(length, dtype=jnp.int32) - last).astype(F32)
    frequency = jnp.exp(jnp.arange(HALF, dtype=F32) * (-2.0 * math.log(10000.0) / HD))
    angle = frequency[:, None] * position[None, :]
    cosine, sine = jnp.cos(angle), jnp.sin(angle)
    blocks = length // BQ
    by_block = last.reshape(blocks, BQ)
    starts = jnp.tile(by_block, (1, group)).reshape(blocks, 1, group * BQ)
    first_row = jnp.arange(blocks, dtype=jnp.int32) * BQ
    low = by_block[:, 0] // BK
    high = (first_row + BQ + BK - 1) // BK
    begin = jnp.minimum((by_block[:, -1] + BK - 1) // BK, high)
    end = jnp.maximum((first_row + 1) // BK, begin)
    bounds = jnp.stack([low, begin, end, high], axis=1)
    w_ext = attn_all.transpose(1, 0, 2, 3).reshape(width, attn_cols + extra_cols)
    n1_all, projected, wt_ext = project(x_all, w_ext, attn_cols)
    attn_t = wt_ext[:attn_cols]
    gain_one = wt_ext[attn_cols].astype(F32)
    gain_two = wt_ext[attn_cols + 1].astype(F32)
    projected, cosine, sine, starts, bounds, ffn_last, dy = fence(
        projected, cosine, sine, starts, bounds, ffn_pieces[-1], dy
    )
    ffn_pieces[-1] = ffn_last

    dy_all = lax.all_gather(dy, "seq", axis=0, tiled=False)
    cut = blocks * 11 // 16
    ready = (bounds, projected, cosine, sine, starts, group, count, local)
    if len(ffn_pieces) < parts:
        ffn_pieces.append(hop(*ffn_pieces[-1]))
    o_half, lse_one, qt_one, k_t, k_n, v_n, v_t = attend(*ready, 0, cut, None)
    o_half, lse_one, qt_one, k_t, k_n, v_n, v_t, ffn_last, out_w = fence(
        o_half, lse_one, qt_one, k_t, k_n, v_n, v_t, ffn_pieces[-1], out_w
    )
    ffn_pieces[-1] = ffn_last
    while len(ffn_pieces) < parts:
        ffn_pieces.append(hop(*ffn_pieces[-1]))
    o_heads, lse_two, qt_two = attend(*ready, cut, blocks - cut, (o_half, k_n, v_t))
    o_heads, lse_two, qt_two, ffn_pieces = fence(o_heads, lse_two, qt_two, ffn_pieces)

    o_t = exchange(o_heads).reshape(count * group_width, local)
    o_t, dy_all, qt_one, qt_two, lse_one, lse_two = fence(
        o_t, dy_all, qt_one, qt_two, lse_one, lse_two
    )

    ffn_w = collect([piece[0] for piece in ffn_pieces], "fsdp").transpose(2, 1, 0, 3, 4).reshape(2, width, hidden)
    gate_w, up_w = ffn_w[0], ffn_w[1]
    x = own.astype(F32)
    r1 = lax.rsqrt(jnp.mean(x * x, axis=-1, keepdims=True) + EPS)
    h1 = x + jnp.einsum("et,ed->td", o_t, out_w, preferred_element_type=F32)
    r2 = lax.rsqrt(jnp.mean(h1 * h1, axis=-1, keepdims=True) + EPS)
    n2 = (h1 * r2 * gain_two).astype(BF)
    n2, h1, r2 = fence(n2, h1, r2)

    def over_seq(part):
        whole = part.reshape(-1, part.shape[-1])
        return lax.psum_scatter(whole, "seq", scatter_dimension=0, tiled=True)

    kept = None

    def chunk(kept, first, second, c):
        places = jnp.stack([me ^ c, me ^ (c + 1)]).astype(jnp.int32)
        return ffn_chunk(places, first, second, dy_all, gate_w, up_w, down_w, kept)

    if cube:
        side, over_x, over_y = swap(n2, 1), swap(n2, 2), swap(n2, 4)
        side, gate_w, up_w = fence(side, gate_w, up_w)
        kept, own_a, own_b = chunk(kept, n2, side, 0)
        kept, own_a, own_b, over_x, over_y = fence(kept, own_a, own_b, over_x, over_y)

        far_a, far_b = far_halves(over_x, over_y)
        side_x, side_y, own_c = swap(over_x, 1), swap(over_y, 1), swap(own_b, 1)
        side_x, side_y, over_x, over_y, kept = fence(side_x, side_y, over_x, over_y, kept)
        kept, x_a, x_b = chunk(kept, over_x, side_x, 2)
        kept, x_a, x_b, far_a, far_b, own_c = fence(kept, x_a, x_b, far_a, far_b, own_c)

        far = jnp.concatenate([far_a, far_b], axis=0)
        side_far = swap(far, 1)
        x_sum = chip_sum(x_a, x_b)
        x_first = swap(x_sum[:half].astype(BF), 2)
        kept, y_a, y_b = chunk(kept, over_y, side_y, 4)
        kept, y_a, y_b, far, side_far, x_sum = fence(kept, y_a, y_b, far, side_far, x_sum)

        y_sum = chip_sum(y_a, y_b)
        y_second = swap(y_sum[half:].astype(BF), 4)
        kept, far_one, far_two = chunk(kept, far, side_far, 6)
        kept, far_one, far_two, x_first, y_second, y_sum = fence(
            kept, far_one, far_two, x_first, y_second, y_sum
        )
        act, d_gate, d_up, n2_all, y_one, y_two = kept
        n2_all, dy_rows = n2_all.reshape(sheet), dy_all.reshape(sheet)
        act, d_gate, d_up = [a.reshape(length, hidden) for a in (act, d_gate, d_up)]

        far_sum = chip_sum(far_one, far_two).astype(BF)
        x_far, y_far = swap(far_sum[:half], 2), swap(far_sum[half:], 4)
        gate_t = side_terms(n2_all, d_gate, count, parts)
        x_far, y_far, gate_t, y_one = fence(x_far, y_far, gate_t, y_one)

        x_second = swap((x_sum[half:] + y_far.astype(F32)).astype(BF), 2)
        y_first = swap((y_sum[:half] + x_far.astype(F32)).astype(BF), 4)
        (gate_moved,) = launch([term_of(gate_t, 0)])
        y_one = over_seq(y_one)
        up_t = side_terms(n2_all, d_up, count, parts)
        x_second, y_first, up_t, gate_moved, act = fence(x_second, y_first, up_t, gate_moved, act)
        own_sum = own_a.astype(F32) + own_c.astype(F32)
        first = own_sum[:half] + x_first.astype(F32) + y_first.astype(F32)
        second = own_sum[half:] + x_second.astype(F32) + y_second.astype(F32)
        dn2 = jnp.concatenate([first, second], axis=0)
    else:
        n2_blocks = gather_plain(n2)
        dn2_parts = []
        for c in range(0, count, 2):
            kept, part_a, part_b = chunk(kept, n2_blocks[c], n2_blocks[c + 1], c)
            dn2_parts += [part_a, part_b]
        act, d_gate, d_up, n2_all, y_one, y_two = kept
        n2_all, dy_rows = n2_all.reshape(sheet), dy_all.reshape(sheet)
        act, d_gate, d_up = [a.reshape(length, hidden) for a in (act, d_gate, d_up)]
        dn2 = scatter_plain(dn2_parts)
        gate_t = side_terms(n2_all, d_gate, count, parts)
        up_t = side_terms(n2_all, d_up, count, parts)
        (gate_moved,) = launch([term_of(gate_t, 0)])
        y_one = over_seq(y_one)

    m2 = h1 * r2
    e2 = dn2 * gain_two
    dh1 = dy.astype(F32) + r2 * (e2 - m2 * jnp.mean(e2 * m2, axis=-1, keepdims=True))
    db = dh1.astype(BF)
    do_t = jnp.einsum("ed,td->et", out_w, db, preferred_element_type=F32).astype(BF)
    (up_moved,) = launch([term_of(up_t, 0)])
    (gate_state,) = landed([gate_moved], [gate_t], 1)
    if parts > 2:
        (gate_moved,) = launch([gate_state])
    do_t, db, dh1, up_moved, gate_moved, gate_state, y_two = fence(
        do_t, db, dh1, up_moved, gate_moved, gate_state, y_two
    )
    y_two = over_seq(y_two)
    do_heads = exchange(do_t.reshape(count, group_width, local))
    term_out = dot_f32(o_t, db).astype(BF)
    term_down = down_terms_of(act, dy_rows).reshape(parts, hidden // parts, width)
    (up_state,) = landed([up_moved], [up_t], 1)
    if parts > 2:
        (up_moved,) = launch([up_state])
    do_heads, term_out, term_down, y_one, up_moved, up_state = fence(
        do_heads, term_out, term_down, y_one, up_moved, up_state
    )

    pair_t = [gate_t, up_t]
    pair = [gate_state, up_state]
    if parts > 2:
        pair = landed([gate_moved, up_moved], pair_t, 2)
    moved = launch((pair if parts > 3 else []) + [term_of(term_down, 0)])
    saved = (bounds, qt_one, k_n, k_t, v_n, cosine, sine, starts, o_heads, do_heads, lse_one, group)
    dq_one, dk, dv = attend_back(*saved, 0, cut, None)
    dq_one, dk, dv, moved, pair, do_heads, y_two, term_out = fence(
        dq_one, dk, dv, moved, pair, do_heads, y_two, term_out
    )
    part_out = over_seq(term_out)
    down_state = landed(moved[-1:], [term_down], 1)
    if parts > 3:
        pair = ring_finish(moved[:2], pair_t, 3)
    ffn_back = exchange(jnp.stack(pair, axis=1).astype(BF))
    moved = launch(down_state if parts > 2 else [])
    saved = (bounds, qt_two, k_n, k_t, v_n, cosine, sine, starts, o_heads, do_heads, lse_two, group)
    dq_two, dkv_t = attend_back(*saved, cut, blocks - cut, (dk, dv))
    dq_two, dkv_t, moved, down_state, part_out, ffn_back = fence(
        dq_two, dkv_t, moved, down_state, part_out, ffn_back
    )

    d_t = jnp.concatenate([jnp.concatenate([dq_one, dq_two], axis=1), dkv_t], axis=0)
    def pair_of(c):
        return jnp.concatenate(
            [lax.dynamic_slice_in_dim(d_t, (me ^ n) * local, local, 1) for n in (c, c + 1)], axis=1
        )

    def dn1_chunk(c):
        part = jnp.einsum("et,ed->td", pair_of(c), attn_t, preferred_element_type=F32).astype(BF)
        return part[:local], part[local:]

    n1_rows = n1_all.reshape(sheet)
    if parts > 2:
        down_state = landed(moved, [term_down], 2)
    moved = launch(down_state if parts > 3 else [])
    grad_out = lax.psum_scatter(part_out, "fsdp", scatter_dimension=0, tiled=True).astype(F32)
    if cube:
        grad_tokens, attn_back = tail(d_t, wt_ext, own, dh1, n1_rows, attn_cols, count, parts)
    else:
        dn1 = scatter_plain([piece for c in range(0, count, 2) for piece in dn1_chunk(c)])
        attn_terms = [attn_terms_of(d_t, n1_rows, count, parts)]
        (part_attn,) = ring_finish(launch([term_of(attn_terms[0], 0)]), attn_terms, 1)
        attn_back = exchange(part_attn.astype(BF))
        m1 = x * r1
        e1 = dn1 * gain_one
        grad_tokens = dh1 + r1 * (e1 - m1 * jnp.mean(e1 * m1, axis=-1, keepdims=True))
    grad_tokens, attn_back, moved, ffn_back, y_one, y_two, grad_out = fence(
        grad_tokens, attn_back, moved, ffn_back, y_one, y_two, grad_out
    )
    if parts > 3:
        down_state = ring_finish(moved, [term_down], 3)
    grad_down = down_state[0].reshape(hidden // parts, width)
    output = (h1 + jnp.concatenate([y_one, y_two], axis=1).astype(F32)).astype(BF)

    ffn_back = ffn_back.astype(F32)
    grad_gate = ffn_back[:, 0].transpose(1, 0, 2).reshape(rows, count * hidden)
    grad_up = ffn_back[:, 1].transpose(1, 0, 2).reshape(rows, count * hidden)
    attn_back = attn_back.astype(F32)
    grad_query = attn_back[:, :, :group_width].transpose(1, 0, 2).reshape(rows, H * HD)
    pair = attn_back[:, :, group_width:].reshape(KV, share, rows, 2 * HD).sum(axis=1)
    grad_key = pair[:, :, :HD].transpose(1, 0, 2).reshape(rows, KV * HD)
    grad_value = pair[:, :, HD:].transpose(1, 0, 2).reshape(rows, KV * HD)

    def along(weight, grad):
        return jnp.sum(weight.astype(F32) * grad, axis=1)

    grad_gain_attn = (
        along(w_query, grad_query) + along(w_key, grad_key) + along(w_value, grad_value)
    ) / gain_attn.astype(F32)
    grad_gain_ffn = (along(w_gate, grad_gate) + along(w_up, grad_up)) / gain_ffn.astype(F32)
    return (
        output[None],
        grad_tokens[None],
        grad_gain_attn,
        grad_query,
        grad_key,
        grad_value,
        grad_out,
        grad_gain_ffn,
        grad_gate,
        grad_up,
        grad_down,
    )


def solution(mesh):
    sheet = P("fsdp", "seq", None)
    line = P(("seq", "fsdp"))
    matrix = P(("seq", "fsdp"), None)
    return jax.shard_map(
        body,
        mesh=mesh,
        in_specs=(
            sheet, P("fsdp", "seq"), line, matrix, matrix, matrix, matrix, line, matrix, matrix,
            matrix, sheet,
        ),
        out_specs=(
            sheet, sheet, line, matrix, matrix, matrix, matrix, line, matrix, matrix, matrix,
        ),
        check_vma=False,
    )
```

```python
import functools
import math

import jax
import jax.numpy as jnp
from jax import lax
from jax.experimental import pallas as pl
from jax.experimental.pallas import tpu as pltpu
from jax.sharding import PartitionSpec as P

H = 32
KV = 4
HD = 64
HALF = HD // 2
EPS = 1e-05
NEG = -1e30
BQ = 256
BK = 512
BF = jnp.bfloat16
F32 = jnp.float32
VMEM_LIMIT = 56 * 1024 * 1024
FFN_VMEM = 40 * 1024 * 1024
MESH = pl.DeviceIdType.MESH


def dot_f32(a, b):
    return jnp.dot(a, b, preferred_element_type=F32)


def heads_wide(block, group):
    return jnp.concatenate([block[h * HD : (h + 1) * HD] for h in range(group)], axis=1)


def heads_tall(block, group):
    width = block.shape[1] // group
    return jnp.concatenate([block[:, h * width : (h + 1) * width] for h in range(group)], axis=0)


def allowed_block(step, block_keys, first_row, block_rows, wide, starts):
    key = step * block_keys + lax.broadcasted_iota(jnp.int32, (block_keys, 1), 0)
    row = first_row + (lax.broadcasted_iota(jnp.int32, (1, wide), 1) & (block_rows - 1))
    return (key <= row) & (key >= starts)


def three_loops(bounds_ref, index, body):
    low, first, second, high = (bounds_ref[index, n] for n in range(4))
    lax.fori_loop(low, first, lambda j, c: body(j, True), None)
    lax.fori_loop(first, second, lambda j, c: body(j, False), None)
    lax.fori_loop(second, high, lambda j, c: body(j, True), None)


def turned(block, cosine, sine):
    first, second = block[:HALF], block[HALF:]
    return jnp.concatenate(
        [first * cosine - second * sine, second * cosine + first * sine], axis=0
    )


def turned_back(block, cosine, sine):
    first, second = block[:HALF], block[HALF:]
    return jnp.concatenate(
        [first * cosine + second * sine, second * cosine - first * sine], axis=0
    )


def forward_kernel(
    group, skip, final, bounds_ref, q_ref, kv_ref, cos_ref, sin_ref, start_ref, *rest
):
    if final:
        kn_ref, vt, o_ref, lse_ref, qt_ref, acc, top, total = rest
    else:
        o_ref, lse_ref, qt_ref, kt_ref, kn_ref, vn_ref, vt, acc, top, total = rest
    step = pl.program_id(0)
    i = step + skip
    rows = q_ref.shape[1]
    wide = rows * group
    here = pl.ds(pl.multiple_of(i * rows, rows), rows)
    cosine, sine = cos_ref[:, here], sin_ref[:, here]

    if not final:

        @pl.when(step == 0)
        def _():
            for part in range(kv_ref.shape[1] // BK):
                at = pl.ds(part * BK, BK)
                k = turned(kv_ref[:HD, at], cos_ref[:, at], sin_ref[:, at]).astype(BF)
                v = kv_ref[HD:, at].astype(BF)
                kt_ref[:, at] = k
                vt[:, at] = v
                kn_ref[at, :] = k.T
                vn_ref[at, :] = v.T

    heads = [
        turned(q_ref[h * HD : (h + 1) * HD, :], cosine, sine).astype(BF) * BF(HD**-0.5)
        for h in range(group)
    ]
    qt_ref[...] = jnp.concatenate(heads, axis=0)
    q4 = jnp.concatenate(heads, axis=1)
    starts = start_ref[0]
    acc[...] = jnp.zeros_like(acc)
    top[...] = jnp.full_like(top, NEG)
    total[...] = jnp.zeros_like(total)

    def block(j, masked):
        at = pl.multiple_of(j * BK, BK)
        s = dot_f32(kn_ref[pl.ds(at, BK), :], q4)
        if masked:
            s = jnp.where(allowed_block(j, BK, i * rows, rows, wide, starts), s, NEG)
        old = top[...]
        new = jnp.maximum(old, jnp.max(s, axis=0, keepdims=True))
        p = jnp.exp(s - new)
        keep = jnp.exp(old - new)
        top[...] = new
        total[...] = total[...] * keep + jnp.sum(p, axis=0, keepdims=True)
        acc[...] = acc[...] * keep + dot_f32(vt[:, pl.ds(at, BK)], p.astype(BF))

    three_loops(bounds_ref, i, block)
    o = acc[...] / total[...]
    o_ref[0] = heads_tall(o, group).astype(BF)
    lse_ref[0] = top[...] + jnp.log(total[...])


def backward_kernel(
    group, skip, final, bounds_ref, q_ref, k_ref, kt_ref, v_ref, cos_ref, sin_ref, start_ref,
    o_ref, do_ref, lse_ref, *rest
):
    if final:
        dk_before, dv_before, dq_ref, dkv_ref, dk, dv, acc = rest
    else:
        dq_ref, dk, dv, acc = rest
    step = pl.program_id(0)
    i = step + skip
    rows = q_ref.shape[1]
    wide = rows * group
    q4 = heads_wide(q_ref[...], group)
    g4 = heads_wide(do_ref[0], group)
    o4 = heads_wide(o_ref[0], group)
    delta = jnp.sum(g4.astype(F32) * o4.astype(F32), axis=0, keepdims=True)
    q4t = q4.T
    g4t = g4.T
    starts = start_ref[0]
    lse = lse_ref[0]
    acc[...] = jnp.zeros_like(acc)

    @pl.when(step == 0)
    def _():
        dk[...] = dk_before[...] if final else jnp.zeros_like(dk)
        dv[...] = dv_before[...] if final else jnp.zeros_like(dv)

    def block(j, masked):
        at = pl.multiple_of(j * BK, BK)
        s = dot_f32(k_ref[pl.ds(at, BK), :], q4)
        p = jnp.exp(s - lse)
        if masked:
            p = jnp.where(allowed_block(j, BK, i * rows, rows, wide, starts), p, 0.0)
        dp = dot_f32(v_ref[pl.ds(at, BK), :], g4)
        ds = (p * (dp - delta)).astype(BF)
        dv[pl.ds(at, BK), :] += dot_f32(p.astype(BF), g4t)
        dk[pl.ds(at, BK), :] += dot_f32(ds, q4t)
        acc[...] += dot_f32(kt_ref[:, pl.ds(at, BK)], ds)

    three_loops(bounds_ref, i, block)
    here = pl.ds(pl.multiple_of(i * rows, rows), rows)
    cosine, sine = cos_ref[:, here], sin_ref[:, here]
    for h in range(group):
        dq = acc[:, h * rows : (h + 1) * rows] * (HD**-0.5)
        dq_ref[h * HD : (h + 1) * HD, :] = turned_back(dq, cosine, sine).astype(BF)

    if final:

        @pl.when(step == pl.num_programs(0) - 1)
        def _():
            for part in range(dk.shape[0] // BK):
                at = pl.ds(part * BK, BK)
                dk_t = turned_back(dk[at, :].T, cos_ref[:, at], sin_ref[:, at])
                dkv_ref[:HD, at] = dk_t.astype(BF)
                dkv_ref[HD:, at] = dv[at, :].T.astype(BF)


def whole_spec(shape):
    return pl.BlockSpec(shape, lambda i, b: (0,) * len(shape))


def attend(
    bounds, projected, cosine, sine, starts, group, senders, local, skip, blocks, before
):
    length = projected.shape[1]
    per = local // BQ
    wide = group * HD
    final = before is not None
    line = pl.BlockSpec((1, 1, group * BQ), lambda i, b: (i + skip, 0, 0))
    piece = pl.BlockSpec((1, wide, BQ), lambda i, b: ((i + skip) // per, 0, (i + skip) % per))
    own_line = pl.BlockSpec((1, 1, group * BQ), lambda i, b: (i, 0, 0))
    tall, flat = whole_spec((length, HD)), whole_spec((HD, length))
    arrays = [projected, projected, cosine, sine, starts]
    in_specs = [
        pl.BlockSpec((wide, BQ), lambda i, b: (0, i + skip)),
        pl.BlockSpec((2 * HD, length), lambda i, b: (wide // (2 * HD), 0)),
        whole_spec((HALF, length)),
        whole_spec((HALF, length)),
        line,
    ]
    out_shape = [
        jax.ShapeDtypeStruct((senders, wide, local), BF),
        jax.ShapeDtypeStruct((blocks, 1, group * BQ), F32),
        jax.ShapeDtypeStruct((wide, blocks * BQ), BF),
    ]
    out_specs = [piece, own_line, pl.BlockSpec((wide, BQ), lambda i, b: (0, i))]
    scratch = [
        pltpu.VMEM((HD, group * BQ), F32),
        pltpu.VMEM((1, group * BQ), F32),
        pltpu.VMEM((1, group * BQ), F32),
    ]
    aliases = {}
    kernel = functools.partial(forward_kernel, group, skip, final)
    if final:
        o_before, kn, vt = before
        arrays += [kn, vt, o_before]
        in_specs += [tall, flat, pl.BlockSpec(memory_space=pl.ANY)]
        aliases = {8: 0}
        inner = kernel

        def kernel(*refs):
            return inner(*refs[:8], *refs[9:])

    else:
        out_shape += [
            jax.ShapeDtypeStruct((HD, length), BF),
            jax.ShapeDtypeStruct((length, HD), BF),
            jax.ShapeDtypeStruct((length, HD), BF),
            jax.ShapeDtypeStruct((HD, length), BF),
        ]
        out_specs += [flat, tall, tall, flat]
    return pl.pallas_call(
        kernel,
        out_shape=out_shape,
        grid_spec=pltpu.PrefetchScalarGridSpec(
            num_scalar_prefetch=1,
            grid=(blocks,),
            in_specs=in_specs,
            out_specs=out_specs,
            scratch_shapes=scratch,
        ),
        input_output_aliases=aliases,
        compiler_params=pltpu.CompilerParams(
            dimension_semantics=("arbitrary",), vmem_limit_bytes=VMEM_LIMIT
        ),
        cost_estimate=pl.CostEstimate(
            flops=20 * group * length * length * HD // 2,
            bytes_accessed=4 * group * length * HD,
            transcendentals=group * length * length // 8,
        ),
        name="attend",
    )(bounds, *arrays)


def attend_back(
    bounds, qt, k, kt, v, cosine, sine, starts, o, do, lse, group, skip, blocks, before
):
    length = k.shape[0]
    senders, _, local = o.shape
    per = local // BQ
    final = before is not None
    wide = group * HD
    piece = pl.BlockSpec((1, wide, BQ), lambda i, b: ((i + skip) // per, 0, (i + skip) % per))
    line = pl.BlockSpec((1, 1, group * BQ), lambda i, b: (i + skip, 0, 0))
    tall = whole_spec((length, HD))
    arrays = [qt, k, kt, v, cosine, sine, starts, o, do, lse]
    in_specs = [
        pl.BlockSpec((wide, BQ), lambda i, b: (0, i)),
        tall,
        whole_spec((HD, length)),
        tall,
        whole_spec((HALF, length)),
        whole_spec((HALF, length)),
        line,
        piece,
        piece,
        pl.BlockSpec((1, 1, group * BQ), lambda i, b: (i, 0, 0)),
    ]
    out_specs = [pl.BlockSpec((wide, BQ), lambda i, b: (0, i))]
    out_shape = [jax.ShapeDtypeStruct((wide, blocks * BQ), BF)]
    scratch = [pltpu.VMEM((HD, group * BQ), F32)]
    if final:
        arrays += list(before)
        in_specs += [tall, tall]
        out_specs += [whole_spec((2 * HD, length))]
        out_shape += [jax.ShapeDtypeStruct((2 * HD, length), BF)]
        scratch = [pltpu.VMEM((length, HD), F32), pltpu.VMEM((length, HD), F32)] + scratch
    else:
        out_specs += [tall, tall]
        out_shape += [jax.ShapeDtypeStruct((length, HD), F32)] * 2
    return pl.pallas_call(
        functools.partial(backward_kernel, group, skip, final),
        out_shape=out_shape,
        grid_spec=pltpu.PrefetchScalarGridSpec(
            num_scalar_prefetch=1,
            grid=(blocks,),
            in_specs=in_specs,
            out_specs=out_specs,
            scratch_shapes=scratch,
        ),
        compiler_params=pltpu.CompilerParams(
            dimension_semantics=("arbitrary",), vmem_limit_bytes=VMEM_LIMIT
        ),
        cost_estimate=pl.CostEstimate(
            flops=25 * group * length * length * HD // 2,
            bytes_accessed=8 * group * length * HD,
            transcendentals=group * length * length // 8,
        ),
        name="attend_back",
    )(bounds, *arrays)


def project_kernel(cols, x_ref, w_ref, n_ref, p_ref, wt_ref):
    @pl.when(pl.program_id(0) == 0)
    def _():
        wt_ref[...] = w_ref[...].T

    wide = x_ref[0].astype(F32)
    scale = lax.rsqrt(jnp.mean(wide * wide, axis=-1, keepdims=True) + EPS)
    gain = wt_ref[pl.ds(cols, 8), :].astype(F32)[0:1]
    normed = (wide * scale * gain).astype(BF)
    n_ref[0] = normed
    p_ref[...] = lax.dot_general(
        wt_ref[:cols, :], normed, (((1,), (1,)), ((), ())), preferred_element_type=F32
    )


def project(x_all, w_ext, cols):
    count, local, width = x_all.shape
    wide = w_ext.shape[1]
    block = pl.BlockSpec((1, local, width), lambda i: (i, 0, 0))
    return pl.pallas_call(
        functools.partial(project_kernel, cols),
        out_shape=(
            jax.ShapeDtypeStruct(x_all.shape, BF),
            jax.ShapeDtypeStruct((cols, count * local), F32),
            jax.ShapeDtypeStruct((wide, width), BF),
        ),
        grid=(count,),
        in_specs=[block, pl.BlockSpec((width, wide), lambda i: (0, 0))],
        out_specs=(
            block,
            pl.BlockSpec((cols, local), lambda i: (0, i)),
            pl.BlockSpec((wide, width), lambda i: (0, 0)),
        ),
        compiler_params=pltpu.CompilerParams(
            dimension_semantics=("arbitrary",), vmem_limit_bytes=VMEM_LIMIT
        ),
        cost_estimate=pl.CostEstimate(
            flops=2 * cols * width * count * local,
            bytes_accessed=4 * width * count * local,
            transcendentals=0,
        ),
        name="project",
    )(x_all, w_ext)


def ffn_kernel(tiles, places_ref, *refs):
    n_refs, (dy_ref, gate_ref, up_ref, down_ref) = refs[:tiles], refs[tiles : tiles + 4]
    outs = refs[-(6 + tiles) :]
    act_ref, dg_ref, du_ref, n_ref, ya_ref, yb_ref = outs[:6]
    which = pl.program_id(0)
    n = n_refs[0][...]
    for t in range(1, tiles):
        n = jnp.where(which == t, n_refs[t][...], n)
    n_ref[0] = n
    dy = dy_ref[0]
    across = (((1,), (1,)), ((), ()))
    gate = dot_f32(n, gate_ref[...])
    up = dot_f32(n, up_ref[...])
    d_act = lax.dot_general(dy, down_ref[...], across, preferred_element_type=F32)
    sig = jax.nn.sigmoid(gate)
    silu = gate * sig
    act = (silu * up).astype(BF)
    d_gate = (d_act * up * sig * (1.0 + gate * (1.0 - sig))).astype(BF)
    d_up = (d_act * silu).astype(BF)
    act_ref[0] = act
    dg_ref[0] = d_gate
    du_ref[0] = d_up
    split = ya_ref.shape[-1]
    ya_ref[0] = dot_f32(act, down_ref[:, :split]).astype(BF)
    yb_ref[0] = dot_f32(act, down_ref[:, split:]).astype(BF)
    part = lax.dot_general(d_gate, gate_ref[...], across, preferred_element_type=F32)
    part += lax.dot_general(d_up, up_ref[...], across, preferred_element_type=F32)
    part = part.astype(BF)
    for t in range(tiles):

        @pl.when(which == t)
        def _(t=t):
            outs[6 + t][...] = part


def ffn_chunk(tiles, dy_all, gate_w, up_w, down_w, kept):
    count, local, width = dy_all.shape
    hidden = gate_w.shape[1]
    tall = min(256, local)
    number = len(tiles)
    places = jnp.stack(
        [jnp.asarray(t[2], jnp.int32) for t in tiles] + [jnp.int32(t[3]) for t in tiles]
    )

    def at_place(last):
        return pl.BlockSpec((1, tall, last), lambda i, p: (p[i], p[number + i], 0))

    def fixed(n):
        return pl.BlockSpec((tall, width), lambda i, p: (n, 0))

    held = pl.BlockSpec(memory_space=pltpu.VMEM)
    in_specs = [fixed(t[1]) for t in tiles] + [at_place(width), held, held, held]
    arrays = [t[0] for t in tiles] + [dy_all, gate_w, up_w, down_w]
    aliases = {}
    if kept is not None:
        aliases = {1 + len(arrays) + n: n for n in range(6)}
        in_specs += [pl.BlockSpec(memory_space=pl.ANY)] * 6
        arrays += list(kept)
    narrow = jax.ShapeDtypeStruct((count, local, hidden), BF)
    broad = jax.ShapeDtypeStruct((count, local, width), BF)
    part = jax.ShapeDtypeStruct((count, local, width // 2), BF)
    single = jax.ShapeDtypeStruct((tall, width), BF)
    outs = pl.pallas_call(
        functools.partial(ffn_kernel, number),
        out_shape=(narrow, narrow, narrow, broad, part, part) + (single,) * number,
        grid_spec=pltpu.PrefetchScalarGridSpec(
            num_scalar_prefetch=1,
            grid=(number,),
            in_specs=in_specs,
            out_specs=(
                at_place(hidden), at_place(hidden), at_place(hidden), at_place(width),
                at_place(width // 2), at_place(width // 2),
            )
            + (fixed(0),) * number,
        ),
        input_output_aliases=aliases,
        compiler_params=pltpu.CompilerParams(
            dimension_semantics=("arbitrary",), vmem_limit_bytes=FFN_VMEM
        ),
        cost_estimate=pl.CostEstimate(
            flops=12 * number * tall * width * hidden,
            bytes_accessed=2 * (5 * number * tall * width + 3 * width * hidden),
            transcendentals=number * tall * hidden,
        ),
        name="ffn",
    )(places, *arrays)
    return outs[:6], list(outs[6:])


def spread(out_ref, value, per, parts, rows):
    for s in range(per):
        for f in range(parts):
            at = (s * parts + f) * rows
            out_ref[f, s] = value[at : at + rows].astype(BF)


def side_kernel(per, parts, rows, n_ref, d_ref, t_ref):
    spread(t_ref, dot_f32(n_ref[...].T, d_ref[...]), per, parts, rows)


def side_terms(n2, d, count, parts):
    length, width = n2.shape
    hidden = d.shape[1]
    rows = width // (count * parts)
    per = max(1, 512 // (parts * rows))
    wide = per * parts * rows
    return pl.pallas_call(
        functools.partial(side_kernel, per, parts, rows),
        out_shape=jax.ShapeDtypeStruct((parts, count, rows, hidden), BF),
        grid=(width // wide,),
        in_specs=[
            pl.BlockSpec((length, wide), lambda i: (0, i)),
            pl.BlockSpec((length, hidden), lambda i: (0, 0), pipeline_mode=pl.Buffered(1)),
        ],
        out_specs=pl.BlockSpec((parts, per, rows, hidden), lambda i: (0, i, 0, 0)),
        compiler_params=pltpu.CompilerParams(
            dimension_semantics=("arbitrary",), vmem_limit_bytes=VMEM_LIMIT
        ),
        cost_estimate=pl.CostEstimate(
            flops=2 * length * width * hidden,
            bytes_accessed=2 * length * (width + 2 * hidden),
            transcendentals=0,
        ),
        name="side_terms",
    )(n2, d)


def down_kernel(a_ref, dy_ref, t_ref, a_t):
    @pl.when(pl.program_id(0) == 0)
    def _():
        a_t[...] = a_ref[...].T

    t_ref[...] = dot_f32(a_t[...], dy_ref[...]).astype(BF)


def down_terms_of(act, dy):
    length, width = dy.shape
    hidden = act.shape[1]
    wide = min(512, width)
    return pl.pallas_call(
        down_kernel,
        out_shape=jax.ShapeDtypeStruct((hidden, width), BF),
        grid=(width // wide,),
        in_specs=[
            pl.BlockSpec((length, hidden), lambda i: (0, 0), pipeline_mode=pl.Buffered(1)),
            pl.BlockSpec((length, wide), lambda i: (0, i)),
        ],
        out_specs=pl.BlockSpec((hidden, wide), lambda i: (0, i)),
        scratch_shapes=[pltpu.VMEM((hidden, length), BF)],
        compiler_params=pltpu.CompilerParams(
            dimension_semantics=("arbitrary",), vmem_limit_bytes=VMEM_LIMIT
        ),
        cost_estimate=pl.CostEstimate(
            flops=2 * length * width * hidden,
            bytes_accessed=2 * length * (width + hidden),
            transcendentals=0,
        ),
        name="down_terms",
    )(act, dy)


def attn_kernel(per, parts, rows, d_ref, n_ref, t_ref):
    spread(t_ref, dot_f32(d_ref[...], n_ref[...]).T, per, parts, rows)


def attn_terms_of(d_t, n1, count, parts):
    cols, length = d_t.shape
    width = n1.shape[1]
    rows = width // (count * parts)
    per = max(1, 512 // (parts * rows))
    wide = per * parts * rows
    return pl.pallas_call(
        functools.partial(attn_kernel, per, parts, rows),
        out_shape=jax.ShapeDtypeStruct((parts, count, rows, cols), BF),
        grid=(width // wide,),
        in_specs=[
            pl.BlockSpec((cols, length), lambda i: (0, 0), pipeline_mode=pl.Buffered(1)),
            pl.BlockSpec((length, wide), lambda i: (0, i)),
        ],
        out_specs=pl.BlockSpec((parts, per, rows, cols), lambda i: (0, i, 0, 0)),
        compiler_params=pltpu.CompilerParams(
            dimension_semantics=("arbitrary",), vmem_limit_bytes=VMEM_LIMIT
        ),
        cost_estimate=pl.CostEstimate(
            flops=2 * length * width * cols,
            bytes_accessed=2 * length * (width + cols),
            transcendentals=0,
        ),
        name="attn_terms",
    )(d_t, n1)


def tail_kernel(
    parts, cols, d_ref, w_ref, x_ref, dh_ref, n_ref, grad_ref, back_ref,
    even, side_send, side_recv, landing, n_buf, terms, hop_send, hop_recv, last, mid,
    send, arrive, n_sem, own_sem,
):
    me = lax.axis_index("seq")
    z = lax.axis_index("fsdp")
    after_z, before_z = (z + 1) % parts, (z + parts - 1) % parts
    local, width = x_ref.shape
    half = local // 2
    low, high = pl.ds(0, half), pl.ds(half, half)
    barrier = pltpu.get_barrier_semaphore()
    for bit in (1, 2, 4):
        pl.semaphore_signal(barrier, inc=1, device_id=(me ^ bit, z), device_id_type=MESH)
    for other in (after_z, before_z):
        pl.semaphore_signal(barrier, inc=1, device_id=(me, other), device_id_type=MESH)
    pl.semaphore_wait(barrier, 5)
    made = {}

    def start(name, source, target, device):
        n = len(made)
        copy = pltpu.make_async_remote_copy(
            src_ref=source, dst_ref=target, send_sem=send.at[n], recv_sem=arrive.at[n],
            device_id=device, device_id_type=MESH,
        )
        made[name] = copy
        copy.start()

    def to_bit(name, bit, source, target):
        start(name, source, target, (me ^ bit, z))

    def arrived(*names):
        for name in names:
            made[name].wait_recv()

    chunk = n_buf.shape[2]
    chunks = width // chunk

    def fetch(i):
        return pltpu.make_async_copy(
            n_ref.at[:, pl.ds(i * chunk, chunk)], n_buf.at[i % 2], n_sem.at[i % 2]
        )

    fetch(0).start()
    tile = 512

    def product(c, out):
        at = pl.multiple_of((me ^ c) * local, local)
        d = d_ref[:, pl.ds(at, local)].T

        def one(t, carry):
            here = pl.ds(pl.multiple_of(t * tile, tile), tile)
            out[:, here] = dot_f32(d, w_ref[pl.ds(0, cols), here]).astype(BF)
            return carry

        lax.fori_loop(0, width // tile, one, 0)

    def chip(pair):
        product(2 * pair + 1, side_send.at[pair])
        to_bit("s" + str(pair), 1, side_send.at[pair], side_recv.at[pair])
        product(2 * pair, even.at[pair])

    def add_side(pair, part):
        even[pair, part] = (
            even[pair, part].astype(F32) + side_recv[pair, part].astype(F32)
        ).astype(BF)

    chip(3)
    chip(1)
    arrived("s3")
    add_side(3, low)
    to_bit("far_x", 2, even.at[3, low], landing.at[0])
    add_side(3, high)
    to_bit("far_y", 4, even.at[3, high], landing.at[1])
    chip(2)
    arrived("s1")
    add_side(1, low)
    to_bit("first_x", 2, even.at[1, low], landing.at[2])
    add_side(1, high)
    chip(0)
    arrived("s2")
    add_side(2, high)
    to_bit("second_y", 4, even.at[2, high], landing.at[3])
    add_side(2, low)

    count, rows = back_ref.shape[0], back_ref.shape[1]
    per = chunk // (parts * rows)
    for i in range(chunks):
        if i + 1 < chunks:
            fetch(i + 1).start()
        fetch(i).wait()
        value = dot_f32(d_ref[...], n_buf[i % 2]).T
        for s in range(per):
            for f in range(parts):
                at = (s * parts + f) * rows
                terms[f, i * per + s] = value[at : at + rows].astype(BF)
    start("r1", terms.at[before_z], hop_recv.at[0], (me, after_z))

    def add_far(pair, part, slot):
        even[pair, part] = (even[pair, part].astype(F32) + landing[slot].astype(F32)).astype(BF)

    arrived("far_x")
    add_far(2, low, 0)
    to_bit("first_y", 4, even.at[2, low], landing.at[4])
    arrived("far_y")
    add_far(1, high, 1)
    to_bit("second_x", 2, even.at[1, high], landing.at[5])
    arrived("s0")
    for step in range(1, parts):
        arrived("r" + str(step))
        state = hop_recv[step - 1].astype(F32)
        state = state + terms[(z + 2 * parts - 1 - step) % parts].astype(F32)
        if step < parts - 1:
            hop_send[step - 1] = state.astype(BF)
            start("r" + str(step + 1), hop_send.at[step - 1], hop_recv.at[step], (me, after_z))
        else:
            last[...] = state.astype(BF)

    mine = pltpu.make_async_copy(last.at[me], back_ref.at[me], own_sem.at[0])
    mine.start()
    to_bit("b3", 2, last.at[me ^ 6], mid.at[4])
    to_bit("a2", 1, last.at[me ^ 3], mid.at[1])
    to_bit("a4", 1, last.at[me ^ 7], mid.at[3])
    to_bit("a3", 1, last.at[me ^ 5], mid.at[2])
    to_bit("a1", 1, last.at[me ^ 1], back_ref.at[me])
    to_bit("b1", 2, last.at[me ^ 2], back_ref.at[me])
    to_bit("c1", 4, last.at[me ^ 4], back_ref.at[me])
    arrived("a4", "a2", "a3")
    to_bit("b4", 2, mid.at[3], mid.at[5])
    to_bit("b2", 2, mid.at[1], back_ref.at[me ^ 1])
    to_bit("c2", 4, mid.at[2], back_ref.at[me ^ 1])
    arrived("b3")
    to_bit("c3", 4, mid.at[4], back_ref.at[me ^ 2])
    arrived("b4")
    to_bit("c4", 4, mid.at[5], back_ref.at[me ^ 3])

    arrived("first_x", "second_y", "first_y", "second_x")
    gain = w_ref[pl.ds(cols, 8), :].astype(F32)[0:1]
    tall = 64

    def finish(first_slot, second_slot, offset):
        def one(t, carry):
            from_half = pl.ds(pl.multiple_of(t * tall, tall), tall)
            at = pl.ds(pl.multiple_of(t * tall + offset, tall), tall)
            dn = even[0, at].astype(F32) + side_recv[0, at].astype(F32)
            dn = dn + landing[first_slot, from_half].astype(F32)
            dn = dn + landing[second_slot, from_half].astype(F32)
            x = x_ref[at].astype(F32)
            r = lax.rsqrt(jnp.mean(x * x, axis=-1, keepdims=True) + EPS)
            m = x * r
            e = dn * gain
            inner = jnp.mean(e * m, axis=-1, keepdims=True)
            grad_ref[at] = dh_ref[at] + r * (e - m * inner)
            return carry

        lax.fori_loop(0, half // tall, one, 0)

    finish(2, 4, 0)
    finish(3, 5, half)
    arrived("a1", "b1", "c1", "b2", "c2", "c3", "c4")
    mine.wait()
    for copy in made.values():
        copy.wait_send()


def tail(d_t, wt_ext, x, dh1, n1, cols, count, parts):
    local, width = x.shape
    length = n1.shape[0]
    rows = width // (count * parts)
    half = local // 2
    chunk = 512
    anyspace = pl.BlockSpec(memory_space=pl.ANY)
    vmem = pl.BlockSpec(memory_space=pltpu.VMEM)
    copies = 4 + 6 + parts - 1 + 12
    block = (count, rows, cols)
    return pl.pallas_call(
        functools.partial(tail_kernel, parts, cols),
        out_shape=(
            jax.ShapeDtypeStruct((local, width), F32),
            jax.ShapeDtypeStruct(block, BF),
        ),
        in_specs=[vmem, vmem, vmem, vmem, anyspace],
        out_specs=(vmem, anyspace),
        scratch_shapes=[
            pltpu.VMEM((4, local, width), BF),
            pltpu.VMEM((4, local, width), BF),
            pltpu.VMEM((4, local, width), BF),
            pltpu.VMEM((6, half, width), BF),
            pltpu.VMEM((2, length, chunk), BF),
            pltpu.VMEM((parts,) + block, BF),
            pltpu.VMEM((max(1, parts - 2),) + block, BF),
            pltpu.VMEM((parts - 1,) + block, BF),
            pltpu.VMEM(block, BF),
            pltpu.VMEM((6, rows, cols), BF),
            pltpu.SemaphoreType.DMA((copies,)),
            pltpu.SemaphoreType.DMA((copies,)),
            pltpu.SemaphoreType.DMA((2,)),
            pltpu.SemaphoreType.DMA((1,)),
        ],
        compiler_params=pltpu.CompilerParams(
            collective_id=1, has_side_effects=True, vmem_limit_bytes=62 * 1024 * 1024
        ),
        cost_estimate=pl.CostEstimate(
            flops=1 << 30, bytes_accessed=1 << 20, transcendentals=0
        ),
        name="tail",
    )(d_t, wt_ext, x, dh1, n1)


def start_kernel(
    parts, x_ref, attn_ref, ffn_ref, out_ref, down_ref, x_all, attn_all, ffn_mine, out_all,
    down_all, attn_mid, ffn_mid, send, arrive, local_sem,
):
    me = lax.axis_index("seq")
    z = lax.axis_index("fsdp")
    after_z, before_z = (z + 1) % parts, (z + parts - 1) % parts
    half = x_ref.shape[0] // 2
    barrier = pltpu.get_barrier_semaphore()
    for bit in (1, 2, 4):
        pl.semaphore_signal(barrier, inc=1, device_id=(me ^ bit, z), device_id_type=MESH)
    for other in (after_z, before_z):
        pl.semaphore_signal(barrier, inc=1, device_id=(me, other), device_id_type=MESH)
    pl.semaphore_wait(barrier, 5)
    made = {}

    def start(name, source, target, device):
        n = len(made)
        copy = pltpu.make_async_remote_copy(
            src_ref=source, dst_ref=target, send_sem=send.at[n], recv_sem=arrive.at[n],
            device_id=device, device_id_type=MESH,
        )
        made[name] = copy
        copy.start()

    def to_bit(name, bit, source, target):
        start(name, source, target, (me ^ bit, z))

    def arrived(*names):
        for name in names:
            made[name].wait_recv()

    held = [
        pltpu.make_async_copy(x_ref, x_all.at[me], local_sem.at[0]),
        pltpu.make_async_copy(attn_ref.at[me], attn_all.at[z, me], local_sem.at[1]),
        pltpu.make_async_copy(ffn_ref.at[me], ffn_mine.at[me], local_sem.at[2]),
        pltpu.make_async_copy(out_ref, out_all.at[z], local_sem.at[3]),
        pltpu.make_async_copy(down_ref, down_all.at[z], local_sem.at[4]),
    ]
    for copy in held:
        copy.start()

    def swap_first(tag, source, final, mid):
        to_bit(tag + "a2", 1, source.at[me ^ 3], mid.at[1])
        to_bit(tag + "a4", 1, source.at[me ^ 7], mid.at[3])
        to_bit(tag + "a3", 1, source.at[me ^ 5], mid.at[2])
        to_bit(tag + "a1", 1, source.at[me ^ 1], final.at[me])

    def swap_second(tag, source, final, mid):
        to_bit(tag + "b3", 2, source.at[me ^ 6], mid.at[4])
        to_bit(tag + "b1", 2, source.at[me ^ 2], final.at[me])
        arrived(tag + "a4", tag + "a2")
        to_bit(tag + "b4", 2, mid.at[3], mid.at[5])
        to_bit(tag + "b2", 2, mid.at[1], final.at[me ^ 1])

    def swap_third(tag, source, final, mid):
        to_bit(tag + "c1", 4, source.at[me ^ 4], final.at[me])
        arrived(tag + "a3")
        to_bit(tag + "c2", 4, mid.at[2], final.at[me ^ 1])
        arrived(tag + "b3")
        to_bit(tag + "c3", 4, mid.at[4], final.at[me ^ 2])
        arrived(tag + "b4")
        to_bit(tag + "c4", 4, mid.at[5], final.at[me ^ 3])

    def swap_end(tag):
        arrived(*[tag + n for n in ("a1", "b1", "c1", "b2", "c2", "c3", "c4")])

    def around(tag, step, whole):
        if step > 1:
            arrived(tag + str(step - 1))
        at = (z + parts + 1 - step) % parts
        start(tag + str(step), whole.at[at], whole.at[at], (me, after_z))

    attn_sets = (attn_ref, attn_all.at[z], attn_mid)
    ffn_sets = (ffn_ref, ffn_mine, ffn_mid)
    start("o1", out_ref, out_all.at[z], (me, after_z))
    swap_first("attn", *attn_sets)
    swap_second("attn", *attn_sets)
    to_bit("x2", 2, x_ref, x_all.at[me])
    swap_third("attn", *attn_sets)
    to_bit("x4", 4, x_ref, x_all.at[me])
    to_bit("x1", 1, x_ref, x_all.at[me])
    swap_first("ffn", *ffn_sets)
    swap_end("attn")
    held[1].wait()
    around("z", 1, attn_all)
    held[4].wait()
    around("d", 1, down_all)
    for step in range(2, parts):
        around("o", step, out_all)
        around("z", step, attn_all)
    arrived("x2")
    to_bit("x3", 1, x_all.at[me ^ 2], x_all.at[me ^ 2])
    to_bit("f1", 4, x_all.at[me ^ 2, pl.ds(0, half)], x_all.at[me ^ 2, pl.ds(0, half)])
    arrived("x4")
    to_bit("x5", 1, x_all.at[me ^ 4], x_all.at[me ^ 4])
    to_bit("f2", 2, x_all.at[me ^ 4, pl.ds(half, half)], x_all.at[me ^ 4, pl.ds(half, half)])
    around("d", 2, down_all)
    swap_second("ffn", *ffn_sets)
    swap_third("ffn", *ffn_sets)
    for step in range(3, parts):
        around("d", step, down_all)
    arrived("f1", "f2")
    to_bit("x7", 1, x_all.at[me ^ 6], x_all.at[me ^ 6])
    swap_end("ffn")
    arrived("x1", "x3", "x5", "x7", "z" + str(parts - 1), "o" + str(parts - 1))
    arrived("d" + str(parts - 1))
    for copy in made.values():
        copy.wait_send()
    for copy in (held[0], held[2], held[3]):
        copy.wait()


def start_gather(x, attn_send, ffn_send, w_out, w_down, count, parts):
    anyspace = pl.BlockSpec(memory_space=pl.ANY)
    copies = 8 + 2 * 12 + 3 * (parts - 1)
    shapes = (
        jax.ShapeDtypeStruct((count,) + x.shape, BF),
        jax.ShapeDtypeStruct((parts,) + attn_send.shape, BF),
        jax.ShapeDtypeStruct(ffn_send.shape, BF),
        jax.ShapeDtypeStruct((parts,) + w_out.shape, BF),
        jax.ShapeDtypeStruct((parts,) + w_down.shape, BF),
        jax.ShapeDtypeStruct((6,) + attn_send.shape[1:], BF),
        jax.ShapeDtypeStruct((6,) + ffn_send.shape[1:], BF),
    )
    return pl.pallas_call(
        functools.partial(start_kernel, parts),
        out_shape=shapes,
        in_specs=[anyspace] * 5,
        out_specs=(anyspace,) * 7,
        scratch_shapes=[
            pltpu.SemaphoreType.DMA((copies,)),
            pltpu.SemaphoreType.DMA((copies,)),
            pltpu.SemaphoreType.DMA((5,)),
        ],
        compiler_params=pltpu.CompilerParams(
            collective_id=0, has_side_effects=True, vmem_limit_bytes=8 * 1024 * 1024
        ),
        name="start_gather",
    )(x, attn_send, ffn_send, w_out, w_down)[:5]


def ring(axis):
    count = lax.axis_size(axis)
    return [(n, (n + 1) % count) for n in range(count)]


def hop(*blocks):
    return [lax.ppermute(block, "fsdp", ring("fsdp")) for block in blocks]


def collect(pieces, axis):
    count = lax.axis_size(axis)
    me = lax.axis_index(axis)
    whole = jnp.zeros((count,) + pieces[0].shape, pieces[0].dtype)
    for back, piece in enumerate(pieces):
        whole = lax.dynamic_update_index_in_dim(whole, piece, (me + count - back) % count, 0)
    return whole


def term_of(terms, step):
    count = lax.axis_size("fsdp")
    me = lax.axis_index("fsdp")
    return lax.dynamic_index_in_dim(terms, (me + 2 * count - 1 - step) % count, 0, False)


def launch(states):
    return hop(*[state.astype(BF) for state in states])


def landed(moved, terms, step):
    return [m.astype(F32) + term_of(t, step).astype(F32) for m, t in zip(moved, terms)]


def ring_finish(moved, terms, step):
    states = landed(moved, terms, step)
    for n in range(step + 1, lax.axis_size("fsdp")):
        states = landed(launch(states), terms, n)
    return states


def fence(*values):
    return lax.optimization_barrier(values)


def swap(block, bit):
    count = lax.axis_size("seq")
    return lax.ppermute(block, "seq", [(n, n ^ bit) for n in range(count)])


def gather_plain(block):
    me = lax.axis_index("seq")
    whole = lax.all_gather(block, "seq", axis=0, tiled=False)
    return [lax.dynamic_index_in_dim(whole, me ^ c, 0, False) for c in range(whole.shape[0])]


def scatter_plain(parts):
    me = lax.axis_index("seq")
    whole = jnp.zeros((len(parts),) + parts[0].shape, BF)
    for c, part in enumerate(parts):
        whole = lax.dynamic_update_index_in_dim(whole, part.astype(BF), me ^ c, 0)
    return lax.psum_scatter(whole, "seq", scatter_dimension=0, tiled=False).astype(F32)


def far_halves(over_x, over_y):
    half = over_x.shape[0] // 2
    return swap(over_x[:half], 4), swap(over_y[half:], 2)


def chip_sum(own, other):
    return own.astype(F32) + swap(other, 1).astype(F32)


def total_of(*terms):
    total = terms[0].astype(F32)
    for term in terms[1:]:
        total = total + term.astype(F32)
    return total


def plus(*terms):
    return total_of(*terms).astype(BF)


def exchange(array):
    return lax.all_to_all(array, "seq", split_axis=0, concat_axis=0, tiled=True)


def document_starts(flags_all):
    length = flags_all.shape[0]
    lanes = 128
    table = flags_all.reshape(length // lanes, lanes)
    place = jnp.arange(length, dtype=jnp.int32).reshape(table.shape)
    marked = jnp.where((table != 0) & (place > 0), place, 0)
    inside = jnp.arange(lanes)[None, :] <= jnp.arange(lanes)[:, None]
    local = jnp.max(jnp.where(inside[None], marked[:, None, :], 0), axis=-1)
    rows = jnp.max(marked, axis=1)
    count = length // lanes
    before = jnp.arange(count)[None, :] < jnp.arange(count)[:, None]
    carried = jnp.max(jnp.where(before, rows[None, :], 0), axis=-1)
    return jnp.maximum(local, carried[:, None]).reshape(length)


def body(
    tokens, doc_starts, gain_attn, w_query, w_key, w_value, w_out, gain_ffn, w_gate, w_up, w_down,
    cotangent,
):
    streams, local, width = tokens.shape
    assert streams == 1
    count = lax.axis_size("seq")
    parts = lax.axis_size("fsdp")
    me = lax.axis_index("seq")
    cube = count == 8
    length = local * count
    half = local // 2
    group = H // count
    share = (H // KV) // group
    rows = w_query.shape[0]
    hidden = w_gate.shape[1] // count
    group_width = group * HD
    attn_cols = group_width + 2 * HD
    flag_cols = local // rows
    extra_cols = 128
    sheet = (length, width)

    own = tokens[0]
    attn_send = jnp.concatenate(
        [
            w_query.reshape(rows, count, group_width),
            jnp.repeat(w_key.reshape(rows, KV, HD), share, axis=1),
            jnp.repeat(w_value.reshape(rows, KV, HD), share, axis=1),
        ],
        axis=2,
    ).transpose(1, 0, 2)
    extra = jnp.concatenate(
        [
            gain_attn[:, None],
            gain_ffn[:, None],
            doc_starts[0].astype(BF).reshape(rows, flag_cols),
            jnp.zeros((rows, extra_cols - 2 - flag_cols), BF),
        ],
        axis=1,
    )
    attn_send = jnp.concatenate(
        [attn_send, jnp.broadcast_to(extra[None], (count,) + extra.shape)], axis=2
    )
    ffn_send = jnp.concatenate(
        [w_gate.reshape(rows, count, hidden), w_up.reshape(rows, count, hidden)], axis=0
    ).transpose(1, 0, 2)
    z = lax.axis_index("fsdp")
    if cube:
        x_all, attn_all, ffn_part, out_part, down_w = start_gather(
            own, attn_send, ffn_send, w_out, w_down, count, parts
        )
    else:
        x_all = lax.all_gather(own, "seq", axis=0, tiled=False)
        attn_all = lax.all_gather(exchange(attn_send), "fsdp", axis=0, tiled=False)
        ffn_part = exchange(ffn_send)
        out_part = lax.all_gather(w_out, "fsdp", axis=0, tiled=False)
        down_w = lax.all_gather(w_down, "fsdp", axis=0, tiled=False)
    down_w = down_w.reshape(hidden, width)
    dy = cotangent[0]
    own, x_all, attn_all, ffn_part, out_part, dy = fence(
        own, x_all, attn_all, ffn_part, out_part, dy
    )
    ffn_pieces = [[ffn_part.reshape(count, 2, rows, hidden)]]

    out_w = lax.all_gather(out_part.reshape(parts * rows, width), "seq", axis=0, tiled=True)
    if len(ffn_pieces) < parts:
        ffn_pieces.append(hop(*ffn_pieces[-1]))
    flags = lax.dynamic_index_in_dim(attn_all, z, 0, False)
    flags = flags[:, :, attn_cols + 2 : attn_cols + 2 + flag_cols].reshape(length)
    last = document_starts(flags)
    position = (jnp.arange(length, dtype=jnp.int32) - last).astype(F32)
    frequency = jnp.exp(jnp.arange(HALF, dtype=F32) * (-2.0 * math.log(10000.0) / HD))
    angle = frequency[:, None] * position[None, :]
    cosine, sine = jnp.cos(angle), jnp.sin(angle)
    blocks = length // BQ
    by_block = last.reshape(blocks, BQ)
    starts = jnp.tile(by_block, (1, group)).reshape(blocks, 1, group * BQ)
    first_row = jnp.arange(blocks, dtype=jnp.int32) * BQ
    low = by_block[:, 0] // BK
    high = (first_row + BQ + BK - 1) // BK
    begin = jnp.minimum((by_block[:, -1] + BK - 1) // BK, high)
    end = jnp.maximum((first_row + 1) // BK, begin)
    bounds = jnp.stack([low, begin, end, high], axis=1)
    w_ext = attn_all.transpose(1, 0, 2, 3).reshape(width, attn_cols + extra_cols)
    n1_all, projected, wt_ext = project(x_all, w_ext, attn_cols)
    attn_t = wt_ext[:attn_cols]
    gain_one = wt_ext[attn_cols].astype(F32)
    gain_two = wt_ext[attn_cols + 1].astype(F32)
    projected, cosine, sine, starts, bounds, ffn_last, dy = fence(
        projected, cosine, sine, starts, bounds, ffn_pieces[-1], dy
    )
    ffn_pieces[-1] = ffn_last

    dy_all = lax.all_gather(dy, "seq", axis=0, tiled=False)
    cut = blocks * 11 // 16
    ready = (bounds, projected, cosine, sine, starts, group, count, local)
    if len(ffn_pieces) < parts:
        ffn_pieces.append(hop(*ffn_pieces[-1]))
    o_half, lse_one, qt_one, k_t, k_n, v_n, v_t = attend(*ready, 0, cut, None)
    o_half, lse_one, qt_one, k_t, k_n, v_n, v_t, ffn_last, out_w = fence(
        o_half, lse_one, qt_one, k_t, k_n, v_n, v_t, ffn_pieces[-1], out_w
    )
    ffn_pieces[-1] = ffn_last
    while len(ffn_pieces) < parts:
        ffn_pieces.append(hop(*ffn_pieces[-1]))
    o_heads, lse_two, qt_two = attend(*ready, cut, blocks - cut, (o_half, k_n, v_t))
    o_heads, lse_two, qt_two, ffn_pieces = fence(o_heads, lse_two, qt_two, ffn_pieces)

    o_t = exchange(o_heads).reshape(count * group_width, local)
    o_t, dy_all, qt_one, qt_two, lse_one, lse_two = fence(
        o_t, dy_all, qt_one, qt_two, lse_one, lse_two
    )

    ffn_w = collect([piece[0] for piece in ffn_pieces], "fsdp").transpose(2, 1, 0, 3, 4).reshape(2, width, hidden)
    gate_w, up_w = ffn_w[0], ffn_w[1]
    x = own.astype(F32)
    r1 = lax.rsqrt(jnp.mean(x * x, axis=-1, keepdims=True) + EPS)
    h1 = x + jnp.einsum("et,ed->td", o_t, out_w, preferred_element_type=F32)
    r2 = lax.rsqrt(jnp.mean(h1 * h1, axis=-1, keepdims=True) + EPS)
    n2 = (h1 * r2 * gain_two).astype(BF)
    n2, h1, r2 = fence(n2, h1, r2)

    def over_seq(part):
        whole = part.reshape(-1, part.shape[-1])
        return lax.psum_scatter(whole, "seq", scatter_dimension=0, tiled=True)

    kept = None

    weights = (dy_all, gate_w, up_w, down_w)

    if cube:
        side = swap(n2, 1)
        low_n, high_n = n2[:half], n2[half:]
        x_low, y_low = swap(low_n, 2), swap(low_n, 4)
        x_high, y_high = swap(high_n, 2), swap(high_n, 4)
        side, gate_w, up_w = fence(side, gate_w, up_w)
        weights = (dy_all, gate_w, up_w, down_w)
        kept, (own_a, own_b, own_c, own_d) = ffn_chunk(
            [(n2, 0, me, 0), (n2, 1, me, 1), (side, 0, me ^ 1, 0), (side, 1, me ^ 1, 1)],
            *weights, kept,
        )
        kept, own_a, own_b, own_c, own_d, x_low, y_low = fence(
            kept, own_a, own_b, own_c, own_d, x_low, y_low
        )

        far_a = swap(x_low, 4)
        side_x, side_y = swap(x_low, 1), swap(y_low, 1)
        own_c, own_d = swap(own_c, 1), swap(own_d, 1)
        side_x, side_y, x_low, y_low, kept = fence(side_x, side_y, x_low, y_low, kept)
        kept, (x_a, x_b, y_a, y_b) = ffn_chunk(
            [(x_low, 0, me ^ 2, 0), (side_x, 0, me ^ 3, 0), (y_low, 0, me ^ 4, 0),
             (side_y, 0, me ^ 5, 0)],
            *weights, kept,
        )
        kept, x_a, x_b, y_a, y_b, x_high, y_high, own_c, own_d = fence(
            kept, x_a, x_b, y_a, y_b, x_high, y_high, own_c, own_d
        )

        far_b = swap(y_high, 2)
        side_x, side_y = swap(x_high, 1), swap(y_high, 1)
        x_b, y_b = swap(x_b, 1), swap(y_b, 1)
        side_x, side_y, x_high, y_high, kept, x_a, x_b = fence(
            side_x, side_y, x_high, y_high, kept, x_a, x_b
        )
        x_first = swap(plus(x_a, x_b), 2)
        kept, (x_c, x_d, y_c, y_d) = ffn_chunk(
            [(x_high, 0, me ^ 2, 1), (side_x, 0, me ^ 3, 1), (y_high, 0, me ^ 4, 1),
             (side_y, 0, me ^ 5, 1)],
            *weights, kept,
        )
        kept, x_c, x_d, y_c, y_d, far_a, far_b, y_a, y_b = fence(
            kept, x_c, x_d, y_c, y_d, far_a, far_b, y_a, y_b
        )

        side_far, side_more = swap(far_a, 1), swap(far_b, 1)
        x_d, y_d = swap(x_d, 1), swap(y_d, 1)
        side_far, side_more, y_c, y_d = fence(side_far, side_more, y_c, y_d)
        y_second = swap(plus(y_c, y_d), 4)
        kept, (far_one, far_two, far_three, far_four) = ffn_chunk(
            [(far_a, 0, me ^ 6, 0), (far_b, 0, me ^ 6, 1), (side_far, 0, me ^ 7, 0),
             (side_more, 0, me ^ 7, 1)],
            *weights, kept,
        )
        kept, far_one, far_two, far_three, far_four, x_first, y_second, x_c, x_d = fence(
            kept, far_one, far_two, far_three, far_four, x_first, y_second, x_c, x_d
        )
        act, d_gate, d_up, n2_all, y_one, y_two = kept
        n2_all, dy_rows = n2_all.reshape(sheet), dy_all.reshape(sheet)
        act, d_gate, d_up = [a.reshape(length, hidden) for a in (act, d_gate, d_up)]

        x_far = swap(plus(far_one, swap(far_three, 1)), 2)
        y_far = swap(plus(far_two, swap(far_four, 1)), 4)
        gate_t = side_terms(n2_all, d_gate, count, parts)
        x_far, y_far, gate_t, y_one = fence(x_far, y_far, gate_t, y_one)

        x_second = swap(plus(x_c, x_d, y_far), 2)
        y_first = swap(plus(y_a, y_b, x_far), 4)
        (gate_moved,) = launch([term_of(gate_t, 0)])
        y_one = over_seq(y_one)
        up_t = side_terms(n2_all, d_up, count, parts)
        x_second, y_first, up_t, gate_moved, act = fence(x_second, y_first, up_t, gate_moved, act)
        dn2 = jnp.concatenate(
            [
                total_of(own_a, own_c, x_first, y_first),
                total_of(own_b, own_d, x_second, y_second),
            ],
            axis=0,
        )
    else:
        n2_blocks = gather_plain(n2)
        dn2_parts = []
        for c in range(0, count, 2):
            each = range(max(1, local // 256))
            kept, found = ffn_chunk(
                [(n2_blocks[n], t, me ^ n, t) for n in (c, c + 1) for t in each], *weights, kept
            )
            dn2_parts += [
                jnp.concatenate(found[: len(each)], axis=0),
                jnp.concatenate(found[len(each) :], axis=0),
            ]
        act, d_gate, d_up, n2_all, y_one, y_two = kept
        n2_all, dy_rows = n2_all.reshape(sheet), dy_all.reshape(sheet)
        act, d_gate, d_up = [a.reshape(length, hidden) for a in (act, d_gate, d_up)]
        dn2 = scatter_plain(dn2_parts)
        gate_t = side_terms(n2_all, d_gate, count, parts)
        up_t = side_terms(n2_all, d_up, count, parts)
        (gate_moved,) = launch([term_of(gate_t, 0)])
        y_one = over_seq(y_one)

    m2 = h1 * r2
    e2 = dn2 * gain_two
    dh1 = dy.astype(F32) + r2 * (e2 - m2 * jnp.mean(e2 * m2, axis=-1, keepdims=True))
    db = dh1.astype(BF)
    do_t = jnp.einsum("ed,td->et", out_w, db, preferred_element_type=F32).astype(BF)
    (up_moved,) = launch([term_of(up_t, 0)])
    (gate_state,) = landed([gate_moved], [gate_t], 1)
    if parts > 2:
        (gate_moved,) = launch([gate_state])
    do_t, db, dh1, up_moved, gate_moved, gate_state, y_two = fence(
        do_t, db, dh1, up_moved, gate_moved, gate_state, y_two
    )
    y_two = over_seq(y_two)
    do_heads = exchange(do_t.reshape(count, group_width, local))
    term_out = dot_f32(o_t, db).astype(BF)
    term_down = down_terms_of(act, dy_rows).reshape(parts, hidden // parts, width)
    (up_state,) = landed([up_moved], [up_t], 1)
    if parts > 2:
        (up_moved,) = launch([up_state])
    do_heads, term_out, term_down, y_one, up_moved, up_state = fence(
        do_heads, term_out, term_down, y_one, up_moved, up_state
    )

    pair_t = [gate_t, up_t]
    pair = [gate_state, up_state]
    if parts > 2:
        pair = landed([gate_moved, up_moved], pair_t, 2)
    moved = launch((pair if parts > 3 else []) + [term_of(term_down, 0)])
    saved = (bounds, qt_one, k_n, k_t, v_n, cosine, sine, starts, o_heads, do_heads, lse_one, group)
    dq_one, dk, dv = attend_back(*saved, 0, cut, None)
    dq_one, dk, dv, moved, pair, do_heads, y_two, term_out = fence(
        dq_one, dk, dv, moved, pair, do_heads, y_two, term_out
    )
    part_out = over_seq(term_out)
    down_state = landed(moved[-1:], [term_down], 1)
    if parts > 3:
        pair = ring_finish(moved[:2], pair_t, 3)
    ffn_back = exchange(jnp.stack(pair, axis=1).astype(BF))
    moved = launch(down_state if parts > 2 else [])
    saved = (bounds, qt_two, k_n, k_t, v_n, cosine, sine, starts, o_heads, do_heads, lse_two, group)
    dq_two, dkv_t = attend_back(*saved, cut, blocks - cut, (dk, dv))

    def along(weight, grad):
        return jnp.sum(weight.astype(F32) * grad, axis=1)

    ffn_back, dq_two, dkv_t = fence(ffn_back, dq_two, dkv_t)
    ffn_back = ffn_back.astype(F32)
    grad_gate = ffn_back[:, 0].transpose(1, 0, 2).reshape(rows, count * hidden)
    grad_up = ffn_back[:, 1].transpose(1, 0, 2).reshape(rows, count * hidden)
    gain_sum = along(w_gate, grad_gate) + along(w_up, grad_up)
    output = (h1 + jnp.concatenate([y_one, y_two], axis=1).astype(F32)).astype(BF)
    dq_two, dkv_t, moved, down_state, part_out, grad_gate, grad_up, gain_sum, output = fence(
        dq_two, dkv_t, moved, down_state, part_out, grad_gate, grad_up, gain_sum, output
    )

    d_t = jnp.concatenate([jnp.concatenate([dq_one, dq_two], axis=1), dkv_t], axis=0)
    def pair_of(c):
        return jnp.concatenate(
            [lax.dynamic_slice_in_dim(d_t, (me ^ n) * local, local, 1) for n in (c, c + 1)], axis=1
        )

    def dn1_chunk(c):
        part = jnp.einsum("et,ed->td", pair_of(c), attn_t, preferred_element_type=F32).astype(BF)
        return part[:local], part[local:]

    n1_rows = n1_all.reshape(sheet)
    if parts > 2:
        down_state = landed(moved, [term_down], 2)
    moved = launch(down_state if parts > 3 else [])
    grad_out = lax.psum_scatter(part_out, "fsdp", scatter_dimension=0, tiled=True).astype(F32)
    if cube:
        grad_tokens, attn_back = tail(d_t, wt_ext, own, dh1, n1_rows, attn_cols, count, parts)
    else:
        dn1 = scatter_plain([piece for c in range(0, count, 2) for piece in dn1_chunk(c)])
        attn_terms = [attn_terms_of(d_t, n1_rows, count, parts)]
        (part_attn,) = ring_finish(launch([term_of(attn_terms[0], 0)]), attn_terms, 1)
        attn_back = exchange(part_attn.astype(BF))
        m1 = x * r1
        e1 = dn1 * gain_one
        grad_tokens = dh1 + r1 * (e1 - m1 * jnp.mean(e1 * m1, axis=-1, keepdims=True))
    grad_tokens, attn_back, moved, grad_out = fence(grad_tokens, attn_back, moved, grad_out)
    if parts > 3:
        down_state = ring_finish(moved, [term_down], 3)
    grad_down = down_state[0].reshape(hidden // parts, width)

    attn_back = attn_back.astype(F32)
    grad_query = attn_back[:, :, :group_width].transpose(1, 0, 2).reshape(rows, H * HD)
    pair = attn_back[:, :, group_width:].reshape(KV, share, rows, 2 * HD).sum(axis=1)
    grad_key = pair[:, :, :HD].transpose(1, 0, 2).reshape(rows, KV * HD)
    grad_value = pair[:, :, HD:].transpose(1, 0, 2).reshape(rows, KV * HD)

    grad_gain_attn = (
        along(w_query, grad_query) + along(w_key, grad_key) + along(w_value, grad_value)
    ) / gain_attn.astype(F32)
    grad_gain_ffn = gain_sum / gain_ffn.astype(F32)
    return (
        output[None],
        grad_tokens[None],
        grad_gain_attn,
        grad_query,
        grad_key,
        grad_value,
        grad_out,
        grad_gain_ffn,
        grad_gate,
        grad_up,
        grad_down,
    )


def solution(mesh):
    sheet = P("fsdp", "seq", None)
    line = P(("seq", "fsdp"))
    matrix = P(("seq", "fsdp"), None)
    return jax.shard_map(
        body,
        mesh=mesh,
        in_specs=(
            sheet, P("fsdp", "seq"), line, matrix, matrix, matrix, matrix, line, matrix, matrix,
            matrix, sheet,
        ),
        out_specs=(
            sheet, sheet, line, matrix, matrix, matrix, matrix, line, matrix, matrix, matrix,
        ),
        check_vma=False,
    )
```

```python
import functools
import math

import jax
import jax.numpy as jnp
from jax import lax
from jax.experimental import pallas as pl
from jax.experimental.pallas import tpu as pltpu
from jax.sharding import PartitionSpec as P

H = 32
KV = 4
HD = 64
HALF = HD // 2
EPS = 1e-05
NEG = -1e30
BQ = 256
BK = 512
BF = jnp.bfloat16
F32 = jnp.float32
VMEM_LIMIT = 56 * 1024 * 1024
FFN_VMEM = 40 * 1024 * 1024
MESH = pl.DeviceIdType.MESH


def dot_f32(a, b):
    return jnp.dot(a, b, preferred_element_type=F32)


def heads_wide(block, group):
    return jnp.concatenate([block[h * HD : (h + 1) * HD] for h in range(group)], axis=1)


def heads_tall(block, group):
    width = block.shape[1] // group
    return jnp.concatenate([block[:, h * width : (h + 1) * width] for h in range(group)], axis=0)


def allowed_block(step, block_keys, first_row, block_rows, wide, starts):
    key = step * block_keys + lax.broadcasted_iota(jnp.int32, (block_keys, 1), 0)
    row = first_row + (lax.broadcasted_iota(jnp.int32, (1, wide), 1) & (block_rows - 1))
    return (key <= row) & (key >= starts)


def three_loops(bounds_ref, index, body):
    low, first, second, high = (bounds_ref[index, n] for n in range(4))
    lax.fori_loop(low, first, lambda j, c: body(j, True), None)
    lax.fori_loop(first, second, lambda j, c: body(j, False), None)
    lax.fori_loop(second, high, lambda j, c: body(j, True), None)


def turned(block, cosine, sine):
    first, second = block[:HALF], block[HALF:]
    return jnp.concatenate(
        [first * cosine - second * sine, second * cosine + first * sine], axis=0
    )


def turned_back(block, cosine, sine):
    first, second = block[:HALF], block[HALF:]
    return jnp.concatenate(
        [first * cosine + second * sine, second * cosine - first * sine], axis=0
    )


def forward_kernel(
    group, skip, final, bounds_ref, q_ref, kv_ref, cos_ref, sin_ref, start_ref, *rest
):
    if final:
        kn_ref, vt, o_ref, lse_ref, qt_ref, acc, top, total = rest
    else:
        o_ref, lse_ref, qt_ref, kt_ref, kn_ref, vn_ref, vt, acc, top, total = rest
    step = pl.program_id(0)
    i = step + skip
    rows = q_ref.shape[1]
    wide = rows * group
    here = pl.ds(pl.multiple_of(i * rows, rows), rows)
    cosine, sine = cos_ref[:, here], sin_ref[:, here]

    if not final:

        @pl.when(step == 0)
        def _():
            for part in range(kv_ref.shape[1] // BK):
                at = pl.ds(part * BK, BK)
                k = turned(kv_ref[:HD, at], cos_ref[:, at], sin_ref[:, at]).astype(BF)
                v = kv_ref[HD:, at].astype(BF)
                kt_ref[:, at] = k
                vt[:, at] = v
                kn_ref[at, :] = k.T
                vn_ref[at, :] = v.T

    heads = [
        turned(q_ref[h * HD : (h + 1) * HD, :], cosine, sine).astype(BF) * BF(HD**-0.5)
        for h in range(group)
    ]
    qt_ref[...] = jnp.concatenate(heads, axis=0)
    starts = start_ref[0]
    acc[...] = jnp.zeros_like(acc)
    top[...] = jnp.full_like(top, NEG)
    total[...] = jnp.zeros_like(total)

    parts_of = [pl.ds(h * rows, rows) for h in range(group)]
    row = i * rows + lax.broadcasted_iota(jnp.int32, (1, rows), 1)
    floor = starts[:, :rows]

    def block(j, masked):
        at = pl.multiple_of(j * BK, BK)
        k = kn_ref[pl.ds(at, BK), :]
        v = vt[:, pl.ds(at, BK)]
        scores = [dot_f32(k, q) for q in heads]
        if masked:
            key = at + lax.broadcasted_iota(jnp.int32, (BK, 1), 0)
            ok = (key <= row) & (key >= floor)
        for part, s in zip(parts_of, scores):
            if masked:
                s = jnp.where(ok, s, NEG)
            old = top[:, part]
            new = jnp.maximum(old, jnp.max(s, axis=0, keepdims=True))
            p = jnp.exp(s - new)
            keep = jnp.exp(old - new)
            top[:, part] = new
            total[:, part] = total[:, part] * keep + jnp.sum(p, axis=0, keepdims=True)
            acc[:, part] = acc[:, part] * keep + dot_f32(v, p.astype(BF))

    three_loops(bounds_ref, i, block)
    o = acc[...] / total[...]
    o_ref[0] = heads_tall(o, group).astype(BF)
    lse_ref[0] = top[...] + jnp.log(total[...])


def backward_kernel(
    group, skip, final, bounds_ref, q_ref, k_ref, kt_ref, v_ref, cos_ref, sin_ref, start_ref,
    o_ref, do_ref, lse_ref, *rest
):
    if final:
        dk_before, dv_before, dq_ref, dkv_ref, dk, dv, acc = rest
    else:
        dq_ref, dk, dv, acc = rest
    step = pl.program_id(0)
    i = step + skip
    rows = q_ref.shape[1]
    wide = rows * group
    q4 = heads_wide(q_ref[...], group)
    g4 = heads_wide(do_ref[0], group)
    o4 = heads_wide(o_ref[0], group)
    delta = jnp.sum(g4.astype(F32) * o4.astype(F32), axis=0, keepdims=True)
    q4t = q4.T
    g4t = g4.T
    starts = start_ref[0]
    lse = lse_ref[0]
    acc[...] = jnp.zeros_like(acc)

    @pl.when(step == 0)
    def _():
        dk[...] = dk_before[...] if final else jnp.zeros_like(dk)
        dv[...] = dv_before[...] if final else jnp.zeros_like(dv)

    def block(j, masked):
        at = pl.multiple_of(j * BK, BK)
        s = dot_f32(k_ref[pl.ds(at, BK), :], q4)
        p = jnp.exp(s - lse)
        if masked:
            p = jnp.where(allowed_block(j, BK, i * rows, rows, wide, starts), p, 0.0)
        dp = dot_f32(v_ref[pl.ds(at, BK), :], g4)
        ds = (p * (dp - delta)).astype(BF)
        dv[pl.ds(at, BK), :] += dot_f32(p.astype(BF), g4t)
        dk[pl.ds(at, BK), :] += dot_f32(ds, q4t)
        acc[...] += dot_f32(kt_ref[:, pl.ds(at, BK)], ds)

    three_loops(bounds_ref, i, block)
    here = pl.ds(pl.multiple_of(i * rows, rows), rows)
    cosine, sine = cos_ref[:, here], sin_ref[:, here]
    for h in range(group):
        dq = acc[:, h * rows : (h + 1) * rows] * (HD**-0.5)
        dq_ref[h * HD : (h + 1) * HD, :] = turned_back(dq, cosine, sine).astype(BF)

    if final:

        @pl.when(step == pl.num_programs(0) - 1)
        def _():
            for part in range(dk.shape[0] // BK):
                at = pl.ds(part * BK, BK)
                dk_t = turned_back(dk[at, :].T, cos_ref[:, at], sin_ref[:, at])
                dkv_ref[:HD, at] = dk_t.astype(BF)
                dkv_ref[HD:, at] = dv[at, :].T.astype(BF)


def whole_spec(shape):
    return pl.BlockSpec(shape, lambda i, b: (0,) * len(shape))


def attend(
    bounds, projected, cosine, sine, starts, group, senders, local, skip, blocks, before
):
    length = projected.shape[1]
    per = local // BQ
    wide = group * HD
    final = before is not None
    line = pl.BlockSpec((1, 1, group * BQ), lambda i, b: (i + skip, 0, 0))
    piece = pl.BlockSpec((1, wide, BQ), lambda i, b: ((i + skip) // per, 0, (i + skip) % per))
    own_line = pl.BlockSpec((1, 1, group * BQ), lambda i, b: (i, 0, 0))
    tall, flat = whole_spec((length, HD)), whole_spec((HD, length))
    arrays = [projected, projected, cosine, sine, starts]
    in_specs = [
        pl.BlockSpec((wide, BQ), lambda i, b: (0, i + skip)),
        pl.BlockSpec((2 * HD, length), lambda i, b: (wide // (2 * HD), 0)),
        whole_spec((HALF, length)),
        whole_spec((HALF, length)),
        line,
    ]
    out_shape = [
        jax.ShapeDtypeStruct((senders, wide, local), BF),
        jax.ShapeDtypeStruct((blocks, 1, group * BQ), F32),
        jax.ShapeDtypeStruct((wide, blocks * BQ), BF),
    ]
    out_specs = [piece, own_line, pl.BlockSpec((wide, BQ), lambda i, b: (0, i))]
    scratch = [
        pltpu.VMEM((HD, group * BQ), F32),
        pltpu.VMEM((1, group * BQ), F32),
        pltpu.VMEM((1, group * BQ), F32),
    ]
    aliases = {}
    kernel = functools.partial(forward_kernel, group, skip, final)
    if final:
        o_before, kn, vt = before
        arrays += [kn, vt, o_before]
        in_specs += [tall, flat, pl.BlockSpec(memory_space=pl.ANY)]
        aliases = {8: 0}
        inner = kernel

        def kernel(*refs):
            return inner(*refs[:8], *refs[9:])

    else:
        out_shape += [
            jax.ShapeDtypeStruct((HD, length), BF),
            jax.ShapeDtypeStruct((length, HD), BF),
            jax.ShapeDtypeStruct((length, HD), BF),
            jax.ShapeDtypeStruct((HD, length), BF),
        ]
        out_specs += [flat, tall, tall, flat]
    return pl.pallas_call(
        kernel,
        out_shape=out_shape,
        grid_spec=pltpu.PrefetchScalarGridSpec(
            num_scalar_prefetch=1,
            grid=(blocks,),
            in_specs=in_specs,
            out_specs=out_specs,
            scratch_shapes=scratch,
        ),
        input_output_aliases=aliases,
        compiler_params=pltpu.CompilerParams(
            dimension_semantics=("arbitrary",), vmem_limit_bytes=VMEM_LIMIT
        ),
        cost_estimate=pl.CostEstimate(
            flops=20 * group * length * length * HD // 2,
            bytes_accessed=4 * group * length * HD,
            transcendentals=group * length * length // 8,
        ),
        name="attend",
    )(bounds, *arrays)


def attend_back(
    bounds, qt, k, kt, v, cosine, sine, starts, o, do, lse, group, skip, blocks, before
):
    length = k.shape[0]
    senders, _, local = o.shape
    per = local // BQ
    final = before is not None
    wide = group * HD
    piece = pl.BlockSpec((1, wide, BQ), lambda i, b: ((i + skip) // per, 0, (i + skip) % per))
    line = pl.BlockSpec((1, 1, group * BQ), lambda i, b: (i + skip, 0, 0))
    tall = whole_spec((length, HD))
    arrays = [qt, k, kt, v, cosine, sine, starts, o, do, lse]
    in_specs = [
        pl.BlockSpec((wide, BQ), lambda i, b: (0, i)),
        tall,
        whole_spec((HD, length)),
        tall,
        whole_spec((HALF, length)),
        whole_spec((HALF, length)),
        line,
        piece,
        piece,
        pl.BlockSpec((1, 1, group * BQ), lambda i, b: (i, 0, 0)),
    ]
    out_specs = [pl.BlockSpec((wide, BQ), lambda i, b: (0, i))]
    out_shape = [jax.ShapeDtypeStruct((wide, blocks * BQ), BF)]
    scratch = [pltpu.VMEM((HD, group * BQ), F32)]
    if final:
        arrays += list(before)
        in_specs += [tall, tall]
        out_specs += [whole_spec((2 * HD, length))]
        out_shape += [jax.ShapeDtypeStruct((2 * HD, length), BF)]
        scratch = [pltpu.VMEM((length, HD), F32), pltpu.VMEM((length, HD), F32)] + scratch
    else:
        out_specs += [tall, tall]
        out_shape += [jax.ShapeDtypeStruct((length, HD), F32)] * 2
    return pl.pallas_call(
        functools.partial(backward_kernel, group, skip, final),
        out_shape=out_shape,
        grid_spec=pltpu.PrefetchScalarGridSpec(
            num_scalar_prefetch=1,
            grid=(blocks,),
            in_specs=in_specs,
            out_specs=out_specs,
            scratch_shapes=scratch,
        ),
        compiler_params=pltpu.CompilerParams(
            dimension_semantics=("arbitrary",), vmem_limit_bytes=VMEM_LIMIT
        ),
        cost_estimate=pl.CostEstimate(
            flops=25 * group * length * length * HD // 2,
            bytes_accessed=8 * group * length * HD,
            transcendentals=group * length * length // 8,
        ),
        name="attend_back",
    )(bounds, *arrays)


def project_kernel(cols, x_ref, w_ref, n_ref, p_ref, wt_ref):
    @pl.when(pl.program_id(0) == 0)
    def _():
        wt_ref[...] = w_ref[...].T

    wide = x_ref[0].astype(F32)
    scale = lax.rsqrt(jnp.mean(wide * wide, axis=-1, keepdims=True) + EPS)
    gain = wt_ref[pl.ds(cols, 8), :].astype(F32)[0:1]
    normed = (wide * scale * gain).astype(BF)
    n_ref[0] = normed
    p_ref[...] = lax.dot_general(
        wt_ref[:cols, :], normed, (((1,), (1,)), ((), ())), preferred_element_type=F32
    )


def project(x_all, w_ext, cols):
    count, local, width = x_all.shape
    wide = w_ext.shape[1]
    block = pl.BlockSpec((1, local, width), lambda i: (i, 0, 0))
    return pl.pallas_call(
        functools.partial(project_kernel, cols),
        out_shape=(
            jax.ShapeDtypeStruct(x_all.shape, BF),
            jax.ShapeDtypeStruct((cols, count * local), F32),
            jax.ShapeDtypeStruct((wide, width), BF),
        ),
        grid=(count,),
        in_specs=[block, pl.BlockSpec((width, wide), lambda i: (0, 0))],
        out_specs=(
            block,
            pl.BlockSpec((cols, local), lambda i: (0, i)),
            pl.BlockSpec((wide, width), lambda i: (0, 0)),
        ),
        compiler_params=pltpu.CompilerParams(
            dimension_semantics=("arbitrary",), vmem_limit_bytes=VMEM_LIMIT
        ),
        cost_estimate=pl.CostEstimate(
            flops=2 * cols * width * count * local,
            bytes_accessed=4 * width * count * local,
            transcendentals=0,
        ),
        name="project",
    )(x_all, w_ext)


def ffn_kernel(tiles, places_ref, *refs):
    n_refs, (dy_ref, gate_ref, up_ref, down_ref) = refs[:tiles], refs[tiles : tiles + 4]
    outs = refs[-(6 + tiles) :]
    act_ref, dg_ref, du_ref, n_ref, ya_ref, yb_ref = outs[:6]
    which = pl.program_id(0)
    n = n_refs[0][...]
    for t in range(1, tiles):
        n = jnp.where(which == t, n_refs[t][...], n)
    n_ref[0] = n
    dy = dy_ref[0]
    across = (((1,), (1,)), ((), ()))
    gate = dot_f32(n, gate_ref[...])
    up = dot_f32(n, up_ref[...])
    d_act = lax.dot_general(dy, down_ref[...], across, preferred_element_type=F32)
    sig = jax.nn.sigmoid(gate)
    silu = gate * sig
    act = (silu * up).astype(BF)
    d_gate = (d_act * up * sig * (1.0 + gate * (1.0 - sig))).astype(BF)
    d_up = (d_act * silu).astype(BF)
    act_ref[0] = act
    dg_ref[0] = d_gate
    du_ref[0] = d_up
    split = ya_ref.shape[-1]
    ya_ref[0] = dot_f32(act, down_ref[:, :split]).astype(BF)
    yb_ref[0] = dot_f32(act, down_ref[:, split:]).astype(BF)
    part = lax.dot_general(d_gate, gate_ref[...], across, preferred_element_type=F32)
    part += lax.dot_general(d_up, up_ref[...], across, preferred_element_type=F32)
    part = part.astype(BF)
    for t in range(tiles):

        @pl.when(which == t)
        def _(t=t):
            outs[6 + t][...] = part


def ffn_chunk(tiles, dy_all, gate_w, up_w, down_w, kept):
    count, local, width = dy_all.shape
    hidden = gate_w.shape[1]
    tall = min(256, local)
    number = len(tiles)
    places = jnp.stack(
        [jnp.asarray(t[2], jnp.int32) for t in tiles] + [jnp.int32(t[3]) for t in tiles]
    )

    def at_place(last):
        return pl.BlockSpec((1, tall, last), lambda i, p: (p[i], p[number + i], 0))

    def fixed(n):
        return pl.BlockSpec((tall, width), lambda i, p: (n, 0))

    held = pl.BlockSpec(memory_space=pltpu.VMEM)
    in_specs = [fixed(t[1]) for t in tiles] + [at_place(width), held, held, held]
    arrays = [t[0] for t in tiles] + [dy_all, gate_w, up_w, down_w]
    aliases = {}
    if kept is not None:
        aliases = {1 + len(arrays) + n: n for n in range(6)}
        in_specs += [pl.BlockSpec(memory_space=pl.ANY)] * 6
        arrays += list(kept)
    narrow = jax.ShapeDtypeStruct((count, local, hidden), BF)
    broad = jax.ShapeDtypeStruct((count, local, width), BF)
    part = jax.ShapeDtypeStruct((count, local, width // 2), BF)
    single = jax.ShapeDtypeStruct((tall, width), BF)
    outs = pl.pallas_call(
        functools.partial(ffn_kernel, number),
        out_shape=(narrow, narrow, narrow, broad, part, part) + (single,) * number,
        grid_spec=pltpu.PrefetchScalarGridSpec(
            num_scalar_prefetch=1,
            grid=(number,),
            in_specs=in_specs,
            out_specs=(
                at_place(hidden), at_place(hidden), at_place(hidden), at_place(width),
                at_place(width // 2), at_place(width // 2),
            )
            + (fixed(0),) * number,
        ),
        input_output_aliases=aliases,
        compiler_params=pltpu.CompilerParams(
            dimension_semantics=("arbitrary",), vmem_limit_bytes=FFN_VMEM
        ),
        cost_estimate=pl.CostEstimate(
            flops=12 * number * tall * width * hidden,
            bytes_accessed=2 * (5 * number * tall * width + 3 * width * hidden),
            transcendentals=number * tall * hidden,
        ),
        name="ffn",
    )(places, *arrays)
    return outs[:6], list(outs[6:])


def spread(out_ref, value, per, parts, rows):
    for s in range(per):
        for f in range(parts):
            at = (s * parts + f) * rows
            out_ref[f, s] = value[at : at + rows].astype(BF)


def side_kernel(per, parts, rows, n_ref, d_ref, t_ref):
    spread(t_ref, dot_f32(n_ref[...].T, d_ref[...]), per, parts, rows)


def side_terms(n2, d, count, parts):
    length, width = n2.shape
    hidden = d.shape[1]
    rows = width // (count * parts)
    per = max(1, 512 // (parts * rows))
    wide = per * parts * rows
    return pl.pallas_call(
        functools.partial(side_kernel, per, parts, rows),
        out_shape=jax.ShapeDtypeStruct((parts, count, rows, hidden), BF),
        grid=(width // wide,),
        in_specs=[
            pl.BlockSpec((length, wide), lambda i: (0, i)),
            pl.BlockSpec((length, hidden), lambda i: (0, 0), pipeline_mode=pl.Buffered(1)),
        ],
        out_specs=pl.BlockSpec((parts, per, rows, hidden), lambda i: (0, i, 0, 0)),
        compiler_params=pltpu.CompilerParams(
            dimension_semantics=("arbitrary",), vmem_limit_bytes=VMEM_LIMIT
        ),
        cost_estimate=pl.CostEstimate(
            flops=2 * length * width * hidden,
            bytes_accessed=2 * length * (width + 2 * hidden),
            transcendentals=0,
        ),
        name="side_terms",
    )(n2, d)


def down_kernel(a_ref, dy_ref, t_ref, a_t):
    @pl.when(pl.program_id(0) == 0)
    def _():
        a_t[...] = a_ref[...].T

    t_ref[...] = dot_f32(a_t[...], dy_ref[...]).astype(BF)


def down_terms_of(act, dy):
    length, width = dy.shape
    hidden = act.shape[1]
    wide = min(512, width)
    return pl.pallas_call(
        down_kernel,
        out_shape=jax.ShapeDtypeStruct((hidden, width), BF),
        grid=(width // wide,),
        in_specs=[
            pl.BlockSpec((length, hidden), lambda i: (0, 0), pipeline_mode=pl.Buffered(1)),
            pl.BlockSpec((length, wide), lambda i: (0, i)),
        ],
        out_specs=pl.BlockSpec((hidden, wide), lambda i: (0, i)),
        scratch_shapes=[pltpu.VMEM((hidden, length), BF)],
        compiler_params=pltpu.CompilerParams(
            dimension_semantics=("arbitrary",), vmem_limit_bytes=VMEM_LIMIT
        ),
        cost_estimate=pl.CostEstimate(
            flops=2 * length * width * hidden,
            bytes_accessed=2 * length * (width + hidden),
            transcendentals=0,
        ),
        name="down_terms",
    )(act, dy)


def attn_kernel(per, parts, rows, d_ref, n_ref, t_ref):
    spread(t_ref, dot_f32(d_ref[...], n_ref[...]).T, per, parts, rows)


def attn_terms_of(d_t, n1, count, parts):
    cols, length = d_t.shape
    width = n1.shape[1]
    rows = width // (count * parts)
    per = max(1, 512 // (parts * rows))
    wide = per * parts * rows
    return pl.pallas_call(
        functools.partial(attn_kernel, per, parts, rows),
        out_shape=jax.ShapeDtypeStruct((parts, count, rows, cols), BF),
        grid=(width // wide,),
        in_specs=[
            pl.BlockSpec((cols, length), lambda i: (0, 0), pipeline_mode=pl.Buffered(1)),
            pl.BlockSpec((length, wide), lambda i: (0, i)),
        ],
        out_specs=pl.BlockSpec((parts, per, rows, cols), lambda i: (0, i, 0, 0)),
        compiler_params=pltpu.CompilerParams(
            dimension_semantics=("arbitrary",), vmem_limit_bytes=VMEM_LIMIT
        ),
        cost_estimate=pl.CostEstimate(
            flops=2 * length * width * cols,
            bytes_accessed=2 * length * (width + cols),
            transcendentals=0,
        ),
        name="attn_terms",
    )(d_t, n1)


def tail_kernel(
    parts, cols, d_ref, w_ref, x_ref, dh_ref, n_ref, grad_ref, back_ref,
    even, side_send, side_recv, landing, n_buf, terms, hop_send, hop_recv, last, mid,
    send, arrive, n_sem, own_sem,
):
    me = lax.axis_index("seq")
    z = lax.axis_index("fsdp")
    after_z, before_z = (z + 1) % parts, (z + parts - 1) % parts
    local, width = x_ref.shape
    half = local // 2
    low, high = pl.ds(0, half), pl.ds(half, half)
    barrier = pltpu.get_barrier_semaphore()
    for bit in (1, 2, 4):
        pl.semaphore_signal(barrier, inc=1, device_id=(me ^ bit, z), device_id_type=MESH)
    for other in (after_z, before_z):
        pl.semaphore_signal(barrier, inc=1, device_id=(me, other), device_id_type=MESH)
    pl.semaphore_wait(barrier, 5)
    made = {}

    def start(name, source, target, device):
        n = len(made)
        copy = pltpu.make_async_remote_copy(
            src_ref=source, dst_ref=target, send_sem=send.at[n], recv_sem=arrive.at[n],
            device_id=device, device_id_type=MESH,
        )
        made[name] = copy
        copy.start()

    def to_bit(name, bit, source, target):
        start(name, source, target, (me ^ bit, z))

    def arrived(*names):
        for name in names:
            made[name].wait_recv()

    chunk = n_buf.shape[2]
    chunks = width // chunk

    def fetch(i):
        return pltpu.make_async_copy(
            n_ref.at[:, pl.ds(i * chunk, chunk)], n_buf.at[i % 2], n_sem.at[i % 2]
        )

    fetch(0).start()
    tile = 512

    def product(c, out):
        at = pl.multiple_of((me ^ c) * local, local)
        d = d_ref[:, pl.ds(at, local)].T

        def one(t, carry):
            here = pl.ds(pl.multiple_of(t * tile, tile), tile)
            out[:, here] = dot_f32(d, w_ref[pl.ds(0, cols), here]).astype(BF)
            return carry

        lax.fori_loop(0, width // tile, one, 0)

    def chip(pair):
        product(2 * pair + 1, side_send.at[pair])
        to_bit("s" + str(pair), 1, side_send.at[pair], side_recv.at[pair])
        product(2 * pair, even.at[pair])

    def add_side(pair, part):
        even[pair, part] = (
            even[pair, part].astype(F32) + side_recv[pair, part].astype(F32)
        ).astype(BF)

    chip(3)
    chip(1)
    arrived("s3")
    add_side(3, low)
    to_bit("far_x", 2, even.at[3, low], landing.at[0])
    add_side(3, high)
    to_bit("far_y", 4, even.at[3, high], landing.at[1])
    chip(2)
    arrived("s1")
    add_side(1, low)
    to_bit("first_x", 2, even.at[1, low], landing.at[2])
    add_side(1, high)
    chip(0)
    arrived("s2")
    add_side(2, high)
    to_bit("second_y", 4, even.at[2, high], landing.at[3])
    add_side(2, low)

    count, rows = back_ref.shape[0], back_ref.shape[1]
    per = chunk // (parts * rows)
    for i in range(chunks):
        if i + 1 < chunks:
            fetch(i + 1).start()
        fetch(i).wait()
        value = dot_f32(d_ref[...], n_buf[i % 2]).T
        for s in range(per):
            for f in range(parts):
                at = (s * parts + f) * rows
                terms[f, i * per + s] = value[at : at + rows].astype(BF)
    start("r1", terms.at[before_z], hop_recv.at[0], (me, after_z))

    def add_far(pair, part, slot):
        even[pair, part] = (even[pair, part].astype(F32) + landing[slot].astype(F32)).astype(BF)

    arrived("far_x")
    add_far(2, low, 0)
    to_bit("first_y", 4, even.at[2, low], landing.at[4])
    arrived("far_y")
    add_far(1, high, 1)
    to_bit("second_x", 2, even.at[1, high], landing.at[5])
    arrived("s0")
    for step in range(1, parts):
        arrived("r" + str(step))
        state = hop_recv[step - 1].astype(F32)
        state = state + terms[(z + 2 * parts - 1 - step) % parts].astype(F32)
        if step < parts - 1:
            hop_send[step - 1] = state.astype(BF)
            start("r" + str(step + 1), hop_send.at[step - 1], hop_recv.at[step], (me, after_z))
        else:
            last[...] = state.astype(BF)

    mine = pltpu.make_async_copy(last.at[me], back_ref.at[me], own_sem.at[0])
    mine.start()
    to_bit("b3", 2, last.at[me ^ 6], mid.at[4])
    to_bit("a2", 1, last.at[me ^ 3], mid.at[1])
    to_bit("a4", 1, last.at[me ^ 7], mid.at[3])
    to_bit("a3", 1, last.at[me ^ 5], mid.at[2])
    to_bit("a1", 1, last.at[me ^ 1], back_ref.at[me])
    to_bit("b1", 2, last.at[me ^ 2], back_ref.at[me])
    to_bit("c1", 4, last.at[me ^ 4], back_ref.at[me])
    arrived("a4", "a2", "a3")
    to_bit("b4", 2, mid.at[3], mid.at[5])
    to_bit("b2", 2, mid.at[1], back_ref.at[me ^ 1])
    to_bit("c2", 4, mid.at[2], back_ref.at[me ^ 1])
    arrived("b3")
    to_bit("c3", 4, mid.at[4], back_ref.at[me ^ 2])
    arrived("b4")
    to_bit("c4", 4, mid.at[5], back_ref.at[me ^ 3])

    arrived("first_x", "second_y", "first_y", "second_x")
    gain = w_ref[pl.ds(cols, 8), :].astype(F32)[0:1]
    tall = 64

    def finish(first_slot, second_slot, offset):
        def one(t, carry):
            from_half = pl.ds(pl.multiple_of(t * tall, tall), tall)
            at = pl.ds(pl.multiple_of(t * tall + offset, tall), tall)
            dn = even[0, at].astype(F32) + side_recv[0, at].astype(F32)
            dn = dn + landing[first_slot, from_half].astype(F32)
            dn = dn + landing[second_slot, from_half].astype(F32)
            x = x_ref[at].astype(F32)
            r = lax.rsqrt(jnp.mean(x * x, axis=-1, keepdims=True) + EPS)
            m = x * r
            e = dn * gain
            inner = jnp.mean(e * m, axis=-1, keepdims=True)
            grad_ref[at] = dh_ref[at] + r * (e - m * inner)
            return carry

        lax.fori_loop(0, half // tall, one, 0)

    finish(2, 4, 0)
    finish(3, 5, half)
    arrived("a1", "b1", "c1", "b2", "c2", "c3", "c4")
    mine.wait()
    for copy in made.values():
        copy.wait_send()


def tail(d_t, wt_ext, x, dh1, n1, cols, count, parts):
    local, width = x.shape
    length = n1.shape[0]
    rows = width // (count * parts)
    half = local // 2
    chunk = 512
    anyspace = pl.BlockSpec(memory_space=pl.ANY)
    vmem = pl.BlockSpec(memory_space=pltpu.VMEM)
    copies = 4 + 6 + parts - 1 + 12
    block = (count, rows, cols)
    return pl.pallas_call(
        functools.partial(tail_kernel, parts, cols),
        out_shape=(
            jax.ShapeDtypeStruct((local, width), F32),
            jax.ShapeDtypeStruct(block, BF),
        ),
        in_specs=[vmem, vmem, vmem, vmem, anyspace],
        out_specs=(vmem, anyspace),
        scratch_shapes=[
            pltpu.VMEM((4, local, width), BF),
            pltpu.VMEM((4, local, width), BF),
            pltpu.VMEM((4, local, width), BF),
            pltpu.VMEM((6, half, width), BF),
            pltpu.VMEM((2, length, chunk), BF),
            pltpu.VMEM((parts,) + block, BF),
            pltpu.VMEM((max(1, parts - 2),) + block, BF),
            pltpu.VMEM((parts - 1,) + block, BF),
            pltpu.VMEM(block, BF),
            pltpu.VMEM((6, rows, cols), BF),
            pltpu.SemaphoreType.DMA((copies,)),
            pltpu.SemaphoreType.DMA((copies,)),
            pltpu.SemaphoreType.DMA((2,)),
            pltpu.SemaphoreType.DMA((1,)),
        ],
        compiler_params=pltpu.CompilerParams(
            collective_id=1, has_side_effects=True, vmem_limit_bytes=62 * 1024 * 1024
        ),
        cost_estimate=pl.CostEstimate(
            flops=1 << 30, bytes_accessed=1 << 20, transcendentals=0
        ),
        name="tail",
    )(d_t, wt_ext, x, dh1, n1)


def start_kernel(
    parts, x_ref, attn_ref, ffn_ref, out_ref, down_ref, x_all, attn_all, ffn_mine, out_all,
    down_all, attn_mid, ffn_mid, send, arrive, local_sem,
):
    me = lax.axis_index("seq")
    z = lax.axis_index("fsdp")
    after_z, before_z = (z + 1) % parts, (z + parts - 1) % parts
    half = x_ref.shape[0] // 2
    barrier = pltpu.get_barrier_semaphore()
    for bit in (1, 2, 4):
        pl.semaphore_signal(barrier, inc=1, device_id=(me ^ bit, z), device_id_type=MESH)
    for other in (after_z, before_z):
        pl.semaphore_signal(barrier, inc=1, device_id=(me, other), device_id_type=MESH)
    pl.semaphore_wait(barrier, 5)
    made = {}

    def start(name, source, target, device):
        n = len(made)
        copy = pltpu.make_async_remote_copy(
            src_ref=source, dst_ref=target, send_sem=send.at[n], recv_sem=arrive.at[n],
            device_id=device, device_id_type=MESH,
        )
        made[name] = copy
        copy.start()

    def to_bit(name, bit, source, target):
        start(name, source, target, (me ^ bit, z))

    def arrived(*names):
        for name in names:
            made[name].wait_recv()

    held = [
        pltpu.make_async_copy(x_ref, x_all.at[me], local_sem.at[0]),
        pltpu.make_async_copy(attn_ref.at[me], attn_all.at[z, me], local_sem.at[1]),
        pltpu.make_async_copy(ffn_ref.at[me], ffn_mine.at[me], local_sem.at[2]),
        pltpu.make_async_copy(out_ref, out_all.at[z], local_sem.at[3]),
        pltpu.make_async_copy(down_ref, down_all.at[z], local_sem.at[4]),
    ]
    for copy in held:
        copy.start()

    def swap_first(tag, source, final, mid):
        to_bit(tag + "a2", 1, source.at[me ^ 3], mid.at[1])
        to_bit(tag + "a4", 1, source.at[me ^ 7], mid.at[3])
        to_bit(tag + "a3", 1, source.at[me ^ 5], mid.at[2])
        to_bit(tag + "a1", 1, source.at[me ^ 1], final.at[me])

    def swap_second(tag, source, final, mid):
        to_bit(tag + "b3", 2, source.at[me ^ 6], mid.at[4])
        to_bit(tag + "b1", 2, source.at[me ^ 2], final.at[me])
        arrived(tag + "a4", tag + "a2")
        to_bit(tag + "b4", 2, mid.at[3], mid.at[5])
        to_bit(tag + "b2", 2, mid.at[1], final.at[me ^ 1])

    def swap_third(tag, source, final, mid):
        to_bit(tag + "c1", 4, source.at[me ^ 4], final.at[me])
        arrived(tag + "a3")
        to_bit(tag + "c2", 4, mid.at[2], final.at[me ^ 1])
        arrived(tag + "b3")
        to_bit(tag + "c3", 4, mid.at[4], final.at[me ^ 2])
        arrived(tag + "b4")
        to_bit(tag + "c4", 4, mid.at[5], final.at[me ^ 3])

    def swap_end(tag):
        arrived(*[tag + n for n in ("a1", "b1", "c1", "b2", "c2", "c3", "c4")])

    def around(tag, step, whole):
        if step > 1:
            arrived(tag + str(step - 1))
        at = (z + parts + 1 - step) % parts
        start(tag + str(step), whole.at[at], whole.at[at], (me, after_z))

    attn_sets = (attn_ref, attn_all.at[z], attn_mid)
    ffn_sets = (ffn_ref, ffn_mine, ffn_mid)
    start("o1", out_ref, out_all.at[z], (me, after_z))
    swap_first("attn", *attn_sets)
    swap_second("attn", *attn_sets)
    to_bit("x2", 2, x_ref, x_all.at[me])
    swap_third("attn", *attn_sets)
    to_bit("x4", 4, x_ref, x_all.at[me])
    to_bit("x1", 1, x_ref, x_all.at[me])
    swap_first("ffn", *ffn_sets)
    swap_end("attn")
    held[1].wait()
    around("z", 1, attn_all)
    held[4].wait()
    around("d", 1, down_all)
    for step in range(2, parts):
        around("o", step, out_all)
        around("z", step, attn_all)
    arrived("x2")
    to_bit("x3", 1, x_all.at[me ^ 2], x_all.at[me ^ 2])
    to_bit("f1", 4, x_all.at[me ^ 2, pl.ds(0, half)], x_all.at[me ^ 2, pl.ds(0, half)])
    arrived("x4")
    to_bit("x5", 1, x_all.at[me ^ 4], x_all.at[me ^ 4])
    to_bit("f2", 2, x_all.at[me ^ 4, pl.ds(half, half)], x_all.at[me ^ 4, pl.ds(half, half)])
    around("d", 2, down_all)
    swap_second("ffn", *ffn_sets)
    swap_third("ffn", *ffn_sets)
    for step in range(3, parts):
        around("d", step, down_all)
    arrived("f1", "f2")
    to_bit("x7", 1, x_all.at[me ^ 6], x_all.at[me ^ 6])
    swap_end("ffn")
    arrived("x1", "x3", "x5", "x7", "z" + str(parts - 1), "o" + str(parts - 1))
    arrived("d" + str(parts - 1))
    for copy in made.values():
        copy.wait_send()
    for copy in (held[0], held[2], held[3]):
        copy.wait()


def start_gather(x, attn_send, ffn_send, w_out, w_down, count, parts):
    anyspace = pl.BlockSpec(memory_space=pl.ANY)
    copies = 8 + 2 * 12 + 3 * (parts - 1)
    shapes = (
        jax.ShapeDtypeStruct((count,) + x.shape, BF),
        jax.ShapeDtypeStruct((parts,) + attn_send.shape, BF),
        jax.ShapeDtypeStruct(ffn_send.shape, BF),
        jax.ShapeDtypeStruct((parts,) + w_out.shape, BF),
        jax.ShapeDtypeStruct((parts,) + w_down.shape, BF),
        jax.ShapeDtypeStruct((6,) + attn_send.shape[1:], BF),
        jax.ShapeDtypeStruct((6,) + ffn_send.shape[1:], BF),
    )
    return pl.pallas_call(
        functools.partial(start_kernel, parts),
        out_shape=shapes,
        in_specs=[anyspace] * 5,
        out_specs=(anyspace,) * 7,
        scratch_shapes=[
            pltpu.SemaphoreType.DMA((copies,)),
            pltpu.SemaphoreType.DMA((copies,)),
            pltpu.SemaphoreType.DMA((5,)),
        ],
        compiler_params=pltpu.CompilerParams(
            collective_id=0, has_side_effects=True, vmem_limit_bytes=8 * 1024 * 1024
        ),
        name="start_gather",
    )(x, attn_send, ffn_send, w_out, w_down)[:5]


def ring(axis):
    count = lax.axis_size(axis)
    return [(n, (n + 1) % count) for n in range(count)]


def hop(*blocks):
    return [lax.ppermute(block, "fsdp", ring("fsdp")) for block in blocks]


def collect(pieces, axis):
    count = lax.axis_size(axis)
    me = lax.axis_index(axis)
    whole = jnp.zeros((count,) + pieces[0].shape, pieces[0].dtype)
    for back, piece in enumerate(pieces):
        whole = lax.dynamic_update_index_in_dim(whole, piece, (me + count - back) % count, 0)
    return whole


def term_of(terms, step):
    count = lax.axis_size("fsdp")
    me = lax.axis_index("fsdp")
    return lax.dynamic_index_in_dim(terms, (me + 2 * count - 1 - step) % count, 0, False)


def launch(states):
    return hop(*[state.astype(BF) for state in states])


def landed(moved, terms, step):
    return [m.astype(F32) + term_of(t, step).astype(F32) for m, t in zip(moved, terms)]


def ring_finish(moved, terms, step):
    states = landed(moved, terms, step)
    for n in range(step + 1, lax.axis_size("fsdp")):
        states = landed(launch(states), terms, n)
    return states


def fence(*values):
    return lax.optimization_barrier(values)


def swap(block, bit):
    count = lax.axis_size("seq")
    return lax.ppermute(block, "seq", [(n, n ^ bit) for n in range(count)])


def gather_plain(block):
    me = lax.axis_index("seq")
    whole = lax.all_gather(block, "seq", axis=0, tiled=False)
    return [lax.dynamic_index_in_dim(whole, me ^ c, 0, False) for c in range(whole.shape[0])]


def scatter_plain(parts):
    me = lax.axis_index("seq")
    whole = jnp.zeros((len(parts),) + parts[0].shape, BF)
    for c, part in enumerate(parts):
        whole = lax.dynamic_update_index_in_dim(whole, part.astype(BF), me ^ c, 0)
    return lax.psum_scatter(whole, "seq", scatter_dimension=0, tiled=False).astype(F32)


def far_halves(over_x, over_y):
    half = over_x.shape[0] // 2
    return swap(over_x[:half], 4), swap(over_y[half:], 2)


def chip_sum(own, other):
    return own.astype(F32) + swap(other, 1).astype(F32)


def total_of(*terms):
    total = terms[0].astype(F32)
    for term in terms[1:]:
        total = total + term.astype(F32)
    return total


def plus(*terms):
    return total_of(*terms).astype(BF)


def exchange(array):
    return lax.all_to_all(array, "seq", split_axis=0, concat_axis=0, tiled=True)


def document_starts(flags_all):
    length = flags_all.shape[0]
    lanes = 128
    table = flags_all.reshape(length // lanes, lanes)
    place = jnp.arange(length, dtype=jnp.int32).reshape(table.shape)
    marked = jnp.where((table != 0) & (place > 0), place, 0)
    inside = jnp.arange(lanes)[None, :] <= jnp.arange(lanes)[:, None]
    local = jnp.max(jnp.where(inside[None], marked[:, None, :], 0), axis=-1)
    rows = jnp.max(marked, axis=1)
    count = length // lanes
    before = jnp.arange(count)[None, :] < jnp.arange(count)[:, None]
    carried = jnp.max(jnp.where(before, rows[None, :], 0), axis=-1)
    return jnp.maximum(local, carried[:, None]).reshape(length)


def body(
    tokens, doc_starts, gain_attn, w_query, w_key, w_value, w_out, gain_ffn, w_gate, w_up, w_down,
    cotangent,
):
    streams, local, width = tokens.shape
    assert streams == 1
    count = lax.axis_size("seq")
    parts = lax.axis_size("fsdp")
    me = lax.axis_index("seq")
    cube = count == 8
    length = local * count
    half = local // 2
    group = H // count
    share = (H // KV) // group
    rows = w_query.shape[0]
    hidden = w_gate.shape[1] // count
    group_width = group * HD
    attn_cols = group_width + 2 * HD
    flag_cols = local // rows
    extra_cols = 128
    sheet = (length, width)

    own = tokens[0]
    attn_send = jnp.concatenate(
        [
            w_query.reshape(rows, count, group_width),
            jnp.repeat(w_key.reshape(rows, KV, HD), share, axis=1),
            jnp.repeat(w_value.reshape(rows, KV, HD), share, axis=1),
        ],
        axis=2,
    ).transpose(1, 0, 2)
    extra = jnp.concatenate(
        [
            gain_attn[:, None],
            gain_ffn[:, None],
            doc_starts[0].astype(BF).reshape(rows, flag_cols),
            jnp.zeros((rows, extra_cols - 2 - flag_cols), BF),
        ],
        axis=1,
    )
    attn_send = jnp.concatenate(
        [attn_send, jnp.broadcast_to(extra[None], (count,) + extra.shape)], axis=2
    )
    ffn_send = jnp.concatenate(
        [w_gate.reshape(rows, count, hidden), w_up.reshape(rows, count, hidden)], axis=0
    ).transpose(1, 0, 2)
    z = lax.axis_index("fsdp")
    if cube:
        x_all, attn_all, ffn_part, out_part, down_w = start_gather(
            own, attn_send, ffn_send, w_out, w_down, count, parts
        )
    else:
        x_all = lax.all_gather(own, "seq", axis=0, tiled=False)
        attn_all = lax.all_gather(exchange(attn_send), "fsdp", axis=0, tiled=False)
        ffn_part = exchange(ffn_send)
        out_part = lax.all_gather(w_out, "fsdp", axis=0, tiled=False)
        down_w = lax.all_gather(w_down, "fsdp", axis=0, tiled=False)
    down_w = down_w.reshape(hidden, width)
    dy = cotangent[0]
    own, x_all, attn_all, ffn_part, out_part, dy = fence(
        own, x_all, attn_all, ffn_part, out_part, dy
    )
    ffn_pieces = [[ffn_part.reshape(count, 2, rows, hidden)]]

    out_w = lax.all_gather(out_part.reshape(parts * rows, width), "seq", axis=0, tiled=True)
    if len(ffn_pieces) < parts:
        ffn_pieces.append(hop(*ffn_pieces[-1]))
    flags = lax.dynamic_index_in_dim(attn_all, z, 0, False)
    flags = flags[:, :, attn_cols + 2 : attn_cols + 2 + flag_cols].reshape(length)
    last = document_starts(flags)
    position = (jnp.arange(length, dtype=jnp.int32) - last).astype(F32)
    frequency = jnp.exp(jnp.arange(HALF, dtype=F32) * (-2.0 * math.log(10000.0) / HD))
    angle = frequency[:, None] * position[None, :]
    cosine, sine = jnp.cos(angle), jnp.sin(angle)
    blocks = length // BQ
    by_block = last.reshape(blocks, BQ)
    starts = jnp.tile(by_block, (1, group)).reshape(blocks, 1, group * BQ)
    first_row = jnp.arange(blocks, dtype=jnp.int32) * BQ
    low = by_block[:, 0] // BK
    high = (first_row + BQ + BK - 1) // BK
    begin = jnp.minimum((by_block[:, -1] + BK - 1) // BK, high)
    end = jnp.maximum((first_row + 1) // BK, begin)
    bounds = jnp.stack([low, begin, end, high], axis=1)
    w_ext = attn_all.transpose(1, 0, 2, 3).reshape(width, attn_cols + extra_cols)
    n1_all, projected, wt_ext = project(x_all, w_ext, attn_cols)
    attn_t = wt_ext[:attn_cols]
    gain_one = wt_ext[attn_cols].astype(F32)
    gain_two = wt_ext[attn_cols + 1].astype(F32)
    projected, cosine, sine, starts, bounds, ffn_last, dy = fence(
        projected, cosine, sine, starts, bounds, ffn_pieces[-1], dy
    )
    ffn_pieces[-1] = ffn_last

    dy_all = lax.all_gather(dy, "seq", axis=0, tiled=False)
    cut = blocks * 11 // 16
    ready = (bounds, projected, cosine, sine, starts, group, count, local)
    if len(ffn_pieces) < parts:
        ffn_pieces.append(hop(*ffn_pieces[-1]))
    o_half, lse_one, qt_one, k_t, k_n, v_n, v_t = attend(*ready, 0, cut, None)
    o_half, lse_one, qt_one, k_t, k_n, v_n, v_t, ffn_last, out_w = fence(
        o_half, lse_one, qt_one, k_t, k_n, v_n, v_t, ffn_pieces[-1], out_w
    )
    ffn_pieces[-1] = ffn_last
    while len(ffn_pieces) < parts:
        ffn_pieces.append(hop(*ffn_pieces[-1]))
    o_heads, lse_two, qt_two = attend(*ready, cut, blocks - cut, (o_half, k_n, v_t))
    o_heads, lse_two, qt_two, ffn_pieces = fence(o_heads, lse_two, qt_two, ffn_pieces)

    o_t = exchange(o_heads).reshape(count * group_width, local)
    o_t, dy_all, qt_one, qt_two, lse_one, lse_two = fence(
        o_t, dy_all, qt_one, qt_two, lse_one, lse_two
    )

    ffn_w = collect([piece[0] for piece in ffn_pieces], "fsdp").transpose(2, 1, 0, 3, 4).reshape(2, width, hidden)
    gate_w, up_w = ffn_w[0], ffn_w[1]
    x = own.astype(F32)
    r1 = lax.rsqrt(jnp.mean(x * x, axis=-1, keepdims=True) + EPS)
    h1 = x + jnp.einsum("et,ed->td", o_t, out_w, preferred_element_type=F32)
    r2 = lax.rsqrt(jnp.mean(h1 * h1, axis=-1, keepdims=True) + EPS)
    n2 = (h1 * r2 * gain_two).astype(BF)
    n2, h1, r2 = fence(n2, h1, r2)

    def over_seq(part):
        whole = part.reshape(-1, part.shape[-1])
        return lax.psum_scatter(whole, "seq", scatter_dimension=0, tiled=True)

    kept = None

    weights = (dy_all, gate_w, up_w, down_w)

    if cube:
        side = swap(n2, 1)
        low_n, high_n = n2[:half], n2[half:]
        x_low, y_low = swap(low_n, 2), swap(low_n, 4)
        x_high, y_high = swap(high_n, 2), swap(high_n, 4)
        side, gate_w, up_w = fence(side, gate_w, up_w)
        weights = (dy_all, gate_w, up_w, down_w)
        kept, (own_a, own_b, own_c, own_d) = ffn_chunk(
            [(n2, 0, me, 0), (n2, 1, me, 1), (side, 0, me ^ 1, 0), (side, 1, me ^ 1, 1)],
            *weights, kept,
        )
        kept, own_a, own_b, own_c, own_d, x_low, y_low = fence(
            kept, own_a, own_b, own_c, own_d, x_low, y_low
        )

        far_a = swap(x_low, 4)
        side_x, side_y = swap(x_low, 1), swap(y_low, 1)
        own_c, own_d = swap(own_c, 1), swap(own_d, 1)
        side_x, side_y, x_low, y_low, kept = fence(side_x, side_y, x_low, y_low, kept)
        kept, (x_a, x_b, y_a, y_b) = ffn_chunk(
            [(x_low, 0, me ^ 2, 0), (side_x, 0, me ^ 3, 0), (y_low, 0, me ^ 4, 0),
             (side_y, 0, me ^ 5, 0)],
            *weights, kept,
        )
        kept, x_a, x_b, y_a, y_b, x_high, y_high, own_c, own_d = fence(
            kept, x_a, x_b, y_a, y_b, x_high, y_high, own_c, own_d
        )

        far_b = swap(y_high, 2)
        side_x, side_y = swap(x_high, 1), swap(y_high, 1)
        x_b, y_b = swap(x_b, 1), swap(y_b, 1)
        side_x, side_y, x_high, y_high, kept, x_a, x_b = fence(
            side_x, side_y, x_high, y_high, kept, x_a, x_b
        )
        x_first = swap(plus(x_a, x_b), 2)
        kept, (x_c, x_d, y_c, y_d) = ffn_chunk(
            [(x_high, 0, me ^ 2, 1), (side_x, 0, me ^ 3, 1), (y_high, 0, me ^ 4, 1),
             (side_y, 0, me ^ 5, 1)],
            *weights, kept,
        )
        kept, x_c, x_d, y_c, y_d, far_a, far_b, y_a, y_b = fence(
            kept, x_c, x_d, y_c, y_d, far_a, far_b, y_a, y_b
        )

        side_far, side_more = swap(far_a, 1), swap(far_b, 1)
        x_d, y_d = swap(x_d, 1), swap(y_d, 1)
        side_far, side_more, y_c, y_d = fence(side_far, side_more, y_c, y_d)
        y_second = swap(plus(y_c, y_d), 4)
        kept, (far_one, far_two, far_three, far_four) = ffn_chunk(
            [(far_a, 0, me ^ 6, 0), (far_b, 0, me ^ 6, 1), (side_far, 0, me ^ 7, 0),
             (side_more, 0, me ^ 7, 1)],
            *weights, kept,
        )
        kept, far_one, far_two, far_three, far_four, x_first, y_second, x_c, x_d = fence(
            kept, far_one, far_two, far_three, far_four, x_first, y_second, x_c, x_d
        )
        act, d_gate, d_up, n2_all, y_one, y_two = kept
        n2_all, dy_rows = n2_all.reshape(sheet), dy_all.reshape(sheet)
        act, d_gate, d_up = [a.reshape(length, hidden) for a in (act, d_gate, d_up)]

        x_far = swap(plus(far_one, swap(far_three, 1)), 2)
        y_far = swap(plus(far_two, swap(far_four, 1)), 4)
        gate_t = side_terms(n2_all, d_gate, count, parts)
        x_far, y_far, gate_t, y_one = fence(x_far, y_far, gate_t, y_one)

        x_second = swap(plus(x_c, x_d, y_far), 2)
        y_first = swap(plus(y_a, y_b, x_far), 4)
        (gate_moved,) = launch([term_of(gate_t, 0)])
        y_one = over_seq(y_one)
        up_t = side_terms(n2_all, d_up, count, parts)
        x_second, y_first, up_t, gate_moved, act = fence(x_second, y_first, up_t, gate_moved, act)
        dn2 = jnp.concatenate(
            [
                total_of(own_a, own_c, x_first, y_first),
                total_of(own_b, own_d, x_second, y_second),
            ],
            axis=0,
        )
    else:
        n2_blocks = gather_plain(n2)
        dn2_parts = []
        for c in range(0, count, 2):
            each = range(max(1, local // 256))
            kept, found = ffn_chunk(
                [(n2_blocks[n], t, me ^ n, t) for n in (c, c + 1) for t in each], *weights, kept
            )
            dn2_parts += [
                jnp.concatenate(found[: len(each)], axis=0),
                jnp.concatenate(found[len(each) :], axis=0),
            ]
        act, d_gate, d_up, n2_all, y_one, y_two = kept
        n2_all, dy_rows = n2_all.reshape(sheet), dy_all.reshape(sheet)
        act, d_gate, d_up = [a.reshape(length, hidden) for a in (act, d_gate, d_up)]
        dn2 = scatter_plain(dn2_parts)
        gate_t = side_terms(n2_all, d_gate, count, parts)
        up_t = side_terms(n2_all, d_up, count, parts)
        (gate_moved,) = launch([term_of(gate_t, 0)])
        y_one = over_seq(y_one)

    m2 = h1 * r2
    e2 = dn2 * gain_two
    dh1 = dy.astype(F32) + r2 * (e2 - m2 * jnp.mean(e2 * m2, axis=-1, keepdims=True))
    db = dh1.astype(BF)
    do_t = jnp.einsum("ed,td->et", out_w, db, preferred_element_type=F32).astype(BF)
    (up_moved,) = launch([term_of(up_t, 0)])
    (gate_state,) = landed([gate_moved], [gate_t], 1)
    if parts > 2:
        (gate_moved,) = launch([gate_state])
    do_t, db, dh1, up_moved, gate_moved, gate_state, y_two = fence(
        do_t, db, dh1, up_moved, gate_moved, gate_state, y_two
    )
    y_two = over_seq(y_two)
    do_heads = exchange(do_t.reshape(count, group_width, local))
    term_out = dot_f32(o_t, db).astype(BF)
    term_down = down_terms_of(act, dy_rows).reshape(parts, hidden // parts, width)
    (up_state,) = landed([up_moved], [up_t], 1)
    if parts > 2:
        (up_moved,) = launch([up_state])
    do_heads, term_out, term_down, y_one, up_moved, up_state = fence(
        do_heads, term_out, term_down, y_one, up_moved, up_state
    )

    pair_t = [gate_t, up_t]
    pair = [gate_state, up_state]
    if parts > 2:
        pair = landed([gate_moved, up_moved], pair_t, 2)
    moved = launch((pair if parts > 3 else []) + [term_of(term_down, 0)])
    saved = (bounds, qt_one, k_n, k_t, v_n, cosine, sine, starts, o_heads, do_heads, lse_one, group)
    dq_one, dk, dv = attend_back(*saved, 0, cut, None)
    dq_one, dk, dv, moved, pair, do_heads, y_two, term_out = fence(
        dq_one, dk, dv, moved, pair, do_heads, y_two, term_out
    )
    part_out = over_seq(term_out)
    down_state = landed(moved[-1:], [term_down], 1)
    if parts > 3:
        pair = ring_finish(moved[:2], pair_t, 3)
    ffn_back = exchange(jnp.stack(pair, axis=1).astype(BF))
    moved = launch(down_state if parts > 2 else [])
    saved = (bounds, qt_two, k_n, k_t, v_n, cosine, sine, starts, o_heads, do_heads, lse_two, group)
    dq_two, dkv_t = attend_back(*saved, cut, blocks - cut, (dk, dv))

    def along(weight, grad):
        return jnp.sum(weight.astype(F32) * grad, axis=1)

    ffn_back, dq_two, dkv_t = fence(ffn_back, dq_two, dkv_t)
    ffn_back = ffn_back.astype(F32)
    grad_gate = ffn_back[:, 0].transpose(1, 0, 2).reshape(rows, count * hidden)
    grad_up = ffn_back[:, 1].transpose(1, 0, 2).reshape(rows, count * hidden)
    gain_sum = along(w_gate, grad_gate) + along(w_up, grad_up)
    output = (h1 + jnp.concatenate([y_one, y_two], axis=1).astype(F32)).astype(BF)
    dq_two, dkv_t, moved, down_state, part_out, grad_gate, grad_up, gain_sum, output = fence(
        dq_two, dkv_t, moved, down_state, part_out, grad_gate, grad_up, gain_sum, output
    )

    d_t = jnp.concatenate([jnp.concatenate([dq_one, dq_two], axis=1), dkv_t], axis=0)
    def pair_of(c):
        return jnp.concatenate(
            [lax.dynamic_slice_in_dim(d_t, (me ^ n) * local, local, 1) for n in (c, c + 1)], axis=1
        )

    def dn1_chunk(c):
        part = jnp.einsum("et,ed->td", pair_of(c), attn_t, preferred_element_type=F32).astype(BF)
        return part[:local], part[local:]

    n1_rows = n1_all.reshape(sheet)
    if parts > 2:
        down_state = landed(moved, [term_down], 2)
    moved = launch(down_state if parts > 3 else [])
    grad_out = lax.psum_scatter(part_out, "fsdp", scatter_dimension=0, tiled=True).astype(F32)
    if cube:
        grad_tokens, attn_back = tail(d_t, wt_ext, own, dh1, n1_rows, attn_cols, count, parts)
    else:
        dn1 = scatter_plain([piece for c in range(0, count, 2) for piece in dn1_chunk(c)])
        attn_terms = [attn_terms_of(d_t, n1_rows, count, parts)]
        (part_attn,) = ring_finish(launch([term_of(attn_terms[0], 0)]), attn_terms, 1)
        attn_back = exchange(part_attn.astype(BF))
        m1 = x * r1
        e1 = dn1 * gain_one
        grad_tokens = dh1 + r1 * (e1 - m1 * jnp.mean(e1 * m1, axis=-1, keepdims=True))
    grad_tokens, attn_back, moved, grad_out = fence(grad_tokens, attn_back, moved, grad_out)
    if parts > 3:
        down_state = ring_finish(moved, [term_down], 3)
    grad_down = down_state[0].reshape(hidden // parts, width)

    attn_back = attn_back.astype(F32)
    grad_query = attn_back[:, :, :group_width].transpose(1, 0, 2).reshape(rows, H * HD)
    pair = attn_back[:, :, group_width:].reshape(KV, share, rows, 2 * HD).sum(axis=1)
    grad_key = pair[:, :, :HD].transpose(1, 0, 2).reshape(rows, KV * HD)
    grad_value = pair[:, :, HD:].transpose(1, 0, 2).reshape(rows, KV * HD)

    grad_gain_attn = (
        along(w_query, grad_query) + along(w_key, grad_key) + along(w_value, grad_value)
    ) / gain_attn.astype(F32)
    grad_gain_ffn = gain_sum / gain_ffn.astype(F32)
    return (
        output[None],
        grad_tokens[None],
        grad_gain_attn,
        grad_query,
        grad_key,
        grad_value,
        grad_out,
        grad_gain_ffn,
        grad_gate,
        grad_up,
        grad_down,
    )


def solution(mesh):
    sheet = P("fsdp", "seq", None)
    line = P(("seq", "fsdp"))
    matrix = P(("seq", "fsdp"), None)
    return jax.shard_map(
        body,
        mesh=mesh,
        in_specs=(
            sheet, P("fsdp", "seq"), line, matrix, matrix, matrix, matrix, line, matrix, matrix,
            matrix, sheet,
        ),
        out_specs=(
            sheet, sheet, line, matrix, matrix, matrix, matrix, line, matrix, matrix, matrix,
        ),
        check_vma=False,
    )
```
